32 devices in a mesh: slab: 16 (over z, x, core), filt: 2 (over y).
Axes of the slice: x: 2, y: 2, z: 4, core: 2. Of those that a mesh axis runs over, the one named last changes fastest.
Arguments:
- volume: bfloat16 [16, 8, 64, 256], P('slab', 'filt'), may hold values from -6 to 6
- kernel_one: bfloat16 [27, 64, 64], replicated, may hold values from -0.15625 to 0.15625
- bias_one: bfloat16 [64], replicated, may hold values from -2.5 to 2.5
- kernel_two: bfloat16 [27, 128, 64], P(None, 'filt'), may hold values from -0.15625 to 0.15625
- bias_two: bfloat16 [128], P('filt'), may hold values from -2.5 to 2.5
- kernel_three: bfloat16 [27, 128, 128], P(None, 'filt'), may hold values from -0.109375 to 0.109375
- bias_three: bfloat16 [128], P('filt'), may hold values from -2.5 to 2.5
Outputs:
- skip_one: bfloat16 [16, 8, 64, 256], P('slab', 'filt')
- features_two: bfloat16 [16, 4, 128, 128], P('slab', None, 'filt')
The draws below stay inside these ranges and needn't reach their ends.
All inputs are finite; a program needn't handle non-finite values.
Results may differ from the reference program's by a relative error of at most 0.0057.
Values may be sent and summed in bfloat16 or wider, within the bound.
No kernel may reach another device: no remote copies, remote signals or barrier semaphores. Data moves between devices by JAX's collectives and lax.ppermute only.
A program may use at most 64 MiB of HBM per device.

```python
import jax
import jax.numpy as jnp
from jax import lax

C0 = 64
C1 = 128
W1 = 256
DEPTH = 16
H1 = 8


def block_levels(key, extent, cuts, smallest, top_value):
    gain = 1.0
    for dim, shards_of in cuts:
        heights = jax.random.uniform(jax.random.fold_in(jax.random.fold_in(key, 6), dim), (shards_of,), jnp.float32, smallest / len(cuts), top_value / len(cuts))
        gain = gain * jnp.repeat(jnp.exp(heights), extent[dim] // shards_of).reshape((-1,) + (1,) * (len(extent) - 1 - dim))
    return gain


def normal_values(rng, dims, spread, bound, cuts=(), held_as=jnp.bfloat16):
    drawn = spread * jax.random.normal(rng, dims, jnp.float32)
    if cuts:
        drawn = drawn * block_levels(rng, dims, cuts, -0.22, 0.18)
    return jnp.clip(drawn, -bound, bound).astype(held_as)


def setup_inputs(seed: int = 0) -> dict:
    arg_keys = jax.random.split(jax.random.key(seed), 8)
    volume = normal_values(arg_keys[0], (DEPTH, H1, C0, W1), 1.0, 6.0, ((0, 16), (1, 2)))
    kernel_one = normal_values(arg_keys[1], (27, C0, C0), (27 * C0) ** -0.5, 0.15625)
    bias_one = normal_values(arg_keys[2], (C0,), 0.5, 2.5)
    kernel_two = normal_values(arg_keys[3], (27, C1, C0), (27 * C0) ** -0.5, 0.15625, ((1, 2),))
    bias_two = normal_values(arg_keys[4], (C1,), 0.5, 2.5, ((0, 2),))
    kernel_three = normal_values(arg_keys[5], (27, C1, C1), (27 * C1) ** -0.5, 0.109375, ((1, 2),))
    bias_three = normal_values(arg_keys[6], (C1,), 0.5, 2.5, ((0, 2),))
    return dict(volume=volume, kernel_one=kernel_one, bias_one=bias_one, kernel_two=kernel_two, bias_two=bias_two, kernel_three=kernel_three, bias_three=bias_three)


def convolve(field, kernel, bias):
    padded = jnp.pad(field, ((1, 1), (1, 1), (0, 0), (1, 1)))
    rows = field.shape[1]
    cols = field.shape[3]
    kern = kernel.astype(jnp.float32)

    def plane(index):
        block = lax.dynamic_slice_in_dim(padded, index, 3, 0).astype(jnp.float32)
        total = jnp.zeros((rows, kernel.shape[1], cols), jnp.float32)
        for kd in range(3):
            for kh in range(3):
                for kw in range(3):
                    tap = 9 * kd + 3 * kh + kw
                    total = total + jnp.einsum("oc,hcw->how", kern[tap], block[kd, kh:kh + rows, :, kw:kw + cols])
        total = total + bias.astype(jnp.float32)[None, :, None]
        return jnp.maximum(total, 0.0).astype(jnp.bfloat16)

    return lax.map(plane, jnp.arange(field.shape[0], dtype=jnp.int32))


def reference(volume, kernel_one, bias_one, kernel_two, bias_two, kernel_three, bias_three):
    skip_one = convolve(volume, kernel_one, bias_one)
    depth, rows, chans, cols = skip_one.shape
    pooled = jnp.max(skip_one.reshape(depth, rows // 2, 2, chans, cols // 2, 2), axis=(2, 5))
    hidden = convolve(pooled, kernel_two, bias_two)
    features_two = convolve(hidden, kernel_three, bias_three)
    return skip_one, features_two
```

```python
import functools

import jax
import jax.numpy as jnp
from jax import lax
from jax.experimental import pallas as pl
from jax.experimental.pallas import tpu as pltpu
from jax.sharding import PartitionSpec as P

BF = jnp.bfloat16
F32 = jnp.float32
NT = (((1,), (1,)), ((), ()))
NN = (((1,), (0,)), ((), ()))

LAYER = 4
RUN = 24
FRAME = 32
LEAD = 4


def extended(block, sides, width):
    for axis, dim in sides:
        count = lax.axis_size(axis)
        forward = [(i, i + 1) for i in range(count - 1)]
        backward = [(target, source) for source, target in forward]
        low = lax.ppermute(
            lax.slice_in_dim(block, block.shape[dim] - width, None, axis=dim), axis, forward
        )
        high = lax.ppermute(lax.slice_in_dim(block, 0, width, axis=dim), axis, backward)
        block = jnp.concatenate([low, block, high], axis=dim)
    return block


def pad_columns(field):
    return jnp.pad(field, ((0, 0), (0, 0), (0, 0), (1, 1)))


def accumulate(total, padded, kernel):
    planes, rows, chans, cols = total.shape
    for kd in range(3):
        for kh in range(3):
            for kw in range(3):
                tap = 9 * kd + 3 * kh + kw
                total = total + jnp.einsum(
                    "oc,dhcw->dhow",
                    kernel[tap],
                    padded[kd : kd + planes, kh : kh + rows, :, kw : kw + cols],
                    preferred_element_type=jnp.float32,
                )
    return total


def finish(total, bias):
    return jnp.maximum(total + bias.astype(jnp.float32)[None, None, :, None], 0.0).astype(
        jnp.bfloat16
    )


def by_planes(volume, kernel_one, bias_one, kernel_two, bias_two, kernel_three, bias_three):
    planes, rows, chans, cols = volume.shape
    rimmed = extended(volume, (("slab", 0), ("filt", 1)), 1)
    start_one = jnp.zeros((planes, rows, kernel_one.shape[1], cols), jnp.float32)
    skip_one = finish(accumulate(start_one, pad_columns(rimmed), kernel_one), bias_one)
    pooled = jnp.max(skip_one.reshape(planes, rows // 2, 2, chans, cols // 2, 2), axis=(2, 5))
    full_rows = lax.all_gather(pooled, "filt", axis=1, tiled=True)
    planed = extended(full_rows, (("slab", 0),), 1)
    padded = jnp.pad(planed, ((0, 0), (1, 1), (0, 0), (1, 1)))
    height = full_rows.shape[1]
    width = full_rows.shape[3]
    start_two = jnp.zeros((planes, height, kernel_two.shape[1], width), jnp.float32)
    hidden = finish(accumulate(start_two, padded, kernel_two), bias_two)
    hidden_planes = extended(hidden, (("slab", 0),), 1)
    start_three = jnp.zeros((planes, height, kernel_three.shape[1], width), jnp.float32)
    piece_padded = jnp.pad(
        lax.all_gather(hidden_planes, "filt", axis=2, tiled=True), ((0, 0), (1, 1), (0, 0), (1, 1))
    )
    summed = accumulate(start_three, piece_padded, kernel_three)
    features_two = finish(summed, bias_three)
    return (skip_one, features_two)


def dot(a, b, dims):
    return lax.dot_general(a, b, dims, preferred_element_type=F32)


def pack_kernel(volume, k2, k3, b23, blocks, sent):
    count, width = blocks.shape[0] // (2 * RUN), volume.shape[1]
    row = lax.broadcasted_iota(jnp.int32, (blocks.shape[0], width), 0)
    col = lax.broadcasted_iota(jnp.int32, (blocks.shape[0], width), 1)
    peer, rest = row // (2 * RUN), row % (2 * RUN)
    wanted = (width // count) * peer + 2 * (rest % RUN - LEAD) + rest // RUN
    chosen = jnp.where(wanted == col, 1.0, 0.0).astype(BF)
    blocks[...] = dot(chosen, volume[...], NT).astype(BF)
    for t in range(27):
        sent[32 * t : 32 * t + 32, :] = jnp.concatenate([k2[t, :32, :], k2[t, 32:, :]], axis=1)
        sent[864 + 64 * t : 928 + 64 * t, :] = k3[t]
    sent[2592:2608, :] = b23[...]


def banded(k_ref):
    def pieces(dp, dw):
        k0, k1, k2 = (k_ref(9 * dp + 3 * dr + dw) for dr in range(3))
        none = jnp.zeros_like(k0)
        join = lambda a, b: jnp.concatenate([a, b], axis=1)
        return join(k1, k2), join(k0, k1), join(k2, none), join(none, k0)

    return pieces


def prep_kernel(half, k1, k2, got, w1a, w1c, w2a, w2c):
    mine = pl.multiple_of(half[0] * 64, 64)
    other = pl.multiple_of(64 - half[0] * 64, 64)
    one = banded(lambda t: k1[t])
    own = banded(lambda t: k2[t])

    def received(t):
        both = got[32 * t : 32 * t + 32, :]
        return jnp.concatenate([both[:, :64], both[:, 64:]], axis=0)

    far = banded(received)
    zero = jnp.zeros((64, 128), BF)
    for dp in range(3):
        for dw in range(3):
            t = 3 * dp + dw
            a, b, c, d = one(dp, dw)
            for i, (low, high) in enumerate(((a, zero), (b, c), (d, a), (zero, b))):
                w1a[64 * i : 64 * i + 64, 256 * t : 256 * t + 128] = low
                w1a[64 * i : 64 * i + 64, 256 * t + 128 : 256 * t + 256] = high
            lanes = slice(128 * t, 128 * t + 128)
            w1c[0:64, lanes] = d
            w1c[64:128, lanes] = c
            for at, pieces in ((mine, own), (other, far)):
                a, b, c, d = pieces(dp, dw)
                w2a[pl.ds(at, 64), lanes] = a
                w2a[pl.ds(128 + at, 64), lanes] = b
                w2c[pl.ds(at, 64), lanes] = c
                w2c[pl.ds(128 + at, 64), lanes] = d


def shifted(x, by):
    return pltpu.roll(x, (-by) % x.shape[0], 0)


def main_kernel(
    place, low, mid, high, w1a, w1c, w2a, w2c, k3, got, b1, b2, b3, out, q, x34, pd, hd
):
    half, layer, group, layers = place[0], place[1], place[2], place[3]
    planes = 3 + LAYER + 3
    pad = jnp.zeros((FRAME - RUN, 256), F32)
    lane = lax.broadcasted_iota(jnp.int32, (1, 128), 1)
    left = lane < 64

    for f in range(2):
        for par in range(2):
            runs = []
            for v in range(planes):
                src, at = ((low, v), (mid, v - 3), (high, v - 3 - LAYER))[
                    (v >= 3) + (v >= 3 + LAYER)
                ]
                runs.append(src[2 * at + f, RUN * par : RUN * par + RUN, :].astype(F32))
                runs.append(pad)
            whole = jnp.concatenate(runs, axis=0)
            q[f, 1 + par] = whole.astype(BF)
            if par == 0:
                q[f, 3] = shifted(whole, 1).astype(BF)
            else:
                q[f, 0] = shifted(whole, -1).astype(BF)
    for a in range(4):
        x34[a] = jnp.where(left, q[1, a, :, 0:128], q[0, a, :, 128:256])

    u = LAYER + 4
    m = u * FRAME
    taps = [(dp, dw) for dp in range(3) for dw in range(3)]

    def pick(ref, f, par):
        parts = [ref[f, par + dw, FRAME * dp : FRAME * dp + m, :] for dp, dw in taps]
        return jnp.concatenate(parts, axis=1)

    cross = []
    for par in range(2):
        parts = [x34[par + dw, FRAME * dp : FRAME * dp + m, :] for dp, dw in taps]
        cross.append(dot(jnp.concatenate(parts, axis=1), w1c[...], NT))
    bias = b1[...].astype(F32)
    row = lax.broadcasted_iota(jnp.int32, (m, 1), 0)
    pooled_col = 16 * group - LEAD + row % FRAME
    plane = LAYER * layer - 2 + row // FRAME
    inside = (plane >= 0) & (plane < LAYER * layers) & (pooled_col >= 0) & (pooled_col < 128)
    tiles = []
    for f in range(2):
        ys = []
        for par in range(2):
            y = dot(pick(q, f, par), w1a[...], NT)
            if f == 0:
                extra = jnp.where(left, 0.0, cross[par])
                y = jnp.concatenate([y[:, :128], y[:, 128:] + extra], axis=1)
            else:
                extra = jnp.where(left, cross[par], 0.0)
                y = jnp.concatenate([y[:, :128] + extra, y[:, 128:]], axis=1)
            y = jnp.maximum(y + bias, 0.0).astype(BF).astype(F32)
            for s in range(LAYER):
                top = FRAME * (2 + s) + LEAD
                out[2 * s + f, 16 * par : 16 * par + 16, :] = y[top : top + 16, :].astype(BF)
            ys.append(y)
        y = jnp.where(inside, jnp.maximum(ys[0], ys[1]), 0.0)
        y0, y1 = y[:, :128], y[:, 128:]
        y0 = jnp.maximum(y0, pltpu.roll(y0, 64, 1))
        y1 = jnp.maximum(y1, pltpu.roll(y1, 64, 1))
        tiles.append(jnp.where(left, y0, y1))
    pooled = jnp.concatenate(tiles, axis=1)

    for dw in range(3):
        pd[dw] = shifted(pooled, dw - 1).astype(BF)
    m = (LAYER + 2) * FRAME

    def lanes_of(ref, n, lo, hi):
        return [ref[dw, FRAME * dp : FRAME * dp + n, lo:hi] for dp, dw in taps]

    pairs = [dot(jnp.concatenate(lanes_of(pd, m, 128 * a, 128 * a + 128), axis=1), w2a[...], NT) for a in range(2)]
    parts = [jnp.where(left, b, a) for a, b in zip(lanes_of(pd, m, 0, 128), lanes_of(pd, m, 128, 256))]
    mixed = dot(jnp.concatenate(parts, axis=1), w2c[...], NT)
    row = lax.broadcasted_iota(jnp.int32, (m, 1), 0)
    pooled_col = 16 * group - LEAD + row % FRAME
    plane = LAYER * layer - 1 + row // FRAME
    inside = (plane >= 0) & (plane < LAYER * layers) & (pooled_col >= 0) & (pooled_col < 128)
    hidden = jnp.concatenate(
        [
            pairs[0][:, :128],
            pairs[0][:, 128:] + mixed[:, :128],
            pairs[1][:, :128] + mixed[:, 128:],
            pairs[1][:, 128:],
        ],
        axis=1,
    )
    bias = jnp.concatenate([b2[...].astype(F32)] * 4, axis=1)
    hidden = jnp.where(inside, jnp.maximum(hidden + bias, 0.0), 0.0).astype(BF).astype(F32)
    for dw in range(3):
        hd[dw] = shifted(hidden, dw - 1).astype(BF)

    m = LAYER * FRAME

    def third(t):
        return jnp.concatenate([k3[t], got[864 + 64 * t : 928 + 64 * t, :]], axis=0)

    none = jnp.zeros((128, 128), BF)
    straight, across = [[], []], [[], []]
    for dp, dw in taps:
        k0, k1, k2 = (third(9 * dp + 3 * dr + dw) for dr in range(3))
        straight[0] += [k1, k2]
        straight[1] += [k0, k1]
        across[0] += [none, k2]
        across[1] += [k0, none]
    w3a = jnp.concatenate([jnp.concatenate(rows, axis=1) for rows in straight], axis=0)
    w3c = jnp.concatenate([jnp.concatenate(rows, axis=1) for rows in across], axis=0)
    both = jnp.concatenate(
        [jnp.concatenate(lanes_of(hd, m, 256 * a, 256 * a + 256), axis=1) for a in range(2)], axis=0
    )
    both = dot(both, w3a, NT)
    mixed = dot(jnp.concatenate(lanes_of(hd, m, 128, 384), axis=1), w3c, NT)
    t0, t1 = both[:m, :128], both[:m, 128:] + mixed[:, :128]
    t2, t3 = both[m:, :128] + mixed[:, 128:], both[m:, 128:]
    bias = b3[...].astype(F32)
    t0, t1, t2, t3 = (jnp.maximum(t + bias, 0.0) for t in (t0, t1, t2, t3))
    r0, r1, r2, r3 = (pltpu.roll(t, 64, 1) for t in (t0, t1, t2, t3))
    first = jnp.concatenate([jnp.where(left, t0, r1), jnp.where(left, t2, r3)], axis=1)
    second = jnp.concatenate([jnp.where(left, r0, t1), jnp.where(left, r2, t3)], axis=1)
    for s in range(LAYER):
        top = FRAME * s + LEAD
        out[2 * s + half, 32:48, :] = first[top : top + 16, :].astype(BF)
        out[2 * s + 1 - half, 32:48, :] = second[top : top + 16, :].astype(BF)


def unpack_kernel(got, skip, features):
    count = got.shape[0]
    ones = got[:, 0:32, :].reshape(count * 32, 256)
    twos = got[:, 32:48, :].reshape(count * 16, 256)
    row = lax.broadcasted_iota(jnp.int32, (256, 256), 0)
    col = lax.broadcasted_iota(jnp.int32, (256, 256), 1)
    source = 32 * (row // 32) + 16 * (row % 2) + row % 32 // 2
    order = jnp.where(source == col, 1.0, 0.0).astype(BF)
    same = jnp.where(row == col, 1.0, 0.0).astype(BF)
    by_column = dot(order, ones, NN).astype(BF)
    skip[...] = dot(same, by_column, NT).astype(BF)
    features[...] = dot(same, twos, NT).astype(BF)


def vmem(count):
    return [pl.BlockSpec(memory_space=pltpu.VMEM)] * count


def smem(count):
    return [pl.BlockSpec(memory_space=pltpu.SMEM)] * count


def shape(*dims):
    return jax.ShapeDtypeStruct(dims, BF)


def by_columns(volume, kernel_one, bias_one, kernel_two, bias_two, kernel_three, bias_three):
    slabs, halves = lax.axis_size("slab"), lax.axis_size("filt")
    peers = LAYER * halves
    slab, half = lax.axis_index("slab"), lax.axis_index("filt")
    groups = [[peers * g + i for i in range(peers)] for g in range(slabs // LAYER)]
    exchange = functools.partial(
        lax.all_to_all,
        axis_name=("slab", "filt"),
        split_axis=0,
        concat_axis=0,
        axis_index_groups=groups,
        tiled=True,
    )
    biases = jnp.pad(jnp.concatenate([bias_two, bias_three])[None, :], ((0, 15), (0, 0)))
    blocks, sent = pl.pallas_call(
        pack_kernel,
        out_shape=(shape(peers * 2 * RUN, 256), shape(2608, 128)),
        in_specs=vmem(4),
        out_specs=tuple(vmem(2)),
        name="pack",
    )(volume.reshape(256, 256), kernel_two, kernel_three, biases)
    got = lax.ppermute(sent, "filt", [(0, 1), (1, 0)])
    mid = exchange(blocks.reshape(peers, 2 * RUN, 256))
    up = [(i, i + LAYER) for i in range(slabs - LAYER)]
    down = [(b, a) for a, b in up]
    low = lax.ppermute(mid[2:8], "slab", up)
    high = lax.ppermute(mid[0:6], "slab", down)
    place = jnp.stack([half, slab // LAYER, slab % LAYER * 2 + half, slabs // LAYER]).astype(jnp.int32)
    w1a, w1c, w2a, w2c = pl.pallas_call(
        prep_kernel,
        out_shape=(shape(256, 2304), shape(128, 1152), shape(256, 1152), shape(256, 1152)),
        in_specs=smem(1) + vmem(3),
        out_specs=tuple(vmem(4)),
        name="prep",
    )(place, kernel_one, kernel_two, got)
    their = got[2592]
    b1 = jnp.tile(bias_one, 4)[None, :]
    first = half == 0
    b2 = jnp.where(
        first, jnp.concatenate([bias_two, their[:64]]), jnp.concatenate([their[:64], bias_two])
    )[None, :]
    b3 = jnp.concatenate([bias_three, their[64:]])[None, :]
    frames = FRAME * (LAYER + 6)
    out = pl.pallas_call(
        main_kernel,
        out_shape=shape(peers, 48, 256),
        in_specs=smem(1) + vmem(12),
        out_specs=vmem(1)[0],
        scratch_shapes=[
            pltpu.VMEM((2, 4, frames, 256), BF),
            pltpu.VMEM((4, frames, 128), BF),
            pltpu.VMEM((3, FRAME * (LAYER + 4), 256), BF),
            pltpu.VMEM((3, FRAME * (LAYER + 2), 512), BF),
        ],
        name="sections",
    )(place, low, mid, high, w1a, w1c, w2a, w2c, kernel_three, got, b1, b2, b3)
    home = exchange(out)
    skip, features = pl.pallas_call(
        unpack_kernel,
        out_shape=(shape(256, 256), shape(256, 128)),
        in_specs=vmem(1),
        out_specs=tuple(vmem(2)),
        name="unpack",
    )(home)
    return skip.reshape(volume.shape), features.reshape(1, 4, 64, 128)


def per_device(volume, kernel_one, *rest):
    fits = (
        volume.shape == (1, 4, 64, 256)
        and lax.axis_size("filt") == 2
        and lax.axis_size("slab") % LAYER == 0
        and kernel_one.shape == (27, 64, 64)
        and rest[1].shape == (27, 64, 64)
        and rest[3].shape == (27, 64, 128)
    )
    return (by_columns if fits else by_planes)(volume, kernel_one, *rest)


def solution(mesh):
    return jax.shard_map(
        per_device,
        mesh=mesh,
        in_specs=(
            P("slab", "filt", None, None),
            P(),
            P(),
            P(None, "filt", None),
            P("filt"),
            P(None, "filt", None),
            P("filt"),
        ),
        out_specs=(P("slab", "filt", None, None), P("slab", None, "filt", None)),
        check_vma=False,
    )
```

```python
import functools

import jax
import jax.numpy as jnp
from jax import lax
from jax.experimental import pallas as pl
from jax.experimental.pallas import tpu as pltpu
from jax.sharding import PartitionSpec as P


BF = jnp.bfloat16
F32 = jnp.float32
NT = (((1,), (1,)), ((), ()))
NN = (((1,), (0,)), ((), ()))

LAYER = 4
RUN = 24
FRAME = 32
LEAD = 4


def extended(block, sides, width):
    for axis, dim in sides:
        count = lax.axis_size(axis)
        forward = [(i, i + 1) for i in range(count - 1)]
        backward = [(target, source) for source, target in forward]
        low = lax.ppermute(
            lax.slice_in_dim(block, block.shape[dim] - width, None, axis=dim), axis, forward
        )
        high = lax.ppermute(lax.slice_in_dim(block, 0, width, axis=dim), axis, backward)
        block = jnp.concatenate([low, block, high], axis=dim)
    return block


def pad_columns(field):
    return jnp.pad(field, ((0, 0), (0, 0), (0, 0), (1, 1)))


def accumulate(total, padded, kernel):
    planes, rows, _, cols = total.shape
    for kd in range(3):
        for kh in range(3):
            for kw in range(3):
                tap = 9 * kd + 3 * kh + kw
                total = total + jnp.einsum(
                    "oc,dhcw->dhow",
                    kernel[tap],
                    padded[kd : kd + planes, kh : kh + rows, :, kw : kw + cols],
                    preferred_element_type=jnp.float32,
                )
    return total


def finish(total, bias):
    return jnp.maximum(total + bias.astype(jnp.float32)[None, None, :, None], 0.0).astype(
        jnp.bfloat16
    )


def by_planes(volume, kernel_one, bias_one, kernel_two, bias_two, kernel_three, bias_three):
    planes, rows, chans, cols = volume.shape
    rimmed = extended(volume, (("slab", 0), ("filt", 1)), 1)
    start_one = jnp.zeros((planes, rows, kernel_one.shape[1], cols), jnp.float32)
    skip_one = finish(accumulate(start_one, pad_columns(rimmed), kernel_one), bias_one)
    pooled = jnp.max(skip_one.reshape(planes, rows // 2, 2, chans, cols // 2, 2), axis=(2, 5))
    full_rows = lax.all_gather(pooled, "filt", axis=1, tiled=True)
    planed = extended(full_rows, (("slab", 0),), 1)
    padded = jnp.pad(planed, ((0, 0), (1, 1), (0, 0), (1, 1)))
    height = full_rows.shape[1]
    width = full_rows.shape[3]
    start_two = jnp.zeros((planes, height, kernel_two.shape[1], width), jnp.float32)
    hidden = finish(accumulate(start_two, padded, kernel_two), bias_two)
    hidden_planes = extended(hidden, (("slab", 0),), 1)
    start_three = jnp.zeros((planes, height, kernel_three.shape[1], width), jnp.float32)
    piece_padded = jnp.pad(
        lax.all_gather(hidden_planes, "filt", axis=2, tiled=True), ((0, 0), (1, 1), (0, 0), (1, 1))
    )
    summed = accumulate(start_three, piece_padded, kernel_three)
    features_two = finish(summed, bias_three)
    return (skip_one, features_two)


def dot(a, b, dims):
    return lax.dot_general(a, b, dims, preferred_element_type=F32)


def pack_kernel(volume, blocks):
    count, width = blocks.shape[0], volume.shape[1]
    shape = (count * 2 * RUN, width)
    row = lax.broadcasted_iota(jnp.int32, shape, 0)
    col = lax.broadcasted_iota(jnp.int32, shape, 1)
    peer, rest = row // (2 * RUN), row % (2 * RUN)
    wanted = (width // count) * peer + 2 * (rest % RUN - LEAD) + rest // RUN
    chosen = jnp.where(wanted == col, 1.0, 0.0).astype(BF)
    blocks[...] = dot(chosen, volume[...], NT).astype(BF).reshape(blocks.shape)


def aligned(at, by):
    return pl.multiple_of(at, by)


def send_kernel(after, k2, k3, b2, b3, sent):
    core = lax.axis_index("slab") % 2
    top = 32 * core
    for t in range(27):
        low = k2[t, pl.ds(aligned(top, 16), 16), :]
        high = k2[t, pl.ds(aligned(top + 16, 16), 16), :]
        sent[16 * t : 16 * t + 16, :] = jnp.concatenate([low, high], axis=1)
        sent[432 + 32 * t : 464 + 32 * t, :] = k3[t, pl.ds(aligned(top, 32), 32), :]
    both = jnp.concatenate([b2[...], b3[...]], axis=1)
    sent[1296:1312, :] = jnp.broadcast_to(both, (16, 128))


def banded(k_ref):
    def pieces(dp, dw):
        k0, k1, k2 = (k_ref(9 * dp + 3 * dr + dw) for dr in range(3))
        none = jnp.zeros_like(k0)
        join = lambda a, b: jnp.concatenate([a, b], axis=1)
        return join(k1, k2), join(k0, k1), join(k2, none), join(none, k0)

    return pieces


def first_kernel(after, k1, b1, w1a, w1c, bias):
    one = banded(lambda t: k1[t])
    zero = jnp.zeros((64, 128), BF)
    for dp in range(3):
        for dw in range(3):
            t = 3 * dp + dw
            a, b, c, d = one(dp, dw)
            for i, (low, high) in enumerate(((a, zero), (b, c), (d, a), (zero, b))):
                w1a[64 * i : 64 * i + 64, 256 * t : 256 * t + 128] = low
                w1a[64 * i : 64 * i + 64, 256 * t + 128 : 256 * t + 256] = high
            lanes = slice(128 * t, 128 * t + 128)
            w1c[0:64, lanes] = d
            w1c[64:128, lanes] = c
    bias[...] = jnp.broadcast_to(jnp.concatenate([b1[...].astype(F32)] * 4, axis=1), bias.shape)


def second_kernel(k2, k3, b2, b3, over, beside, w2a, w2c, w3, bias2, bias3):
    half, core = lax.axis_index("filt"), lax.axis_index("slab") % 2
    mine, other = half * 64, 64 - half * 64

    def own(t):
        return k2[t]

    def piece(ref):
        def rows(t):
            both = ref[16 * t : 16 * t + 16, :]
            return jnp.concatenate([both[:, :64], both[:, 64:]], axis=0)

        return rows

    sources = (
        (own, mine, 64),
        (piece(over), other + 32 * core, 32),
        (piece(beside), other + 32 - 32 * core, 32),
    )
    for dp in range(3):
        for dw in range(3):
            t = 3 * dp + dw
            lanes = slice(128 * t, 128 * t + 128)
            for rows, at, size in sources:
                a, b, c, d = banded(rows)(dp, dw)
                w2a[pl.ds(aligned(at, 32), size), lanes] = a
                w2a[pl.ds(aligned(128 + at, 32), size), lanes] = b
                w2c[pl.ds(aligned(at, 32), size), lanes] = c
                w2c[pl.ds(aligned(128 + at, 32), size), lanes] = d
    for t in range(27):
        w3[t, 0:64, :] = k3[t]
        w3[t, pl.ds(aligned(64 + 32 * core, 32), 32), :] = over[432 + 32 * t : 464 + 32 * t, :]
        w3[t, pl.ds(aligned(96 - 32 * core, 32), 32), :] = beside[432 + 32 * t : 464 + 32 * t, :]
    theirs = over[1296:1297, :].astype(F32)
    b2, b3 = b2[...].astype(F32), b3[...].astype(F32)
    there2, there3 = theirs[:, :64], theirs[:, 64:]
    low = jnp.where(half == 0, b2, there2)
    high = jnp.where(half == 0, there2, b2)
    bias2[...] = jnp.broadcast_to(jnp.concatenate([low, high], axis=1), bias2.shape)
    bias3[...] = jnp.broadcast_to(jnp.concatenate([b3, there3], axis=1), bias3.shape)


def shifted(x, by):
    return pltpu.roll(x, (-by) % x.shape[0], 0)


def main_kernel(
    low, mid, high, w1a, w1c, w2a, w2c, w3, b1, b2, b3, out, q, x34, pd, hd
):
    half, slab = lax.axis_index("filt"), lax.axis_index("slab")
    layer, layers = slab // LAYER, lax.axis_size("slab") // LAYER
    group = slab % LAYER * lax.axis_size("filt") + half
    planes = 3 + LAYER + 3
    pad = jnp.zeros((FRAME - RUN, 256), F32)
    lane = lax.broadcasted_iota(jnp.int32, (1, 128), 1)
    left = lane < 64

    for f in range(2):
        for par in range(2):
            runs = []
            for v in range(planes):
                src, at = ((low, v), (mid, v - 3), (high, v - 3 - LAYER))[
                    (v >= 3) + (v >= 3 + LAYER)
                ]
                runs.append(src[2 * at + f, RUN * par : RUN * par + RUN, :].astype(F32))
                runs.append(pad)
            whole = jnp.concatenate(runs, axis=0)
            q[f, 1 + par] = whole.astype(BF)
            if par == 0:
                q[f, 3] = shifted(whole, 1).astype(BF)
            else:
                q[f, 0] = shifted(whole, -1).astype(BF)
    for a in range(4):
        x34[a] = jnp.where(left, q[1, a, :, 0:128], q[0, a, :, 128:256])

    u = LAYER + 4
    m = u * FRAME
    taps = [(dp, dw) for dp in range(3) for dw in range(3)]

    def pick(ref, f, par):
        parts = [ref[f, par + dw, FRAME * dp : FRAME * dp + m, :] for dp, dw in taps]
        return jnp.concatenate(parts, axis=1)

    cross = []
    for par in range(2):
        parts = [x34[par + dw, FRAME * dp : FRAME * dp + m, :] for dp, dw in taps]
        cross.append(dot(jnp.concatenate(parts, axis=1), w1c[...], NT))
    bias = b1[0:1, :]
    row = lax.broadcasted_iota(jnp.int32, (m, 1), 0)
    pooled_col = 16 * group - LEAD + row % FRAME
    plane = LAYER * layer - 2 + row // FRAME
    inside = (plane >= 0) & (plane < LAYER * layers) & (pooled_col >= 0) & (pooled_col < 128)
    tiles = []
    for f in range(2):
        ys = []
        for par in range(2):
            y = dot(pick(q, f, par), w1a[...], NT)
            if f == 0:
                extra = jnp.where(left, 0.0, cross[par])
                y = jnp.concatenate([y[:, :128], y[:, 128:] + extra], axis=1)
            else:
                extra = jnp.where(left, cross[par], 0.0)
                y = jnp.concatenate([y[:, :128] + extra, y[:, 128:]], axis=1)
            y = jnp.maximum(y + bias, 0.0).astype(BF).astype(F32)
            for s in range(LAYER):
                top = FRAME * (2 + s) + LEAD
                out[2 * s + f, 16 * par : 16 * par + 16, :] = y[top : top + 16, :].astype(BF)
            ys.append(y)
        y = jnp.where(inside, jnp.maximum(ys[0], ys[1]), 0.0)
        y0, y1 = y[:, :128], y[:, 128:]
        y0 = jnp.maximum(y0, pltpu.roll(y0, 64, 1))
        y1 = jnp.maximum(y1, pltpu.roll(y1, 64, 1))
        tiles.append(jnp.where(left, y0, y1))
    pooled = jnp.concatenate(tiles, axis=1)

    for dw in range(3):
        pd[dw] = shifted(pooled, dw - 1).astype(BF)
    m = (LAYER + 2) * FRAME

    def lanes_of(ref, n, lo, hi):
        return [ref[dw, FRAME * dp : FRAME * dp + n, lo:hi] for dp, dw in taps]

    pairs = [dot(jnp.concatenate(lanes_of(pd, m, 128 * a, 128 * a + 128), axis=1), w2a[...], NT) for a in range(2)]
    parts = [jnp.where(left, b, a) for a, b in zip(lanes_of(pd, m, 0, 128), lanes_of(pd, m, 128, 256))]
    mixed = dot(jnp.concatenate(parts, axis=1), w2c[...], NT)
    row = lax.broadcasted_iota(jnp.int32, (m, 1), 0)
    pooled_col = 16 * group - LEAD + row % FRAME
    plane = LAYER * layer - 1 + row // FRAME
    inside = (plane >= 0) & (plane < LAYER * layers) & (pooled_col >= 0) & (pooled_col < 128)
    hidden = jnp.concatenate(
        [
            pairs[0][:, :128],
            pairs[0][:, 128:] + mixed[:, :128],
            pairs[1][:, :128] + mixed[:, 128:],
            pairs[1][:, 128:],
        ],
        axis=1,
    )
    bias = jnp.concatenate([b2[0:1, :]] * 4, axis=1)
    hidden = jnp.where(inside, jnp.maximum(hidden + bias, 0.0), 0.0).astype(BF).astype(F32)
    for dw in range(3):
        hd[dw] = shifted(hidden, dw - 1).astype(BF)

    m = LAYER * FRAME

    none = jnp.zeros((128, 128), BF)
    straight, across = [[], []], [[], []]
    for dp, dw in taps:
        k0, k1, k2 = (w3[9 * dp + 3 * dr + dw] for dr in range(3))
        straight[0] += [k1, k2]
        straight[1] += [k0, k1]
        across[0] += [none, k2]
        across[1] += [k0, none]
    w3a = jnp.concatenate([jnp.concatenate(rows, axis=1) for rows in straight], axis=0)
    w3c = jnp.concatenate([jnp.concatenate(rows, axis=1) for rows in across], axis=0)
    both = jnp.concatenate(
        [jnp.concatenate(lanes_of(hd, m, 256 * a, 256 * a + 256), axis=1) for a in range(2)], axis=0
    )
    both = dot(both, w3a, NT)
    mixed = dot(jnp.concatenate(lanes_of(hd, m, 128, 384), axis=1), w3c, NT)
    t0, t1 = both[:m, :128], both[:m, 128:] + mixed[:, :128]
    t2, t3 = both[m:, :128] + mixed[:, 128:], both[m:, 128:]
    bias = b3[0:1, :]
    t0, t1, t2, t3 = (jnp.maximum(t + bias, 0.0) for t in (t0, t1, t2, t3))
    r0, r1, r2, r3 = (pltpu.roll(t, 64, 1) for t in (t0, t1, t2, t3))
    first = jnp.concatenate([jnp.where(left, t0, r1), jnp.where(left, t2, r3)], axis=1)
    second = jnp.concatenate([jnp.where(left, r0, t1), jnp.where(left, r2, t3)], axis=1)
    for s in range(LAYER):
        top = FRAME * s + LEAD
        out[2 * s + half, 32:48, :] = first[top : top + 16, :].astype(BF)
        out[2 * s + 1 - half, 32:48, :] = second[top : top + 16, :].astype(BF)


def unpack_kernel(got, skip, features):
    count = got.shape[0]
    ones = got[:, 0:32, :].reshape(count * 32, 256)
    twos = got[:, 32:48, :].reshape(count * 16, 256)
    row = lax.broadcasted_iota(jnp.int32, (256, 256), 0)
    col = lax.broadcasted_iota(jnp.int32, (256, 256), 1)
    source = 32 * (row // 32) + 16 * (row % 2) + row % 32 // 2
    order = jnp.where(source == col, 1.0, 0.0).astype(BF)
    same = jnp.where(row == col, 1.0, 0.0).astype(BF)
    by_column = dot(order, ones, NN).astype(BF)
    skip[...] = dot(same, by_column, NT).astype(BF)
    features[...] = dot(same, twos, NT).astype(BF)


def shape(*dims):
    return jax.ShapeDtypeStruct(dims, BF)


def call(kernel, outs, *operands, scratch=(), limit=8):
    spec = pl.BlockSpec(memory_space=pltpu.VMEM)
    return pl.pallas_call(
        kernel,
        out_shape=outs,
        in_specs=[spec] * len(operands),
        out_specs=jax.tree.map(lambda _: spec, outs),
        scratch_shapes=scratch,
        compiler_params=pltpu.CompilerParams(vmem_limit_bytes=limit << 20),
    )(*operands)


def near(x):
    return pltpu.with_memory_space_constraint(x, pltpu.VMEM)


def by_columns(volume, kernel_one, bias_one, kernel_two, bias_two, kernel_three, bias_three):
    slabs, halves = lax.axis_size("slab"), lax.axis_size("filt")
    peers = LAYER * halves
    groups = [[peers * g + i for i in range(peers)] for g in range(slabs // LAYER)]
    exchange = functools.partial(
        lax.all_to_all,
        axis_name=("slab", "filt"),
        split_axis=0,
        concat_axis=0,
        axis_index_groups=groups,
        tiled=True,
    )
    b1, b2, b3 = bias_one[None, :], bias_two[None, :], bias_three[None, :]
    blocks = call(pack_kernel, pltpu.VMEM((peers, 2 * RUN, 256), BF), volume.reshape(256, 256))
    mid = exchange(blocks)
    blocks = near(blocks)
    sent = call(send_kernel, pltpu.VMEM((1312, 128), BF), blocks, kernel_two, kernel_three, b2, b3)
    over = lax.ppermute(sent, "filt", [(0, 1), (1, 0)])
    w1a, w1c, bias1 = call(
        first_kernel,
        (pltpu.VMEM((256, 2304), BF), pltpu.VMEM((128, 1152), BF), pltpu.VMEM((8, 256), F32)),
        blocks,
        kernel_one,
        b1,
    )
    up = [(i, i + LAYER) for i in range(slabs - LAYER)]
    down = [(b, a) for a, b in up]
    low = lax.ppermute(mid[2:8], "slab", up)
    high = lax.ppermute(mid[0:6], "slab", down)
    beside = lax.ppermute(over, "slab", [(i, i ^ 1) for i in range(slabs)])
    w2a, w2c, w3, bias2, bias3 = call(
        second_kernel,
        (
            pltpu.VMEM((256, 1152), BF),
            pltpu.VMEM((256, 1152), BF),
            pltpu.VMEM((27, 128, 128), BF),
            pltpu.VMEM((8, 128), F32),
            pltpu.VMEM((8, 128), F32),
        ),
        kernel_two,
        kernel_three,
        b2,
        b3,
        near(over),
        near(beside),
    )
    frames = FRAME * (LAYER + 6)
    operands = (low, mid, high, w1a, w1c, w2a, w2c, w3, bias1, bias2, bias3)
    out = call(
        main_kernel,
        pltpu.VMEM((peers, 48, 256), BF),
        *map(near, operands),
        scratch=[
            pltpu.VMEM((2, 4, frames, 256), BF),
            pltpu.VMEM((4, frames, 128), BF),
            pltpu.VMEM((3, FRAME * (LAYER + 4), 256), BF),
            pltpu.VMEM((3, FRAME * (LAYER + 2), 512), BF),
        ],
        limit=24,
    )
    home = exchange(out)
    skip, features = call(unpack_kernel, (shape(256, 256), shape(256, 128)), near(home))
    return skip.reshape(volume.shape), features.reshape(1, 4, 64, 128)


def fits(volume, kernels, slabs, halves):
    return (
        volume == (1, 4, 64, 256)
        and kernels == [(27, 64, 64), (27, 64, 64), (27, 64, 128)]
        and halves == 2
        and slabs % LAYER == 0
    )


def per_device(volume, *rest):
    kernels = [r.shape for r in rest[::2]]
    good = fits(volume.shape, kernels, lax.axis_size("slab"), lax.axis_size("filt"))
    if not good:
        return by_planes(volume, *rest)
    return by_columns(volume, *rest)


def solution(mesh):
    return jax.shard_map(
        per_device,
        mesh=mesh,
        in_specs=(
            P("slab", "filt", None, None),
            P(),
            P(),
            P(None, "filt", None),
            P("filt"),
            P(None, "filt", None),
            P("filt"),
        ),
        out_specs=(P("slab", "filt", None, None), P("slab", None, "filt", None)),
        check_vma=False,
    )
```

```python
import functools

import jax
import jax.numpy as jnp
from jax import lax
from jax.experimental import pallas as pl
from jax.experimental.pallas import tpu as pltpu
from jax.sharding import PartitionSpec as P


BF = jnp.bfloat16
F32 = jnp.float32
NT = (((1,), (1,)), ((), ()))
NN = (((1,), (0,)), ((), ()))

LAYER = 4
RUN = 24
FRAME = RUN
LEAD = 4


def extended(block, sides, width):
    for axis, dim in sides:
        count = lax.axis_size(axis)
        forward = [(i, i + 1) for i in range(count - 1)]
        backward = [(target, source) for source, target in forward]
        low = lax.ppermute(
            lax.slice_in_dim(block, block.shape[dim] - width, None, axis=dim), axis, forward
        )
        high = lax.ppermute(lax.slice_in_dim(block, 0, width, axis=dim), axis, backward)
        block = jnp.concatenate([low, block, high], axis=dim)
    return block


def pad_columns(field):
    return jnp.pad(field, ((0, 0), (0, 0), (0, 0), (1, 1)))


def accumulate(total, padded, kernel):
    planes, rows, _, cols = total.shape
    for kd in range(3):
        for kh in range(3):
            for kw in range(3):
                tap = 9 * kd + 3 * kh + kw
                total = total + jnp.einsum(
                    "oc,dhcw->dhow",
                    kernel[tap],
                    padded[kd : kd + planes, kh : kh + rows, :, kw : kw + cols],
                    preferred_element_type=jnp.float32,
                )
    return total


def finish(total, bias):
    return jnp.maximum(total + bias.astype(jnp.float32)[None, None, :, None], 0.0).astype(
        jnp.bfloat16
    )


def by_planes(volume, kernel_one, bias_one, kernel_two, bias_two, kernel_three, bias_three):
    planes, rows, chans, cols = volume.shape
    rimmed = extended(volume, (("slab", 0), ("filt", 1)), 1)
    start_one = jnp.zeros((planes, rows, kernel_one.shape[1], cols), jnp.float32)
    skip_one = finish(accumulate(start_one, pad_columns(rimmed), kernel_one), bias_one)
    pooled = jnp.max(skip_one.reshape(planes, rows // 2, 2, chans, cols // 2, 2), axis=(2, 5))
    full_rows = lax.all_gather(pooled, "filt", axis=1, tiled=True)
    planed = extended(full_rows, (("slab", 0),), 1)
    padded = jnp.pad(planed, ((0, 0), (1, 1), (0, 0), (1, 1)))
    height = full_rows.shape[1]
    width = full_rows.shape[3]
    start_two = jnp.zeros((planes, height, kernel_two.shape[1], width), jnp.float32)
    hidden = finish(accumulate(start_two, padded, kernel_two), bias_two)
    hidden_planes = extended(hidden, (("slab", 0),), 1)
    start_three = jnp.zeros((planes, height, kernel_three.shape[1], width), jnp.float32)
    piece_padded = jnp.pad(
        lax.all_gather(hidden_planes, "filt", axis=2, tiled=True), ((0, 0), (1, 1), (0, 0), (1, 1))
    )
    summed = accumulate(start_three, piece_padded, kernel_three)
    features_two = finish(summed, bias_three)
    return (skip_one, features_two)


def dot(a, b, dims):
    return lax.dot_general(a, b, dims, preferred_element_type=F32)


def pack_kernel(far, blocks, volume, sem):
    copy = pltpu.make_async_copy(far, volume, sem)
    copy.start()
    count, width = blocks.shape[0], volume.shape[1]
    shape = (count * 2 * RUN, width)
    row = lax.broadcasted_iota(jnp.int32, shape, 0)
    col = lax.broadcasted_iota(jnp.int32, shape, 1)
    peer, rest = row // (2 * RUN), row % (2 * RUN)
    wanted = (width // count) * peer + 2 * (rest % RUN - LEAD) + rest // RUN
    chosen = jnp.where(wanted == col, 1.0, 0.0).astype(BF)
    copy.wait()
    blocks[...] = dot(chosen, volume[...], NT).astype(BF).reshape(blocks.shape)


def aligned(at, by):
    return pl.multiple_of(at, by)


def send_kernel(far2, far3, far_b2, far_b3, sent, k2, k3, b2, b3, sems):
    top = aligned(32 * (lax.axis_index("slab") % 2), 32)
    half = pl.ds(top, 32)
    copies = [
        pltpu.make_async_copy(far, near, sems.at[i])
        for i, (far, near) in enumerate(
            ((far_b2, b2), (far_b3, b3), (far2.at[:, half, :], k2), (far3.at[:, half, :], k3))
        )
    ]
    for copy in copies:
        copy.start()
    for copy in copies:
        copy.wait()
    for t in range(27):
        sent[16 * t : 16 * t + 16, :] = jnp.concatenate([k2[t, :16, :], k2[t, 16:, :]], axis=1)
        sent[432 + 32 * t : 464 + 32 * t, :] = k3[t]
    both = jnp.concatenate([b2[...], b3[...]], axis=1)
    sent[1296:1312, :] = jnp.broadcast_to(both, (16, 128))


def banded(k_ref):
    def pieces(dp, dw):
        k0, k1, k2 = (k_ref(9 * dp + 3 * dr + dw) for dr in range(3))
        none = jnp.zeros_like(k0)
        join = lambda a, b: jnp.concatenate([a, b], axis=1)
        return join(k1, k2), join(k0, k1), join(k2, none), join(none, k0)

    return pieces


def rim_kernel(mid, to_first, to_second):
    odd = lax.axis_index("slab") // LAYER % 2
    n = to_first.shape[0]
    to_first[...] = mid[pl.ds(2 - 2 * odd, n)]
    to_second[...] = mid[pl.ds(2 * odd, n)]


def first_kernel(k1, b1, w1a, w1c, bias):
    one = banded(lambda t: k1[t])
    zero = jnp.zeros((64, 128), BF)
    for dp in range(3):
        for dw in range(3):
            t = 3 * dp + dw
            a, b, c, d = one(dp, dw)
            for i, (low, high) in enumerate(((a, zero), (b, c), (d, a), (zero, b))):
                w1a[64 * i : 64 * i + 64, 256 * t : 256 * t + 128] = low
                w1a[64 * i : 64 * i + 64, 256 * t + 128 : 256 * t + 256] = high
            lanes = slice(128 * t, 128 * t + 128)
            w1c[0:64, lanes] = d
            w1c[64:128, lanes] = c
    bias[...] = jnp.broadcast_to(jnp.concatenate([b1[...].astype(F32)] * 4, axis=1), bias.shape)


def second_kernel(k2, k3, b2, b3, over, beside, w2a, w2c, w3, bias2, bias3):
    half, core = lax.axis_index("filt"), lax.axis_index("slab") % 2
    mine, other = half * 64, 64 - half * 64

    def own(t):
        return k2[t]

    def piece(ref):
        def rows(t):
            both = ref[16 * t : 16 * t + 16, :]
            return jnp.concatenate([both[:, :64], both[:, 64:]], axis=0)

        return rows

    sources = (
        (own, mine, 64),
        (piece(over), other + 32 * core, 32),
        (piece(beside), other + 32 - 32 * core, 32),
    )
    for dp in range(3):
        for dw in range(3):
            t = 3 * dp + dw
            lanes = slice(128 * t, 128 * t + 128)
            for rows, at, size in sources:
                a, b, c, d = banded(rows)(dp, dw)
                w2a[pl.ds(aligned(at, 32), size), lanes] = a
                w2a[pl.ds(aligned(128 + at, 32), size), lanes] = b
                w2c[pl.ds(aligned(at, 32), size), lanes] = c
                w2c[pl.ds(aligned(128 + at, 32), size), lanes] = d
    for t in range(27):
        w3[t, 0:64, :] = k3[t]
        w3[t, pl.ds(aligned(64 + 32 * core, 32), 32), :] = over[432 + 32 * t : 464 + 32 * t, :]
        w3[t, pl.ds(aligned(96 - 32 * core, 32), 32), :] = beside[432 + 32 * t : 464 + 32 * t, :]
    theirs = over[1296:1297, :].astype(F32)
    b2, b3 = b2[...].astype(F32), b3[...].astype(F32)
    there2, there3 = theirs[:, :64], theirs[:, 64:]
    low = jnp.where(half == 0, b2, there2)
    high = jnp.where(half == 0, there2, b2)
    bias2[...] = jnp.broadcast_to(jnp.concatenate([low, high], axis=1), bias2.shape)
    bias3[...] = jnp.broadcast_to(jnp.concatenate([b3, there3], axis=1), bias3.shape)


def shifted(x, by):
    return pltpu.roll(x, (-by) % x.shape[0], 0)


def main_kernel(
    rim_a, mid, rim_b, w1a, w1c, w2a, w2c, w3, b1, b2, b3, out, q, x34, pd, hd
):
    half, slab = lax.axis_index("filt"), lax.axis_index("slab")
    layer, layers = slab // LAYER, lax.axis_size("slab") // LAYER
    group = slab % LAYER * lax.axis_size("filt") + half
    planes = 3 + LAYER + 3
    odd = layer % 2 == 1
    lane = lax.broadcasted_iota(jnp.int32, (1, 128), 1)
    left = lane < 64

    for f in range(2):
        for par in range(2):
            runs = []
            for v in range(planes):
                rows = slice(RUN * par, RUN * par + RUN)
                if 3 <= v < 3 + LAYER:
                    run = mid[2 * (v - 3) + f, rows, :]
                else:
                    at = 2 * (v if v < 3 else v - 3 - LAYER) + f
                    run = jnp.where(odd == (v < 3), rim_a[at, rows, :], rim_b[at, rows, :])
                runs.append(run.astype(F32))
            whole = jnp.concatenate(runs, axis=0)
            q[f, 1 + par] = whole.astype(BF)
            if par == 0:
                q[f, 3] = shifted(whole, 1).astype(BF)
            else:
                q[f, 0] = shifted(whole, -1).astype(BF)
    for a in range(4):
        x34[a] = jnp.where(left, q[1, a, :, 0:128], q[0, a, :, 128:256])

    u = LAYER + 4
    m = u * FRAME
    taps = [(dp, dw) for dp in range(3) for dw in range(3)]

    def pick(ref, f, par):
        parts = [ref[f, par + dw, FRAME * dp : FRAME * dp + m, :] for dp, dw in taps]
        return jnp.concatenate(parts, axis=1)

    def pick34(par):
        parts = [x34[par + dw, FRAME * dp : FRAME * dp + m, :] for dp, dw in taps]
        return jnp.concatenate(parts, axis=1)

    def pair(parts, weights):
        n = parts[0].shape[0]
        all_rows = dot(jnp.concatenate(parts, axis=0), weights, NT)
        return [all_rows[n * i : n * i + n] for i in range(len(parts))]

    cross = pair([pick34(0), pick34(1)], w1c[...])
    sums = []
    for f in range(2):
        sums += pair([pick(q, f, par) for par in range(2)], w1a[...])
    bias = b1[0:1, :]
    row = lax.broadcasted_iota(jnp.int32, (m, 1), 0)
    pooled_col = 16 * group - LEAD + row % FRAME
    plane = LAYER * layer - 2 + row // FRAME
    inside = (plane >= 0) & (plane < LAYER * layers) & (pooled_col >= 0) & (pooled_col < 128)
    tiles = []
    for f in range(2):
        ys = []
        for par in range(2):
            y = sums[2 * f + par]
            if f == 0:
                extra = jnp.where(left, 0.0, cross[par])
                y = jnp.concatenate([y[:, :128], y[:, 128:] + extra], axis=1)
            else:
                extra = jnp.where(left, cross[par], 0.0)
                y = jnp.concatenate([y[:, :128] + extra, y[:, 128:]], axis=1)
            y = jnp.maximum(y + bias, 0.0).astype(BF).astype(F32)
            for s in range(LAYER):
                top = FRAME * (2 + s) + LEAD
                out[2 * s + f, 16 * par : 16 * par + 16, :] = y[top : top + 16, :].astype(BF)
            ys.append(y)
        y = jnp.where(inside, jnp.maximum(ys[0], ys[1]), 0.0)
        y0, y1 = y[:, :128], y[:, 128:]
        y0 = jnp.maximum(y0, pltpu.roll(y0, 64, 1))
        y1 = jnp.maximum(y1, pltpu.roll(y1, 64, 1))
        tiles.append(jnp.where(left, y0, y1))
    pooled = jnp.concatenate(tiles, axis=1)

    for dw in range(3):
        pd[dw] = shifted(pooled, dw - 1).astype(BF)
    m = (LAYER + 2) * FRAME

    def lanes_of(ref, n, lo, hi):
        return [ref[dw, FRAME * dp : FRAME * dp + n, lo:hi] for dp, dw in taps]

    pairs = pair(
        [jnp.concatenate(lanes_of(pd, m, 128 * a, 128 * a + 128), axis=1) for a in range(2)],
        w2a[...],
    )
    parts = [jnp.where(left, b, a) for a, b in zip(lanes_of(pd, m, 0, 128), lanes_of(pd, m, 128, 256))]
    mixed = dot(jnp.concatenate(parts, axis=1), w2c[...], NT)
    row = lax.broadcasted_iota(jnp.int32, (m, 1), 0)
    pooled_col = 16 * group - LEAD + row % FRAME
    plane = LAYER * layer - 1 + row // FRAME
    inside = (plane >= 0) & (plane < LAYER * layers) & (pooled_col >= 0) & (pooled_col < 128)
    hidden = jnp.concatenate(
        [
            pairs[0][:, :128],
            pairs[0][:, 128:] + mixed[:, :128],
            pairs[1][:, :128] + mixed[:, 128:],
            pairs[1][:, 128:],
        ],
        axis=1,
    )
    bias = jnp.concatenate([b2[0:1, :]] * 4, axis=1)
    hidden = jnp.where(inside, jnp.maximum(hidden + bias, 0.0), 0.0).astype(BF).astype(F32)
    for dw in range(3):
        hd[dw] = shifted(hidden, dw - 1).astype(BF)

    m = LAYER * FRAME

    none = jnp.zeros((128, 128), BF)
    straight, across = [[], []], [[], []]
    for dp, dw in taps:
        k0, k1, k2 = (w3[9 * dp + 3 * dr + dw] for dr in range(3))
        straight[0] += [k1, k2]
        straight[1] += [k0, k1]
        across[0] += [none, k2]
        across[1] += [k0, none]
    w3a = jnp.concatenate([jnp.concatenate(rows, axis=1) for rows in straight], axis=0)
    w3c = jnp.concatenate([jnp.concatenate(rows, axis=1) for rows in across], axis=0)
    both = jnp.concatenate(
        [jnp.concatenate(lanes_of(hd, m, 256 * a, 256 * a + 256), axis=1) for a in range(2)], axis=0
    )
    both = dot(both, w3a, NT)
    mixed = dot(jnp.concatenate(lanes_of(hd, m, 128, 384), axis=1), w3c, NT)
    t0, t1 = both[:m, :128], both[:m, 128:] + mixed[:, :128]
    t2, t3 = both[m:, :128] + mixed[:, 128:], both[m:, 128:]
    bias = b3[0:1, :]
    t0, t1, t2, t3 = (jnp.maximum(t + bias, 0.0) for t in (t0, t1, t2, t3))
    r0, r1, r2, r3 = (pltpu.roll(t, 64, 1) for t in (t0, t1, t2, t3))
    first = jnp.concatenate([jnp.where(left, t0, r1), jnp.where(left, t2, r3)], axis=1)
    second = jnp.concatenate([jnp.where(left, r0, t1), jnp.where(left, r2, t3)], axis=1)
    for s in range(LAYER):
        top = FRAME * s + LEAD
        out[2 * s + half, 32:48, :] = first[top : top + 16, :].astype(BF)
        out[2 * s + 1 - half, 32:48, :] = second[top : top + 16, :].astype(BF)


def unpack_kernel(got, skip, features):
    count = got.shape[0]
    ones = got[:, 0:32, :].reshape(count * 32, 256)
    twos = got[:, 32:48, :].reshape(count * 16, 256)
    row = lax.broadcasted_iota(jnp.int32, (256, 256), 0)
    col = lax.broadcasted_iota(jnp.int32, (256, 256), 1)
    source = 32 * (row // 32) + 16 * (row % 2) + row % 32 // 2
    order = jnp.where(source == col, 1.0, 0.0).astype(BF)
    same = jnp.where(row == col, 1.0, 0.0).astype(BF)
    by_column = dot(order, ones, NN).astype(BF)
    skip[...] = dot(same, by_column, NT).astype(BF)
    features[...] = dot(same, twos, NT).astype(BF)


def shape(*dims):
    return jax.ShapeDtypeStruct(dims, BF)


def call(kernel, outs, *operands, scratch=(), limit=8, far=False):
    spec = pl.BlockSpec(memory_space=pltpu.VMEM)
    if far:
        operands = [pltpu.with_memory_space_constraint(x, pltpu.HBM) for x in operands]
    return pl.pallas_call(
        kernel,
        out_shape=outs,
        in_specs=[pl.BlockSpec(memory_space=pltpu.HBM) if far else spec] * len(operands),
        out_specs=jax.tree.map(lambda _: spec, outs),
        scratch_shapes=scratch,
        compiler_params=pltpu.CompilerParams(vmem_limit_bytes=limit << 20),
    )(*operands)


def near(x):
    return pltpu.with_memory_space_constraint(x, pltpu.VMEM)


def by_columns(volume, kernel_one, bias_one, kernel_two, bias_two, kernel_three, bias_three):
    slabs, halves = lax.axis_size("slab"), lax.axis_size("filt")
    peers = LAYER * halves
    groups = [[peers * g + i for i in range(peers)] for g in range(slabs // LAYER)]
    exchange = functools.partial(
        lax.all_to_all,
        axis_name=("slab", "filt"),
        split_axis=0,
        concat_axis=0,
        axis_index_groups=groups,
        tiled=True,
    )
    b1, b2, b3 = bias_one[None, :], bias_two[None, :], bias_three[None, :]
    blocks = call(
        pack_kernel,
        pltpu.VMEM((peers, 2 * RUN, 256), BF),
        volume.reshape(256, 256),
        scratch=[pltpu.VMEM((256, 256), BF), pltpu.SemaphoreType.DMA],
        far=True,
    )
    mid = exchange(blocks)
    sent = call(
        send_kernel,
        pltpu.VMEM((1312, 128), BF),
        kernel_two,
        kernel_three,
        b2,
        b3,
        scratch=[
            pltpu.VMEM((27, 32, 64), BF),
            pltpu.VMEM((27, 32, 128), BF),
            pltpu.VMEM((1, 64), BF),
            pltpu.VMEM((1, 64), BF),
            pltpu.SemaphoreType.DMA((4,)),
        ],
        far=True,
    )
    over = lax.ppermute(sent, "filt", [(0, 1), (1, 0)])
    w1a, w1c, bias1 = call(
        first_kernel,
        (pltpu.VMEM((256, 2304), BF), pltpu.VMEM((128, 1152), BF), pltpu.VMEM((8, 256), F32)),
        kernel_one,
        b1,
    )
    planes = pltpu.VMEM((2 * (LAYER - 1), 2 * RUN, 256), BF)
    to_first, to_second = call(rim_kernel, (planes, planes), near(mid))

    def swaps(start):
        up = [(i, i + LAYER) for i in range(slabs - LAYER) if i // LAYER % 2 == start]
        return up + [(b, a) for a, b in up]

    rim_a = lax.ppermute(to_first, "slab", swaps(0))
    rim_b = lax.ppermute(to_second, "slab", swaps(1))
    beside = lax.ppermute(over, "slab", [(i, i ^ 1) for i in range(slabs)])
    w2a, w2c, w3, bias2, bias3 = call(
        second_kernel,
        (
            pltpu.VMEM((256, 1152), BF),
            pltpu.VMEM((256, 1152), BF),
            pltpu.VMEM((27, 128, 128), BF),
            pltpu.VMEM((8, 128), F32),
            pltpu.VMEM((8, 128), F32),
        ),
        kernel_two,
        kernel_three,
        b2,
        b3,
        near(over),
        near(beside),
    )
    frames = FRAME * (LAYER + 6)
    operands = (rim_a, mid, rim_b, w1a, w1c, w2a, w2c, w3, bias1, bias2, bias3)
    out = call(
        main_kernel,
        pltpu.VMEM((peers, 48, 256), BF),
        *map(near, operands),
        scratch=[
            pltpu.VMEM((2, 4, frames, 256), BF),
            pltpu.VMEM((4, frames, 128), BF),
            pltpu.VMEM((3, FRAME * (LAYER + 4), 256), BF),
            pltpu.VMEM((3, FRAME * (LAYER + 2), 512), BF),
        ],
        limit=24,
    )
    home = exchange(out)
    skip, features = call(unpack_kernel, (shape(256, 256), shape(256, 128)), near(home))
    return skip.reshape(volume.shape), features.reshape(1, 4, 64, 128)


def fits(volume, kernels, slabs, halves):
    return (
        volume == (1, 4, 64, 256)
        and kernels == [(27, 64, 64), (27, 64, 64), (27, 64, 128)]
        and halves == 2
        and slabs % LAYER == 0
    )


def per_device(volume, *rest):
    kernels = [r.shape for r in rest[::2]]
    good = fits(volume.shape, kernels, lax.axis_size("slab"), lax.axis_size("filt"))
    if not good:
        return by_planes(volume, *rest)
    return by_columns(volume, *rest)


def solution(mesh):
    return jax.shard_map(
        per_device,
        mesh=mesh,
        in_specs=(
            P("slab", "filt", None, None),
            P(),
            P(),
            P(None, "filt", None),
            P("filt"),
            P(None, "filt", None),
            P("filt"),
        ),
        out_specs=(P("slab", "filt", None, None), P("slab", None, "filt", None)),
        check_vma=False,
    )
```

```python
import functools

import jax
import jax.numpy as jnp
from jax import lax
from jax.experimental import pallas as pl
from jax.experimental.pallas import tpu as pltpu
from jax.sharding import PartitionSpec as P


BF = jnp.bfloat16
F32 = jnp.float32
NT = (((1,), (1,)), ((), ()))
NN = (((1,), (0,)), ((), ()))

LAYER = 4
RUN = 24
FRAME = RUN
LEAD = 4


def extended(block, sides, width):
    for axis, dim in sides:
        count = lax.axis_size(axis)
        forward = [(i, i + 1) for i in range(count - 1)]
        backward = [(target, source) for source, target in forward]
        low = lax.ppermute(
            lax.slice_in_dim(block, block.shape[dim] - width, None, axis=dim), axis, forward
        )
        high = lax.ppermute(lax.slice_in_dim(block, 0, width, axis=dim), axis, backward)
        block = jnp.concatenate([low, block, high], axis=dim)
    return block


def pad_columns(field):
    return jnp.pad(field, ((0, 0), (0, 0), (0, 0), (1, 1)))


def accumulate(total, padded, kernel):
    planes, rows, _, cols = total.shape
    for kd in range(3):
        for kh in range(3):
            for kw in range(3):
                tap = 9 * kd + 3 * kh + kw
                total = total + jnp.einsum(
                    "oc,dhcw->dhow",
                    kernel[tap],
                    padded[kd : kd + planes, kh : kh + rows, :, kw : kw + cols],
                    preferred_element_type=jnp.float32,
                )
    return total


def finish(total, bias):
    return jnp.maximum(total + bias.astype(jnp.float32)[None, None, :, None], 0.0).astype(
        jnp.bfloat16
    )


def by_planes(volume, kernel_one, bias_one, kernel_two, bias_two, kernel_three, bias_three):
    planes, rows, chans, cols = volume.shape
    rimmed = extended(volume, (("slab", 0), ("filt", 1)), 1)
    start_one = jnp.zeros((planes, rows, kernel_one.shape[1], cols), jnp.float32)
    skip_one = finish(accumulate(start_one, pad_columns(rimmed), kernel_one), bias_one)
    pooled = jnp.max(skip_one.reshape(planes, rows // 2, 2, chans, cols // 2, 2), axis=(2, 5))
    full_rows = lax.all_gather(pooled, "filt", axis=1, tiled=True)
    planed = extended(full_rows, (("slab", 0),), 1)
    padded = jnp.pad(planed, ((0, 0), (1, 1), (0, 0), (1, 1)))
    height = full_rows.shape[1]
    width = full_rows.shape[3]
    start_two = jnp.zeros((planes, height, kernel_two.shape[1], width), jnp.float32)
    hidden = finish(accumulate(start_two, padded, kernel_two), bias_two)
    hidden_planes = extended(hidden, (("slab", 0),), 1)
    start_three = jnp.zeros((planes, height, kernel_three.shape[1], width), jnp.float32)
    piece_padded = jnp.pad(
        lax.all_gather(hidden_planes, "filt", axis=2, tiled=True), ((0, 0), (1, 1), (0, 0), (1, 1))
    )
    summed = accumulate(start_three, piece_padded, kernel_three)
    features_two = finish(summed, bias_three)
    return (skip_one, features_two)


def dot(a, b, dims):
    return lax.dot_general(a, b, dims, preferred_element_type=F32)


def pack_kernel(far, blocks, volume, sem):
    copy = pltpu.make_async_copy(far, volume, sem)
    copy.start()
    count, width = blocks.shape[0], volume.shape[1]
    shape = (count * 2 * RUN, width)
    row = lax.broadcasted_iota(jnp.int32, shape, 0)
    col = lax.broadcasted_iota(jnp.int32, shape, 1)
    peer, rest = row // (2 * RUN), row % (2 * RUN)
    wanted = (width // count) * peer + 2 * (rest % RUN - LEAD) + rest // RUN
    chosen = jnp.where(wanted == col, 1.0, 0.0).astype(BF)
    copy.wait()
    blocks[...] = dot(chosen, volume[...], NT).astype(BF).reshape(blocks.shape)


def aligned(at, by):
    return pl.multiple_of(at, by)


def send_kernel(far2, far3, far_b2, far_b3, sent, k2, k3, b2, b3, sems):
    top = aligned(32 * (lax.axis_index("slab") % 2), 32)
    half = pl.ds(top, 32)
    copies = [
        pltpu.make_async_copy(far, near, sems.at[i])
        for i, (far, near) in enumerate(
            ((far_b2, b2), (far_b3, b3), (far2.at[:, half, :], k2), (far3.at[:, half, :], k3))
        )
    ]
    for copy in copies:
        copy.start()
    for copy in copies:
        copy.wait()
    for t in range(27):
        sent[16 * t : 16 * t + 16, :] = jnp.concatenate([k2[t, :16, :], k2[t, 16:, :]], axis=1)
        sent[432 + 32 * t : 464 + 32 * t, :] = k3[t]
    both = jnp.concatenate([b2[...], b3[...]], axis=1)
    sent[1296:1312, :] = jnp.broadcast_to(both, (16, 128))


def banded(k_ref):
    def pieces(dp, dw):
        k0, k1, k2 = (k_ref(9 * dp + 3 * dr + dw) for dr in range(3))
        none = jnp.zeros_like(k0)
        join = lambda a, b: jnp.concatenate([a, b], axis=1)
        return join(k1, k2), join(k0, k1), join(k2, none), join(none, k0)

    return pieces


def rim_kernel(mid, to_first, to_second):
    odd = lax.axis_index("slab") // LAYER % 2
    n = to_first.shape[0]
    to_first[...] = mid[pl.ds(2 - 2 * odd, n)]
    to_second[...] = mid[pl.ds(2 * odd, n)]


def first_kernel(k1, k2, b1, w1a, w1c, v2a, v2c, bias):
    one = banded(lambda t: k1[t])
    two = banded(lambda t: k2[t])
    zero = jnp.zeros((64, 128), BF)
    for dp in range(3):
        for dw in range(3):
            t = 3 * dp + dw
            a, b, c, d = one(dp, dw)
            for i, (low, high) in enumerate(((a, zero), (b, c), (d, a), (zero, b))):
                w1a[64 * i : 64 * i + 64, 256 * t : 256 * t + 128] = low
                w1a[64 * i : 64 * i + 64, 256 * t + 128 : 256 * t + 256] = high
            lanes = slice(128 * t, 128 * t + 128)
            w1c[0:64, lanes] = d
            w1c[64:128, lanes] = c
            a, b, c, d = two(dp, dw)
            v2a[0:64, lanes] = a
            v2a[64:128, lanes] = b
            v2c[0:64, lanes] = c
            v2c[64:128, lanes] = d
    bias[...] = jnp.broadcast_to(jnp.concatenate([b1[...].astype(F32)] * 4, axis=1), bias.shape)


def shifted(x, by):
    return pltpu.roll(x, (-by) % x.shape[0], 0)


TAPS = [(dp, dw) for dp in range(3) for dw in range(3)]


def inside(first, planes):
    half, slab = lax.axis_index("filt"), lax.axis_index("slab")
    layer, layers = slab // LAYER, lax.axis_size("slab") // LAYER
    group = slab % LAYER * lax.axis_size("filt") + half
    row = lax.broadcasted_iota(jnp.int32, (planes * FRAME, 1), 0)
    col = 16 * group - LEAD + row % FRAME
    plane = LAYER * layer + first + row // FRAME
    return (plane >= 0) & (plane < LAYER * layers) & (col >= 0) & (col < 128)


def pair(parts, weights):
    n = parts[0].shape[0]
    all_rows = dot(jnp.concatenate(parts, axis=0), weights, NT)
    return [all_rows[n * i : n * i + n] for i in range(len(parts))]


def lanes_of(ref, n, lo, hi):
    return [ref[dw, FRAME * dp : FRAME * dp + n, lo:hi] for dp, dw in TAPS]


def spread_runs(run, planes, q, x34):
    left = lax.broadcasted_iota(jnp.int32, (1, 128), 1) < 64
    for f in range(2):
        for par in range(2):
            rows = slice(RUN * par, RUN * par + RUN)
            whole = jnp.concatenate([run(v, f, rows).astype(F32) for v in planes], axis=0)
            q[f, 1 + par] = whole.astype(BF)
            if par == 0:
                q[f, 3] = shifted(whole, 1).astype(BF)
            else:
                q[f, 0] = shifted(whole, -1).astype(BF)
    for a in range(4):
        x34[a] = jnp.where(left, q[1, a, :, 0:128], q[0, a, :, 128:256])


def products(q, x34, w1a, w1c, step):
    left = lax.broadcasted_iota(jnp.int32, (1, 128), 1) < 64
    n = LAYER * FRAME
    out = []
    for dp in range(3):
        rows = slice(FRAME * step * dp, FRAME * step * dp + n)

        def pick(ref, par):
            return jnp.concatenate([ref[par + dw, rows, :] for dw in range(3)], axis=1)

        cross = pair([pick(x34, par) for par in range(2)], w1c[:, 384 * dp : 384 * dp + 384])
        sums = []
        for f in range(2):
            ys = pair([pick(q.at[f], par) for par in range(2)], w1a[:, 768 * dp : 768 * dp + 768])
            for par in range(2):
                low, high = ys[par][:, :128], ys[par][:, 128:]
                if f == 0:
                    high = high + jnp.where(left, 0.0, cross[par])
                else:
                    low = low + jnp.where(left, cross[par], 0.0)
                ys[par] = jnp.concatenate([low, high], axis=1)
            sums.append(ys)
        out.append(sums)
    return out


def frame(x, i):
    return x[FRAME * i : FRAME * i + FRAME]


def add(terms):
    return functools.reduce(jnp.add, terms)


def inner_kernel(mid, w1a, w1c, acc, q, x34):
    spread_runs(lambda v, f, rows: mid[2 * v + f, rows, :], range(LAYER), q, x34)
    sums = products(q, x34, w1a, w1c, 0)
    for f in range(2):
        for par in range(2):
            for e in range(LAYER + 2):
                terms = [
                    frame(sums[dp][f][par], e - 2 + dp)
                    for dp in range(3)
                    if 0 <= e - 2 + dp < LAYER
                ]
                acc[f, par, FRAME * e : FRAME * e + FRAME, :] = add(terms)


def one_kernel(rim_a, rim_b, w1a, w1c, b1, acc, skips, pd, q, x34):
    odd = lax.axis_index("slab") // LAYER % 2 == 1
    left = lax.broadcasted_iota(jnp.int32, (1, 128), 1) < 64

    def run(v, f, rows):
        at = 2 * (v % 3) + f
        return jnp.where(odd == (v < 3), rim_a[at, rows, :], rim_b[at, rows, :])

    spread_runs(run, range(6), q, x34)
    sums = products(q, x34, w1a, w1c, 1)
    u = LAYER + 4
    targets = ((0, 1, 2, u - 1), (0, 1, u - 2, u - 1), (0, u - 3, u - 2, u - 1))
    bias = b1[0:1, :]
    within = inside(-2, u)
    tiles = []
    for f in range(2):
        ys = []
        for par in range(2):
            planes = []
            for plane in range(u):
                terms = [
                    frame(sums[dp][f][par], targets[dp].index(plane))
                    for dp in range(3)
                    if plane in targets[dp]
                ]
                if 1 <= plane <= u - 2:
                    terms.append(acc[f, par, FRAME * (plane - 1) : FRAME * plane, :])
                planes.append(add(terms))
            for s in range(LAYER):
                kept = planes[2 + s][LEAD : LEAD + 16, :]
                kept = jnp.maximum(kept + bias, 0.0).astype(BF)
                skips[2 * s + f, 16 * par : 16 * par + 16, :] = kept
            ys.append(jnp.concatenate(planes, axis=0))
        y = jnp.maximum(ys[0], ys[1])
        y0, y1 = y[:, :128], y[:, 128:]
        y0 = jnp.maximum(y0, pltpu.roll(y0, 64, 1))
        y1 = jnp.maximum(y1, pltpu.roll(y1, 64, 1))
        y = jnp.maximum(jnp.where(left, y0, y1) + bias[:, :128], 0.0)
        tiles.append(jnp.where(within, y, 0.0))
    pooled = jnp.concatenate(tiles, axis=1)
    for dw in range(3):
        pd[dw] = shifted(pooled, dw - 1).astype(BF)


def two_kernel(pd, v2a, v2c, k3, over, beside, b2, b3, skips, out, w2a, w2c, hd):
    half, core = lax.axis_index("filt"), lax.axis_index("slab") % 2
    lane = lax.broadcasted_iota(jnp.int32, (1, 128), 1)
    left = lane < 64
    out[:, 0:32, :] = skips[...]

    mine, other = half * 64, 64 - half * 64
    for row in range(2):
        w2a[pl.ds(aligned(128 * row + mine, 64), 64), :] = v2a[64 * row : 64 * row + 64, :]
        w2c[pl.ds(aligned(128 * row + mine, 64), 64), :] = v2c[64 * row : 64 * row + 64, :]

    def piece(ref):
        def rows(t):
            both = ref[16 * t : 16 * t + 16, :]
            return jnp.concatenate([both[:, :64], both[:, 64:]], axis=0)

        return banded(rows)

    for rows, at in ((piece(over), other + 32 * core), (piece(beside), other + 32 - 32 * core)):
        for dp, dw in TAPS:
            lanes = slice(128 * (3 * dp + dw), 128 * (3 * dp + dw) + 128)
            a, b, c, d = rows(dp, dw)
            w2a[pl.ds(aligned(at, 32), 32), lanes] = a
            w2a[pl.ds(aligned(128 + at, 32), 32), lanes] = b
            w2c[pl.ds(aligned(at, 32), 32), lanes] = c
            w2c[pl.ds(aligned(128 + at, 32), 32), lanes] = d
    theirs = over[1296:1297, :].astype(F32)
    here2, here3 = b2[...].astype(F32), b3[...].astype(F32)
    there2, there3 = theirs[:, :64], theirs[:, 64:]
    low = jnp.where(half == 0, here2, there2)
    high = jnp.where(half == 0, there2, here2)
    bias2 = jnp.concatenate([low, high], axis=1)
    turned = jnp.concatenate([there3[:, 32:], there3[:, :32]], axis=1)
    bias3 = jnp.concatenate([here3, jnp.where(core == 1, turned, there3)], axis=1)

    m = (LAYER + 2) * FRAME
    pairs = pair(
        [jnp.concatenate(lanes_of(pd, m, 128 * a, 128 * a + 128), axis=1) for a in range(2)],
        w2a[...],
    )
    parts = [jnp.where(left, b, a) for a, b in zip(lanes_of(pd, m, 0, 128), lanes_of(pd, m, 128, 256))]
    mixed = dot(jnp.concatenate(parts, axis=1), w2c[...], NT)
    hidden = jnp.concatenate(
        [
            pairs[0][:, :128],
            pairs[0][:, 128:] + mixed[:, :128],
            pairs[1][:, :128] + mixed[:, 128:],
            pairs[1][:, 128:],
        ],
        axis=1,
    )
    bias = jnp.concatenate([bias2] * 4, axis=1)
    hidden = jnp.where(inside(-1, LAYER + 2), jnp.maximum(hidden + bias, 0.0), 0.0).astype(BF).astype(F32)
    for dw in range(3):
        hd[dw] = shifted(hidden, dw - 1).astype(BF)

    m = LAYER * FRAME

    def third(t):
        rows = slice(432 + 32 * t, 464 + 32 * t)
        return jnp.concatenate([k3[t], over[rows, :], beside[rows, :]], axis=0)

    none = jnp.zeros((128, 128), BF)
    straight, across = [[], []], [[], []]
    for dp, dw in TAPS:
        k0, k1, k2 = (third(9 * dp + 3 * dr + dw) for dr in range(3))
        straight[0] += [k1, k2]
        straight[1] += [k0, k1]
        across[0] += [none, k2]
        across[1] += [k0, none]
    w3a = jnp.concatenate([jnp.concatenate(rows, axis=1) for rows in straight], axis=0)
    w3c = jnp.concatenate([jnp.concatenate(rows, axis=1) for rows in across], axis=0)
    both = jnp.concatenate(
        [jnp.concatenate(lanes_of(hd, m, 256 * a, 256 * a + 256), axis=1) for a in range(2)], axis=0
    )
    both = dot(both, w3a, NT)
    mixed = dot(jnp.concatenate(lanes_of(hd, m, 128, 384), axis=1), w3c, NT)
    t0, t1 = both[:m, :128], both[:m, 128:] + mixed[:, :128]
    t2, t3 = both[m:, :128] + mixed[:, 128:], both[m:, 128:]
    t0, t1, t2, t3 = (jnp.maximum(t + bias3, 0.0) for t in (t0, t1, t2, t3))
    r0, r1, r2, r3 = (pltpu.roll(t, 64, 1) for t in (t0, t1, t2, t3))
    first = jnp.concatenate([jnp.where(left, t0, r1), jnp.where(left, t2, r3)], axis=1)
    second = jnp.concatenate([jnp.where(left, r0, t1), jnp.where(left, r2, t3)], axis=1)
    lane = lax.broadcasted_iota(jnp.int32, (1, 256), 1)
    swapped = jnp.where(lane % 64 < 32, pltpu.roll(second, 224, 1), pltpu.roll(second, 32, 1))
    second = jnp.where(core == 1, swapped, second)
    for s in range(LAYER):
        top = FRAME * s + LEAD
        out[2 * s + half, 32:48, :] = first[top : top + 16, :].astype(BF)
        out[2 * s + 1 - half, 32:48, :] = second[top : top + 16, :].astype(BF)


def unpack_kernel(got, skip, features):
    count = got.shape[0]
    ones = got[:, 0:32, :].reshape(count * 32, 256)
    twos = got[:, 32:48, :].reshape(count * 16, 256)
    row = lax.broadcasted_iota(jnp.int32, (256, 256), 0)
    col = lax.broadcasted_iota(jnp.int32, (256, 256), 1)
    source = 32 * (row // 32) + 16 * (row % 2) + row % 32 // 2
    order = jnp.where(source == col, 1.0, 0.0).astype(BF)
    same = jnp.where(row == col, 1.0, 0.0).astype(BF)
    by_column = dot(order, ones, NN).astype(BF)
    skip[...] = dot(same, by_column, NT).astype(BF)
    features[...] = dot(same, twos, NT).astype(BF)


def shape(*dims):
    return jax.ShapeDtypeStruct(dims, BF)


def call(kernel, outs, *operands, scratch=(), limit=8, far=False):
    spec = pl.BlockSpec(memory_space=pltpu.VMEM)
    if far:
        operands = [pltpu.with_memory_space_constraint(x, pltpu.HBM) for x in operands]
    return pl.pallas_call(
        kernel,
        out_shape=outs,
        in_specs=[pl.BlockSpec(memory_space=pltpu.HBM) if far else spec] * len(operands),
        out_specs=jax.tree.map(lambda _: spec, outs),
        scratch_shapes=scratch,
        compiler_params=pltpu.CompilerParams(vmem_limit_bytes=limit << 20),
    )(*operands)


def near(x):
    return pltpu.with_memory_space_constraint(x, pltpu.VMEM)


def by_columns(volume, kernel_one, bias_one, kernel_two, bias_two, kernel_three, bias_three):
    slabs, halves = lax.axis_size("slab"), lax.axis_size("filt")
    peers = LAYER * halves
    groups = [[peers * g + i for i in range(peers)] for g in range(slabs // LAYER)]
    exchange = functools.partial(
        lax.all_to_all,
        axis_name=("slab", "filt"),
        split_axis=0,
        concat_axis=0,
        axis_index_groups=groups,
        tiled=True,
    )
    b1, b2, b3 = bias_one[None, :], bias_two[None, :], bias_three[None, :]
    blocks = call(
        pack_kernel,
        pltpu.VMEM((peers, 2 * RUN, 256), BF),
        volume.reshape(256, 256),
        scratch=[pltpu.VMEM((256, 256), BF), pltpu.SemaphoreType.DMA],
        far=True,
    )
    mid = exchange(blocks)
    sent = call(
        send_kernel,
        pltpu.VMEM((1312, 128), BF),
        kernel_two,
        kernel_three,
        b2,
        b3,
        scratch=[
            pltpu.VMEM((27, 32, 64), BF),
            pltpu.VMEM((27, 32, 128), BF),
            pltpu.VMEM((1, 64), BF),
            pltpu.VMEM((1, 64), BF),
            pltpu.SemaphoreType.DMA((4,)),
        ],
        far=True,
    )
    over = lax.ppermute(sent, "filt", [(0, 1), (1, 0)])
    w1a, w1c, v2a, v2c, bias1 = call(
        first_kernel,
        (
            pltpu.VMEM((256, 2304), BF),
            pltpu.VMEM((128, 1152), BF),
            pltpu.VMEM((128, 1152), BF),
            pltpu.VMEM((128, 1152), BF),
            pltpu.VMEM((8, 256), F32),
        ),
        kernel_one,
        kernel_two,
        b1,
    )
    planes = pltpu.VMEM((2 * (LAYER - 1), 2 * RUN, 256), BF)
    to_first, to_second = call(rim_kernel, (planes, planes), near(mid))

    def swaps(start):
        up = [(i, i + LAYER) for i in range(slabs - LAYER) if i // LAYER % 2 == start]
        return up + [(b, a) for a, b in up]

    rim_a = lax.ppermute(to_first, "slab", swaps(0))
    rim_b = lax.ppermute(to_second, "slab", swaps(1))
    beside = lax.ppermute(over, "slab", [(i, i ^ 1) for i in range(slabs)])

    def space(planes):
        rows = FRAME * planes
        return [pltpu.VMEM((2, 4, rows, 256), BF), pltpu.VMEM((4, rows, 128), BF)]

    acc = call(
        inner_kernel,
        pltpu.VMEM((2, 2, FRAME * (LAYER + 2), 256), F32),
        *map(near, (mid, w1a, w1c)),
        scratch=space(LAYER),
        limit=24,
    )
    skips, pooled = call(
        one_kernel,
        (pltpu.VMEM((peers, 32, 256), BF), pltpu.VMEM((3, FRAME * (LAYER + 4), 256), BF)),
        *map(near, (rim_a, rim_b, w1a, w1c, bias1, acc)),
        scratch=space(6),
        limit=24,
    )
    out = call(
        two_kernel,
        pltpu.VMEM((peers, 48, 256), BF),
        *map(near, (pooled, v2a, v2c, kernel_three, over, beside, b2, b3, skips)),
        scratch=[
            pltpu.VMEM((256, 1152), BF),
            pltpu.VMEM((256, 1152), BF),
            pltpu.VMEM((3, FRAME * (LAYER + 2), 512), BF),
        ],
        limit=24,
    )
    home = exchange(out)
    skip, features = call(unpack_kernel, (shape(256, 256), shape(256, 128)), near(home))
    return skip.reshape(volume.shape), features.reshape(1, 4, 64, 128)


def fits(volume, kernels, slabs, halves):
    return (
        volume == (1, 4, 64, 256)
        and kernels == [(27, 64, 64), (27, 64, 64), (27, 64, 128)]
        and halves == 2
        and slabs % LAYER == 0
    )


def per_device(volume, *rest):
    kernels = [r.shape for r in rest[::2]]
    good = fits(volume.shape, kernels, lax.axis_size("slab"), lax.axis_size("filt"))
    if not good:
        return by_planes(volume, *rest)
    return by_columns(volume, *rest)


def solution(mesh):
    return jax.shard_map(
        per_device,
        mesh=mesh,
        in_specs=(
            P("slab", "filt", None, None),
            P(),
            P(),
            P(None, "filt", None),
            P("filt"),
            P(None, "filt", None),
            P("filt"),
        ),
        out_specs=(P("slab", "filt", None, None), P("slab", None, "filt", None)),
        check_vma=False,
    )
```

```python
import functools

import jax
import jax.numpy as jnp
from jax import lax
from jax.experimental import pallas as pl
from jax.experimental.pallas import tpu as pltpu
from jax.sharding import PartitionSpec as P


BF = jnp.bfloat16
F32 = jnp.float32
NT = (((1,), (1,)), ((), ()))
NN = (((1,), (0,)), ((), ()))

LAYER = 4
RUN = 24
FRAME = RUN
LEAD = 4


def extended(block, sides, width):
    for axis, dim in sides:
        count = lax.axis_size(axis)
        forward = [(i, i + 1) for i in range(count - 1)]
        backward = [(target, source) for source, target in forward]
        low = lax.ppermute(
            lax.slice_in_dim(block, block.shape[dim] - width, None, axis=dim), axis, forward
        )
        high = lax.ppermute(lax.slice_in_dim(block, 0, width, axis=dim), axis, backward)
        block = jnp.concatenate([low, block, high], axis=dim)
    return block


def pad_columns(field):
    return jnp.pad(field, ((0, 0), (0, 0), (0, 0), (1, 1)))


def accumulate(total, padded, kernel):
    planes, rows, _, cols = total.shape
    for kd in range(3):
        for kh in range(3):
            for kw in range(3):
                tap = 9 * kd + 3 * kh + kw
                total = total + jnp.einsum(
                    "oc,dhcw->dhow",
                    kernel[tap],
                    padded[kd : kd + planes, kh : kh + rows, :, kw : kw + cols],
                    preferred_element_type=jnp.float32,
                )
    return total


def finish(total, bias):
    return jnp.maximum(total + bias.astype(jnp.float32)[None, None, :, None], 0.0).astype(
        jnp.bfloat16
    )


def by_planes(volume, kernel_one, bias_one, kernel_two, bias_two, kernel_three, bias_three):
    planes, rows, chans, cols = volume.shape
    rimmed = extended(volume, (("slab", 0), ("filt", 1)), 1)
    start_one = jnp.zeros((planes, rows, kernel_one.shape[1], cols), jnp.float32)
    skip_one = finish(accumulate(start_one, pad_columns(rimmed), kernel_one), bias_one)
    pooled = jnp.max(skip_one.reshape(planes, rows // 2, 2, chans, cols // 2, 2), axis=(2, 5))
    full_rows = lax.all_gather(pooled, "filt", axis=1, tiled=True)
    planed = extended(full_rows, (("slab", 0),), 1)
    padded = jnp.pad(planed, ((0, 0), (1, 1), (0, 0), (1, 1)))
    height = full_rows.shape[1]
    width = full_rows.shape[3]
    start_two = jnp.zeros((planes, height, kernel_two.shape[1], width), jnp.float32)
    hidden = finish(accumulate(start_two, padded, kernel_two), bias_two)
    hidden_planes = extended(hidden, (("slab", 0),), 1)
    start_three = jnp.zeros((planes, height, kernel_three.shape[1], width), jnp.float32)
    piece_padded = jnp.pad(
        lax.all_gather(hidden_planes, "filt", axis=2, tiled=True), ((0, 0), (1, 1), (0, 0), (1, 1))
    )
    summed = accumulate(start_three, piece_padded, kernel_three)
    features_two = finish(summed, bias_three)
    return (skip_one, features_two)


def dot(a, b, dims):
    return lax.dot_general(a, b, dims, preferred_element_type=F32)


def pack_kernel(far, far2, far3, far_b2, far_b3, blocks, k2, k3, b2, b3, volume, sems):
    half = pl.ds(aligned(32 * (lax.axis_index("slab") % 2), 32), 32)
    pairs = (
        (far, volume),
        (far2.at[:, half, :], k2),
        (far3.at[:, half, :], k3),
        (far_b2, b2),
        (far_b3, b3),
    )
    copies = [pltpu.make_async_copy(*ends, sems.at[i]) for i, ends in enumerate(pairs)]
    for copy in copies:
        copy.start()
    count, width = blocks.shape[0], volume.shape[1]
    shape = (count * 2 * RUN, width)
    row = lax.broadcasted_iota(jnp.int32, shape, 0)
    col = lax.broadcasted_iota(jnp.int32, shape, 1)
    peer, rest = row // (2 * RUN), row % (2 * RUN)
    wanted = (width // count) * peer + 2 * (rest % RUN - LEAD) + rest // RUN
    chosen = jnp.where(wanted == col, 1.0, 0.0).astype(BF)
    copies[0].wait()
    blocks[...] = dot(chosen, volume[...], NT).astype(BF).reshape(blocks.shape)
    for copy in copies[1:]:
        copy.wait()


def aligned(at, by):
    return pl.multiple_of(at, by)


def send_kernel(k2, k3, b2, b3, sent):
    for t in range(27):
        sent[16 * t : 16 * t + 16, :] = jnp.concatenate([k2[t, :16, :], k2[t, 16:, :]], axis=1)
        sent[432 + 32 * t : 464 + 32 * t, :] = k3[t]
    both = jnp.concatenate([b2[...], b3[...]], axis=1)
    sent[1296:1312, :] = jnp.broadcast_to(both, (16, 128))


def banded(k_ref):
    def pieces(dp, dw):
        k0, k1, k2 = (k_ref(9 * dp + 3 * dr + dw) for dr in range(3))
        none = jnp.zeros_like(k0)
        join = lambda a, b: jnp.concatenate([a, b], axis=1)
        return join(k1, k2), join(k0, k1), join(k2, none), join(none, k0)

    return pieces


def rim_kernel(mid, to_first, to_second):
    odd = lax.axis_index("slab") // LAYER % 2
    n = to_first.shape[0]
    to_first[...] = mid[pl.ds(2 - 2 * odd, n)]
    to_second[...] = mid[pl.ds(2 * odd, n)]


def first_kernel(k1, k2, b1, w1a, w1c, v2a, v2c, bias):
    one = banded(lambda t: k1[t])
    two = banded(lambda t: k2[t])
    zero = jnp.zeros((64, 128), BF)
    for dp in range(3):
        for dw in range(3):
            t = 3 * dp + dw
            a, b, c, d = one(dp, dw)
            for i, (low, high) in enumerate(((a, zero), (b, c), (d, a), (zero, b))):
                w1a[64 * i : 64 * i + 64, 256 * t : 256 * t + 128] = low
                w1a[64 * i : 64 * i + 64, 256 * t + 128 : 256 * t + 256] = high
            lanes = slice(128 * t, 128 * t + 128)
            w1c[0:64, lanes] = d
            w1c[64:128, lanes] = c
            a, b, c, d = two(dp, dw)
            v2a[0:64, lanes] = a
            v2a[64:128, lanes] = b
            v2c[0:64, lanes] = c
            v2c[64:128, lanes] = d
    bias[...] = jnp.broadcast_to(jnp.concatenate([b1[...].astype(F32)] * 4, axis=1), bias.shape)


def shifted(x, by):
    return pltpu.roll(x, (-by) % x.shape[0], 0)


TAPS = [(dp, dw) for dp in range(3) for dw in range(3)]


def inside(first, planes):
    half, slab = lax.axis_index("filt"), lax.axis_index("slab")
    layer, layers = slab // LAYER, lax.axis_size("slab") // LAYER
    group = slab % LAYER * lax.axis_size("filt") + half
    row = lax.broadcasted_iota(jnp.int32, (planes * FRAME, 1), 0)
    col = 16 * group - LEAD + row % FRAME
    plane = LAYER * layer + first + row // FRAME
    return (plane >= 0) & (plane < LAYER * layers) & (col >= 0) & (col < 128)


def pair(parts, weights):
    n = parts[0].shape[0]
    all_rows = dot(jnp.concatenate(parts, axis=0), weights, NT)
    return [all_rows[n * i : n * i + n] for i in range(len(parts))]


def lanes_of(ref, n, lo, hi):
    return [ref[dw, FRAME * dp : FRAME * dp + n, lo:hi] for dp, dw in TAPS]


def spread_runs(run, planes, q, x34):
    left = lax.broadcasted_iota(jnp.int32, (1, 128), 1) < 64
    for f in range(2):
        for par in range(2):
            rows = slice(RUN * par, RUN * par + RUN)
            whole = jnp.concatenate([run(v, f, rows).astype(F32) for v in planes], axis=0)
            q[f, 1 + par] = whole.astype(BF)
            if par == 0:
                q[f, 3] = shifted(whole, 1).astype(BF)
            else:
                q[f, 0] = shifted(whole, -1).astype(BF)
    for a in range(4):
        x34[a] = jnp.where(left, q[1, a, :, 0:128], q[0, a, :, 128:256])


def products(q, x34, w1a, w1c, step):
    left = lax.broadcasted_iota(jnp.int32, (1, 128), 1) < 64
    n = LAYER * FRAME
    out = []
    for dp in range(3):
        rows = slice(FRAME * step * dp, FRAME * step * dp + n)

        def pick(ref, par):
            return jnp.concatenate([ref[par + dw, rows, :] for dw in range(3)], axis=1)

        cross = pair([pick(x34, par) for par in range(2)], w1c[:, 384 * dp : 384 * dp + 384])
        sums = []
        for f in range(2):
            ys = pair([pick(q.at[f], par) for par in range(2)], w1a[:, 768 * dp : 768 * dp + 768])
            for par in range(2):
                low, high = ys[par][:, :128], ys[par][:, 128:]
                if f == 0:
                    high = high + jnp.where(left, 0.0, cross[par])
                else:
                    low = low + jnp.where(left, cross[par], 0.0)
                ys[par] = jnp.concatenate([low, high], axis=1)
            sums.append(ys)
        out.append(sums)
    return out


def frame(x, i):
    return x[FRAME * i : FRAME * i + FRAME]


def add(terms):
    return functools.reduce(jnp.add, terms)


def inner_kernel(mid, w1a, w1c, acc, q, x34):
    spread_runs(lambda v, f, rows: mid[2 * v + f, rows, :], range(LAYER), q, x34)
    sums = products(q, x34, w1a, w1c, 0)
    for f in range(2):
        for par in range(2):
            for e in range(LAYER + 2):
                terms = [
                    frame(sums[dp][f][par], e - 2 + dp)
                    for dp in range(3)
                    if 0 <= e - 2 + dp < LAYER
                ]
                acc[f, par, FRAME * e : FRAME * e + FRAME, :] = add(terms)


def one_kernel(rim_a, rim_b, w1a, w1c, b1, acc, skips, pd, q, x34):
    layer, layers = lax.axis_index("slab") // LAYER, lax.axis_size("slab") // LAYER
    odd = layer % 2 == 1
    left = lax.broadcasted_iota(jnp.int32, (1, 128), 1) < 64

    def run(v, f, rows):
        at = 2 * (v % 3) + f
        got = jnp.where(odd == (v < 3), rim_a[at, rows, :], rim_b[at, rows, :])
        outside = layer == (0 if v < 3 else layers - 1)
        return jnp.where(outside, jnp.zeros_like(got), got)

    spread_runs(run, range(6), q, x34)
    sums = products(q, x34, w1a, w1c, 1)
    u = LAYER + 4
    targets = ((0, 1, 2, u - 1), (0, 1, u - 2, u - 1), (0, u - 3, u - 2, u - 1))
    bias = b1[0:1, :]
    within = inside(-2, u)
    tiles = []
    for f in range(2):
        ys = []
        for par in range(2):
            planes = []
            for plane in range(u):
                terms = [
                    frame(sums[dp][f][par], targets[dp].index(plane))
                    for dp in range(3)
                    if plane in targets[dp]
                ]
                if 1 <= plane <= u - 2:
                    terms.append(acc[f, par, FRAME * (plane - 1) : FRAME * plane, :])
                planes.append(add(terms))
            for s in range(LAYER):
                kept = planes[2 + s][LEAD : LEAD + 16, :]
                kept = jnp.maximum(kept + bias, 0.0).astype(BF)
                skips[2 * s + f, 16 * par : 16 * par + 16, :] = kept
            ys.append(jnp.concatenate(planes, axis=0))
        y = jnp.maximum(ys[0], ys[1])
        y0, y1 = y[:, :128], y[:, 128:]
        y0 = jnp.maximum(y0, pltpu.roll(y0, 64, 1))
        y1 = jnp.maximum(y1, pltpu.roll(y1, 64, 1))
        y = jnp.maximum(jnp.where(left, y0, y1) + bias[:, :128], 0.0)
        tiles.append(jnp.where(within, y, 0.0))
    pooled = jnp.concatenate(tiles, axis=1)
    for dw in range(3):
        pd[dw] = shifted(pooled, dw - 1).astype(BF)


def two_kernel(pd, v2a, v2c, k3, over, beside, b2, b3, skips, out, w2a, w2c, hd):
    half, core = lax.axis_index("filt"), lax.axis_index("slab") % 2
    lane = lax.broadcasted_iota(jnp.int32, (1, 128), 1)
    left = lane < 64
    out[:, 0:32, :] = skips[...]

    mine, other = half * 64, 64 - half * 64
    for row in range(2):
        w2a[pl.ds(aligned(128 * row + mine, 64), 64), :] = v2a[64 * row : 64 * row + 64, :]
        w2c[pl.ds(aligned(128 * row + mine, 64), 64), :] = v2c[64 * row : 64 * row + 64, :]

    def piece(ref):
        def rows(t):
            both = ref[16 * t : 16 * t + 16, :]
            return jnp.concatenate([both[:, :64], both[:, 64:]], axis=0)

        return banded(rows)

    for rows, at in ((piece(over), other + 32 * core), (piece(beside), other + 32 - 32 * core)):
        for dp, dw in TAPS:
            lanes = slice(128 * (3 * dp + dw), 128 * (3 * dp + dw) + 128)
            a, b, c, d = rows(dp, dw)
            w2a[pl.ds(aligned(at, 32), 32), lanes] = a
            w2a[pl.ds(aligned(128 + at, 32), 32), lanes] = b
            w2c[pl.ds(aligned(at, 32), 32), lanes] = c
            w2c[pl.ds(aligned(128 + at, 32), 32), lanes] = d
    theirs = over[1296:1297, :].astype(F32)
    here2, here3 = b2[...].astype(F32), b3[...].astype(F32)
    there2, there3 = theirs[:, :64], theirs[:, 64:]
    low = jnp.where(half == 0, here2, there2)
    high = jnp.where(half == 0, there2, here2)
    bias2 = jnp.concatenate([low, high], axis=1)
    turned = jnp.concatenate([there3[:, 32:], there3[:, :32]], axis=1)
    bias3 = jnp.concatenate([here3, jnp.where(core == 1, turned, there3)], axis=1)

    m = (LAYER + 2) * FRAME
    pairs = pair(
        [jnp.concatenate(lanes_of(pd, m, 128 * a, 128 * a + 128), axis=1) for a in range(2)],
        w2a[...],
    )
    parts = [jnp.where(left, b, a) for a, b in zip(lanes_of(pd, m, 0, 128), lanes_of(pd, m, 128, 256))]
    mixed = dot(jnp.concatenate(parts, axis=1), w2c[...], NT)
    hidden = jnp.concatenate(
        [
            pairs[0][:, :128],
            pairs[0][:, 128:] + mixed[:, :128],
            pairs[1][:, :128] + mixed[:, 128:],
            pairs[1][:, 128:],
        ],
        axis=1,
    )
    bias = jnp.concatenate([bias2] * 4, axis=1)
    hidden = jnp.where(inside(-1, LAYER + 2), jnp.maximum(hidden + bias, 0.0), 0.0).astype(BF).astype(F32)
    for dw in range(3):
        hd[dw] = shifted(hidden, dw - 1).astype(BF)

    m = LAYER * FRAME

    def third(t):
        rows = slice(432 + 32 * t, 464 + 32 * t)
        return jnp.concatenate([k3[t], over[rows, :], beside[rows, :]], axis=0)

    none = jnp.zeros((128, 128), BF)
    straight, across = [[], []], [[], []]
    for dp, dw in TAPS:
        k0, k1, k2 = (third(9 * dp + 3 * dr + dw) for dr in range(3))
        straight[0] += [k1, k2]
        straight[1] += [k0, k1]
        across[0] += [none, k2]
        across[1] += [k0, none]
    w3a = jnp.concatenate([jnp.concatenate(rows, axis=1) for rows in straight], axis=0)
    w3c = jnp.concatenate([jnp.concatenate(rows, axis=1) for rows in across], axis=0)
    both = jnp.concatenate(
        [jnp.concatenate(lanes_of(hd, m, 256 * a, 256 * a + 256), axis=1) for a in range(2)], axis=0
    )
    both = dot(both, w3a, NT)
    mixed = dot(jnp.concatenate(lanes_of(hd, m, 128, 384), axis=1), w3c, NT)
    t0, t1 = both[:m, :128], both[:m, 128:] + mixed[:, :128]
    t2, t3 = both[m:, :128] + mixed[:, 128:], both[m:, 128:]
    t0, t1, t2, t3 = (jnp.maximum(t + bias3, 0.0) for t in (t0, t1, t2, t3))
    r0, r1, r2, r3 = (pltpu.roll(t, 64, 1) for t in (t0, t1, t2, t3))
    first = jnp.concatenate([jnp.where(left, t0, r1), jnp.where(left, t2, r3)], axis=1)
    second = jnp.concatenate([jnp.where(left, r0, t1), jnp.where(left, r2, t3)], axis=1)
    lane = lax.broadcasted_iota(jnp.int32, (1, 256), 1)
    swapped = jnp.where(lane % 64 < 32, pltpu.roll(second, 224, 1), pltpu.roll(second, 32, 1))
    second = jnp.where(core == 1, swapped, second)
    for s in range(LAYER):
        top = FRAME * s + LEAD
        out[2 * s + half, 32:48, :] = first[top : top + 16, :].astype(BF)
        out[2 * s + 1 - half, 32:48, :] = second[top : top + 16, :].astype(BF)


def unpack_kernel(got, skip, features):
    count = got.shape[0]
    ones = got[:, 0:32, :].reshape(count * 32, 256)
    twos = got[:, 32:48, :].reshape(count * 16, 256)
    row = lax.broadcasted_iota(jnp.int32, (256, 256), 0)
    col = lax.broadcasted_iota(jnp.int32, (256, 256), 1)
    source = 32 * (row // 32) + 16 * (row % 2) + row % 32 // 2
    order = jnp.where(source == col, 1.0, 0.0).astype(BF)
    same = jnp.where(row == col, 1.0, 0.0).astype(BF)
    by_column = dot(order, ones, NN).astype(BF)
    skip[...] = dot(same, by_column, NT).astype(BF)
    features[...] = dot(same, twos, NT).astype(BF)


def shape(*dims):
    return jax.ShapeDtypeStruct(dims, BF)


def call(kernel, outs, *operands, scratch=(), limit=8, far=False):
    spec = pl.BlockSpec(memory_space=pltpu.VMEM)
    if far:
        operands = [pltpu.with_memory_space_constraint(x, pltpu.HBM) for x in operands]
    return pl.pallas_call(
        kernel,
        out_shape=outs,
        in_specs=[pl.BlockSpec(memory_space=pltpu.HBM) if far else spec] * len(operands),
        out_specs=jax.tree.map(lambda _: spec, outs),
        scratch_shapes=scratch,
        compiler_params=pltpu.CompilerParams(vmem_limit_bytes=limit << 20),
    )(*operands)


def near(x):
    return pltpu.with_memory_space_constraint(x, pltpu.VMEM)


def by_columns(volume, kernel_one, bias_one, kernel_two, bias_two, kernel_three, bias_three):
    slabs, halves = lax.axis_size("slab"), lax.axis_size("filt")
    peers = LAYER * halves
    groups = [[peers * g + i for i in range(peers)] for g in range(slabs // LAYER)]
    exchange = functools.partial(
        lax.all_to_all,
        axis_name=("slab", "filt"),
        split_axis=0,
        concat_axis=0,
        axis_index_groups=groups,
        tiled=True,
    )
    b1, b2, b3 = bias_one[None, :], bias_two[None, :], bias_three[None, :]
    blocks, *mine = call(
        pack_kernel,
        (
            pltpu.VMEM((peers, 2 * RUN, 256), BF),
            pltpu.VMEM((27, 32, 64), BF),
            pltpu.VMEM((27, 32, 128), BF),
            pltpu.VMEM((1, 64), BF),
            pltpu.VMEM((1, 64), BF),
        ),
        volume.reshape(256, 256),
        kernel_two,
        kernel_three,
        b2,
        b3,
        scratch=[pltpu.VMEM((256, 256), BF), pltpu.SemaphoreType.DMA((5,))],
        far=True,
    )
    mid = exchange(blocks)
    sent = call(send_kernel, pltpu.VMEM((1312, 128), BF), *map(near, mine))
    over = lax.ppermute(sent, "filt", [(0, 1), (1, 0)])
    w1a, w1c, v2a, v2c, bias1 = call(
        first_kernel,
        (
            pltpu.VMEM((256, 2304), BF),
            pltpu.VMEM((128, 1152), BF),
            pltpu.VMEM((128, 1152), BF),
            pltpu.VMEM((128, 1152), BF),
            pltpu.VMEM((8, 256), F32),
        ),
        kernel_one,
        kernel_two,
        b1,
    )
    planes = pltpu.VMEM((2 * (LAYER - 1), 2 * RUN, 256), BF)
    to_first, to_second = call(rim_kernel, (planes, planes), near(mid))

    def swaps(start):
        up = [(i, i + LAYER) for i in range(slabs - LAYER) if i // LAYER % 2 == start]
        both = dict(up + [(b, a) for a, b in up])
        return [(i, both.get(i, i ^ 1)) for i in range(slabs)]

    rim_a = lax.ppermute(to_first, "slab", swaps(0))
    rim_b = lax.ppermute(to_second, "slab", swaps(1))
    beside = lax.ppermute(over, "slab", [(i, i ^ 1) for i in range(slabs)])

    def space(planes):
        rows = FRAME * planes
        return [pltpu.VMEM((2, 4, rows, 256), BF), pltpu.VMEM((4, rows, 128), BF)]

    acc = call(
        inner_kernel,
        pltpu.VMEM((2, 2, FRAME * (LAYER + 2), 256), F32),
        *map(near, (mid, w1a, w1c)),
        scratch=space(LAYER),
        limit=24,
    )
    skips, pooled = call(
        one_kernel,
        (pltpu.VMEM((peers, 32, 256), BF), pltpu.VMEM((3, FRAME * (LAYER + 4), 256), BF)),
        *map(near, (rim_a, rim_b, w1a, w1c, bias1, acc)),
        scratch=space(6),
        limit=24,
    )
    out = call(
        two_kernel,
        pltpu.VMEM((peers, 48, 256), BF),
        *map(near, (pooled, v2a, v2c, kernel_three, over, beside, b2, b3, skips)),
        scratch=[
            pltpu.VMEM((256, 1152), BF),
            pltpu.VMEM((256, 1152), BF),
            pltpu.VMEM((3, FRAME * (LAYER + 2), 512), BF),
        ],
        limit=24,
    )
    home = exchange(out)
    skip, features = call(unpack_kernel, (shape(256, 256), shape(256, 128)), near(home))
    return skip.reshape(volume.shape), features.reshape(1, 4, 64, 128)


def fits(volume, kernels, slabs, halves):
    return (
        volume == (1, 4, 64, 256)
        and kernels == [(27, 64, 64), (27, 64, 64), (27, 64, 128)]
        and halves == 2
        and slabs % LAYER == 0
    )


def per_device(volume, *rest):
    kernels = [r.shape for r in rest[::2]]
    good = fits(volume.shape, kernels, lax.axis_size("slab"), lax.axis_size("filt"))
    if not good:
        return by_planes(volume, *rest)
    return by_columns(volume, *rest)


def solution(mesh):
    return jax.shard_map(
        per_device,
        mesh=mesh,
        in_specs=(
            P("slab", "filt", None, None),
            P(),
            P(),
            P(None, "filt", None),
            P("filt"),
            P(None, "filt", None),
            P("filt"),
        ),
        out_specs=(P("slab", "filt", None, None), P("slab", None, "filt", None)),
        check_vma=False,
    )
```

```python
import functools

import jax
import jax.numpy as jnp
from jax import lax
from jax.experimental import pallas as pl
from jax.experimental.pallas import tpu as pltpu
from jax.sharding import PartitionSpec as P


BF = jnp.bfloat16
F32 = jnp.float32
NT = (((1,), (1,)), ((), ()))
NN = (((1,), (0,)), ((), ()))

LAYER = 4
RUN = 24
FRAME = RUN
LEAD = 4


def extended(block, sides, width):
    for axis, dim in sides:
        count = lax.axis_size(axis)
        forward = [(i, i + 1) for i in range(count - 1)]
        backward = [(target, source) for source, target in forward]
        low = lax.ppermute(
            lax.slice_in_dim(block, block.shape[dim] - width, None, axis=dim), axis, forward
        )
        high = lax.ppermute(lax.slice_in_dim(block, 0, width, axis=dim), axis, backward)
        block = jnp.concatenate([low, block, high], axis=dim)
    return block


def pad_columns(field):
    return jnp.pad(field, ((0, 0), (0, 0), (0, 0), (1, 1)))


def accumulate(total, padded, kernel):
    planes, rows, _, cols = total.shape
    for kd in range(3):
        for kh in range(3):
            for kw in range(3):
                tap = 9 * kd + 3 * kh + kw
                total = total + jnp.einsum(
                    "oc,dhcw->dhow",
                    kernel[tap],
                    padded[kd : kd + planes, kh : kh + rows, :, kw : kw + cols],
                    preferred_element_type=jnp.float32,
                )
    return total


def finish(total, bias):
    return jnp.maximum(total + bias.astype(jnp.float32)[None, None, :, None], 0.0).astype(
        jnp.bfloat16
    )


def by_planes(volume, kernel_one, bias_one, kernel_two, bias_two, kernel_three, bias_three):
    planes, rows, chans, cols = volume.shape
    rimmed = extended(volume, (("slab", 0), ("filt", 1)), 1)
    start_one = jnp.zeros((planes, rows, kernel_one.shape[1], cols), jnp.float32)
    skip_one = finish(accumulate(start_one, pad_columns(rimmed), kernel_one), bias_one)
    pooled = jnp.max(skip_one.reshape(planes, rows // 2, 2, chans, cols // 2, 2), axis=(2, 5))
    full_rows = lax.all_gather(pooled, "filt", axis=1, tiled=True)
    planed = extended(full_rows, (("slab", 0),), 1)
    padded = jnp.pad(planed, ((0, 0), (1, 1), (0, 0), (1, 1)))
    height = full_rows.shape[1]
    width = full_rows.shape[3]
    start_two = jnp.zeros((planes, height, kernel_two.shape[1], width), jnp.float32)
    hidden = finish(accumulate(start_two, padded, kernel_two), bias_two)
    hidden_planes = extended(hidden, (("slab", 0),), 1)
    start_three = jnp.zeros((planes, height, kernel_three.shape[1], width), jnp.float32)
    piece_padded = jnp.pad(
        lax.all_gather(hidden_planes, "filt", axis=2, tiled=True), ((0, 0), (1, 1), (0, 0), (1, 1))
    )
    summed = accumulate(start_three, piece_padded, kernel_three)
    features_two = finish(summed, bias_three)
    return (skip_one, features_two)


def dot(a, b, dims):
    return lax.dot_general(a, b, dims, preferred_element_type=F32)


def pack_kernel(far, far2, far3, far_b2, far_b3, blocks, k2, k3, b2, b3, volume, sems):
    half = pl.ds(aligned(32 * (lax.axis_index("slab") % 2), 32), 32)
    pairs = (
        (far, volume),
        (far2.at[:, half, :], k2),
        (far3.at[:, half, :], k3),
        (far_b2, b2),
        (far_b3, b3),
    )
    copies = [pltpu.make_async_copy(*ends, sems.at[i]) for i, ends in enumerate(pairs)]
    for copy in copies:
        copy.start()
    count, width = blocks.shape[0], volume.shape[1]
    shape = (count * 2 * RUN, width)
    row = lax.broadcasted_iota(jnp.int32, shape, 0)
    col = lax.broadcasted_iota(jnp.int32, shape, 1)
    peer, rest = row // (2 * RUN), row % (2 * RUN)
    wanted = (width // count) * peer + 2 * (rest % RUN - LEAD) + rest // RUN
    chosen = jnp.where(wanted == col, 1.0, 0.0).astype(BF)
    copies[0].wait()
    blocks[...] = dot(chosen, volume[...], NT).astype(BF).reshape(blocks.shape)
    for copy in copies[1:]:
        copy.wait()


def aligned(at, by):
    return pl.multiple_of(at, by)


def send_kernel(k2, k3, b2, b3, sent2, sent3):
    for t in range(27):
        sent2[16 * t : 16 * t + 16, :] = jnp.concatenate([k2[t, :16, :], k2[t, 16:, :]], axis=1)
        sent3[32 * t : 32 * t + 32, :] = k3[t]
    both = jnp.concatenate([b2[...], b3[...]], axis=1)
    sent2[432:448, :] = jnp.broadcast_to(both, (16, 128))


def banded(k_ref):
    def pieces(dp, dw):
        k0, k1, k2 = (k_ref(9 * dp + 3 * dr + dw) for dr in range(3))
        none = jnp.zeros_like(k0)
        join = lambda a, b: jnp.concatenate([a, b], axis=1)
        return join(k1, k2), join(k0, k1), join(k2, none), join(none, k0)

    return pieces


def rim_kernel(mid, to_first, to_second):
    odd = lax.axis_index("slab") // LAYER % 2
    n = to_first.shape[0]
    to_first[...] = mid[pl.ds(2 - 2 * odd, n)]
    to_second[...] = mid[pl.ds(2 * odd, n)]


def first_kernel(far3, k1, k2, b1, w1a, w1c, v2a, v2c, bias, k3, order, same, sem):
    copy = pltpu.make_async_copy(far3, k3, sem)
    copy.start()
    row = lax.broadcasted_iota(jnp.int32, order.shape, 0)
    col = lax.broadcasted_iota(jnp.int32, order.shape, 1)
    source = 32 * (row // 32) + 16 * (row % 2) + row % 32 // 2
    order[...] = jnp.where(source == col, 1.0, 0.0).astype(BF)
    same[...] = jnp.where(row == col, 1.0, 0.0).astype(BF)
    one = banded(lambda t: k1[t])
    two = banded(lambda t: k2[t])
    zero = jnp.zeros((64, 128), BF)
    for dp in range(3):
        for dw in range(3):
            t = 3 * dp + dw
            a, b, c, d = one(dp, dw)
            for i, (low, high) in enumerate(((a, zero), (b, c), (d, a), (zero, b))):
                w1a[64 * i : 64 * i + 64, 256 * t : 256 * t + 128] = low
                w1a[64 * i : 64 * i + 64, 256 * t + 128 : 256 * t + 256] = high
            lanes = slice(128 * t, 128 * t + 128)
            w1c[0:64, lanes] = d
            w1c[64:128, lanes] = c
            a, b, c, d = two(dp, dw)
            v2a[0:64, lanes] = a
            v2a[64:128, lanes] = b
            v2c[0:64, lanes] = c
            v2c[64:128, lanes] = d
    bias[...] = jnp.broadcast_to(jnp.concatenate([b1[...].astype(F32)] * 4, axis=1), bias.shape)
    copy.wait()


def shifted(x, by):
    return pltpu.roll(x, (-by) % x.shape[0], 0)


TAPS = [(dp, dw) for dp in range(3) for dw in range(3)]


def inside(first, planes):
    half, slab = lax.axis_index("filt"), lax.axis_index("slab")
    layer, layers = slab // LAYER, lax.axis_size("slab") // LAYER
    group = slab % LAYER * lax.axis_size("filt") + half
    row = lax.broadcasted_iota(jnp.int32, (planes * FRAME, 1), 0)
    col = 16 * group - LEAD + row % FRAME
    plane = LAYER * layer + first + row // FRAME
    return (plane >= 0) & (plane < LAYER * layers) & (col >= 0) & (col < 128)


def pair(parts, weights):
    n = parts[0].shape[0]
    all_rows = dot(jnp.concatenate(parts, axis=0), weights, NT)
    return [all_rows[n * i : n * i + n] for i in range(len(parts))]


def lanes_of(ref, n, lo, hi):
    return [ref[dw, FRAME * dp : FRAME * dp + n, lo:hi] for dp, dw in TAPS]


def spread_runs(run, planes, q, x34):
    left = lax.broadcasted_iota(jnp.int32, (1, 128), 1) < 64
    for f in range(2):
        for par in range(2):
            rows = slice(RUN * par, RUN * par + RUN)
            whole = jnp.concatenate([run(v, f, rows).astype(F32) for v in planes], axis=0)
            q[f, 1 + par] = whole.astype(BF)
            if par == 0:
                q[f, 3] = shifted(whole, 1).astype(BF)
            else:
                q[f, 0] = shifted(whole, -1).astype(BF)
    for a in range(4):
        x34[a] = jnp.where(left, q[1, a, :, 0:128], q[0, a, :, 128:256])


def products(q, x34, w1a, w1c, step):
    left = lax.broadcasted_iota(jnp.int32, (1, 128), 1) < 64
    n = LAYER * FRAME
    out = []
    for dp in range(3):
        rows = slice(FRAME * step * dp, FRAME * step * dp + n)

        def pick(ref, par):
            return jnp.concatenate([ref[par + dw, rows, :] for dw in range(3)], axis=1)

        cross = pair([pick(x34, par) for par in range(2)], w1c[:, 384 * dp : 384 * dp + 384])
        sums = []
        for f in range(2):
            ys = pair([pick(q.at[f], par) for par in range(2)], w1a[:, 768 * dp : 768 * dp + 768])
            for par in range(2):
                low, high = ys[par][:, :128], ys[par][:, 128:]
                if f == 0:
                    high = high + jnp.where(left, 0.0, cross[par])
                else:
                    low = low + jnp.where(left, cross[par], 0.0)
                ys[par] = jnp.concatenate([low, high], axis=1)
            sums.append(ys)
        out.append(sums)
    return out


def frame(x, i):
    return x[FRAME * i : FRAME * i + FRAME]


def add(terms):
    return functools.reduce(jnp.add, terms)


def inner_kernel(mid, w1a, w1c, acc, q, x34):
    spread_runs(lambda v, f, rows: mid[2 * v + f, rows, :], range(LAYER), q, x34)
    sums = products(q, x34, w1a, w1c, 0)
    for f in range(2):
        for par in range(2):
            for e in range(LAYER + 2):
                terms = [
                    frame(sums[dp][f][par], e - 2 + dp)
                    for dp in range(3)
                    if 0 <= e - 2 + dp < LAYER
                ]
                acc[f, par, FRAME * e : FRAME * e + FRAME, :] = add(terms)


def one_kernel(rim_a, rim_b, w1a, w1c, b1, acc, skips, pd, q, x34):
    layer, layers = lax.axis_index("slab") // LAYER, lax.axis_size("slab") // LAYER
    odd = layer % 2 == 1
    left = lax.broadcasted_iota(jnp.int32, (1, 128), 1) < 64

    def run(v, f, rows):
        at = 2 * (v % 3) + f
        got = jnp.where(odd == (v < 3), rim_a[at, rows, :], rim_b[at, rows, :])
        outside = layer == (0 if v < 3 else layers - 1)
        return jnp.where(outside, jnp.zeros_like(got), got)

    spread_runs(run, range(6), q, x34)
    sums = products(q, x34, w1a, w1c, 1)
    u = LAYER + 4
    targets = ((0, 1, 2, u - 1), (0, 1, u - 2, u - 1), (0, u - 3, u - 2, u - 1))
    bias = b1[0:1, :]
    within = inside(-2, u)
    tiles = []
    for f in range(2):
        ys = []
        for par in range(2):
            planes = []
            for plane in range(u):
                terms = [
                    frame(sums[dp][f][par], targets[dp].index(plane))
                    for dp in range(3)
                    if plane in targets[dp]
                ]
                if 1 <= plane <= u - 2:
                    terms.append(acc[f, par, FRAME * (plane - 1) : FRAME * plane, :])
                planes.append(add(terms))
            for s in range(LAYER):
                kept = planes[2 + s][LEAD : LEAD + 16, :]
                kept = jnp.maximum(kept + bias, 0.0).astype(BF)
                skips[2 * s + f, 16 * par : 16 * par + 16, :] = kept
            ys.append(jnp.concatenate(planes, axis=0))
        y = jnp.maximum(ys[0], ys[1])
        y0, y1 = y[:, :128], y[:, 128:]
        y0 = jnp.maximum(y0, pltpu.roll(y0, 64, 1))
        y1 = jnp.maximum(y1, pltpu.roll(y1, 64, 1))
        y = jnp.maximum(jnp.where(left, y0, y1) + bias[:, :128], 0.0)
        tiles.append(jnp.where(within, y, 0.0))
    pooled = jnp.concatenate(tiles, axis=1)
    for dw in range(3):
        pd[dw] = shifted(pooled, dw - 1).astype(BF)


def second_kernel(v2a, v2c, over, beside, b2, b3, w2a, w2c, bias2, bias3):
    half, core = lax.axis_index("filt"), lax.axis_index("slab") % 2
    mine, other = half * 64, 64 - half * 64
    for row in range(2):
        w2a[pl.ds(aligned(128 * row + mine, 64), 64), :] = v2a[64 * row : 64 * row + 64, :]
        w2c[pl.ds(aligned(128 * row + mine, 64), 64), :] = v2c[64 * row : 64 * row + 64, :]

    def piece(ref):
        def rows(t):
            both = ref[16 * t : 16 * t + 16, :]
            return jnp.concatenate([both[:, :64], both[:, 64:]], axis=0)

        return banded(rows)

    for rows, at in ((piece(over), other + 32 * core), (piece(beside), other + 32 - 32 * core)):
        for dp, dw in TAPS:
            lanes = slice(128 * (3 * dp + dw), 128 * (3 * dp + dw) + 128)
            a, b, c, d = rows(dp, dw)
            w2a[pl.ds(aligned(at, 32), 32), lanes] = a
            w2a[pl.ds(aligned(128 + at, 32), 32), lanes] = b
            w2c[pl.ds(aligned(at, 32), 32), lanes] = c
            w2c[pl.ds(aligned(128 + at, 32), 32), lanes] = d
    theirs = over[432:433, :].astype(F32)
    here2, here3 = b2[...].astype(F32), b3[...].astype(F32)
    there2, there3 = theirs[:, :64], theirs[:, 64:]
    low = jnp.where(half == 0, here2, there2)
    high = jnp.where(half == 0, there2, here2)
    bias2[...] = jnp.broadcast_to(jnp.concatenate([low, high], axis=1), bias2.shape)
    turned = jnp.concatenate([there3[:, 32:], there3[:, :32]], axis=1)
    order3 = jnp.concatenate([here3, jnp.where(core == 1, turned, there3)], axis=1)
    bias3[...] = jnp.broadcast_to(order3, bias3.shape)


def two_kernel(pd, w2a, w2c, b2, hd):
    left = lax.broadcasted_iota(jnp.int32, (1, 128), 1) < 64
    m = (LAYER + 2) * FRAME
    pairs = pair(
        [jnp.concatenate(lanes_of(pd, m, 128 * a, 128 * a + 128), axis=1) for a in range(2)],
        w2a[...],
    )
    parts = [jnp.where(left, b, a) for a, b in zip(lanes_of(pd, m, 0, 128), lanes_of(pd, m, 128, 256))]
    mixed = dot(jnp.concatenate(parts, axis=1), w2c[...], NT)
    hidden = jnp.concatenate(
        [
            pairs[0][:, :128],
            pairs[0][:, 128:] + mixed[:, :128],
            pairs[1][:, :128] + mixed[:, 128:],
            pairs[1][:, 128:],
        ],
        axis=1,
    )
    bias = jnp.concatenate([b2[0:1, :]] * 4, axis=1)
    hidden = jnp.where(inside(-1, LAYER + 2), jnp.maximum(hidden + bias, 0.0), 0.0).astype(BF).astype(F32)
    for dw in range(3):
        hd[dw] = shifted(hidden, dw - 1).astype(BF)


def three_kernel(hd, k3, over, beside, b3, skips, out):
    half, core = lax.axis_index("filt"), lax.axis_index("slab") % 2
    lane = lax.broadcasted_iota(jnp.int32, (1, 128), 1)
    left = lane < 64
    out[:, 0:32, :] = skips[...]
    m = LAYER * FRAME

    def third(t):
        rows = slice(32 * t, 32 * t + 32)
        return jnp.concatenate([k3[t], over[rows, :], beside[rows, :]], axis=0)

    none = jnp.zeros((128, 128), BF)
    straight, across = [[], []], [[], []]
    for dp, dw in TAPS:
        k0, k1, k2 = (third(9 * dp + 3 * dr + dw) for dr in range(3))
        straight[0] += [k1, k2]
        straight[1] += [k0, k1]
        across[0] += [none, k2]
        across[1] += [k0, none]
    w3a = jnp.concatenate([jnp.concatenate(rows, axis=1) for rows in straight], axis=0)
    w3c = jnp.concatenate([jnp.concatenate(rows, axis=1) for rows in across], axis=0)
    both = jnp.concatenate(
        [jnp.concatenate(lanes_of(hd, m, 256 * a, 256 * a + 256), axis=1) for a in range(2)], axis=0
    )
    both = dot(both, w3a, NT)
    mixed = dot(jnp.concatenate(lanes_of(hd, m, 128, 384), axis=1), w3c, NT)
    t0, t1 = both[:m, :128], both[:m, 128:] + mixed[:, :128]
    t2, t3 = both[m:, :128] + mixed[:, 128:], both[m:, 128:]
    t0, t1, t2, t3 = (jnp.maximum(t + b3[0:1, :], 0.0) for t in (t0, t1, t2, t3))
    r0, r1, r2, r3 = (pltpu.roll(t, 64, 1) for t in (t0, t1, t2, t3))
    first = jnp.concatenate([jnp.where(left, t0, r1), jnp.where(left, t2, r3)], axis=1)
    second = jnp.concatenate([jnp.where(left, r0, t1), jnp.where(left, r2, t3)], axis=1)
    lane = lax.broadcasted_iota(jnp.int32, (1, 256), 1)
    swapped = jnp.where(lane % 64 < 32, pltpu.roll(second, 224, 1), pltpu.roll(second, 32, 1))
    second = jnp.where(core == 1, swapped, second)
    for s in range(LAYER):
        top = FRAME * s + LEAD
        out[2 * s + half, 32:48, :] = first[top : top + 16, :].astype(BF)
        out[2 * s + 1 - half, 32:48, :] = second[top : top + 16, :].astype(BF)


def unpack_kernel(got, order, same, skip, features):
    count = got.shape[0]
    ones = got[:, 0:32, :].reshape(count * 32, 256)
    twos = got[:, 32:48, :].reshape(count * 16, 256)
    by_column = dot(order[...], ones, NN).astype(BF)
    skip[...] = dot(same[...], by_column, NT).astype(BF)
    features[...] = dot(same[...], twos, NT).astype(BF)


def shape(*dims):
    return jax.ShapeDtypeStruct(dims, BF)


def call(kernel, outs, *operands, scratch=(), limit=8, far=0):
    spec = pl.BlockSpec(memory_space=pltpu.VMEM)
    hbm = pl.BlockSpec(memory_space=pltpu.HBM)
    there = [pltpu.with_memory_space_constraint(x, pltpu.HBM) for x in operands[:far]]
    operands = [*there, *operands[far:]]
    return pl.pallas_call(
        kernel,
        out_shape=outs,
        in_specs=[hbm] * far + [spec] * (len(operands) - far),
        out_specs=jax.tree.map(lambda _: spec, outs),
        scratch_shapes=scratch,
        compiler_params=pltpu.CompilerParams(vmem_limit_bytes=limit << 20),
    )(*operands)


def near(x):
    return pltpu.with_memory_space_constraint(x, pltpu.VMEM)


def by_columns(volume, kernel_one, bias_one, kernel_two, bias_two, kernel_three, bias_three):
    slabs, halves = lax.axis_size("slab"), lax.axis_size("filt")
    peers = LAYER * halves
    groups = [[peers * g + i for i in range(peers)] for g in range(slabs // LAYER)]
    exchange = functools.partial(
        lax.all_to_all,
        axis_name=("slab", "filt"),
        split_axis=0,
        concat_axis=0,
        axis_index_groups=groups,
        tiled=True,
    )
    b1, b2, b3 = bias_one[None, :], bias_two[None, :], bias_three[None, :]
    blocks, *mine = call(
        pack_kernel,
        (
            pltpu.VMEM((peers, 2 * RUN, 256), BF),
            pltpu.VMEM((27, 32, 64), BF),
            pltpu.VMEM((27, 32, 128), BF),
            pltpu.VMEM((1, 64), BF),
            pltpu.VMEM((1, 64), BF),
        ),
        volume.reshape(256, 256),
        kernel_two,
        kernel_three,
        b2,
        b3,
        scratch=[pltpu.VMEM((256, 256), BF), pltpu.SemaphoreType.DMA((5,))],
        far=5,
    )
    mid = exchange(blocks)
    halves_sent = (pltpu.VMEM((448, 128), BF), pltpu.VMEM((864, 128), BF))
    sent2, sent3 = call(send_kernel, halves_sent, *map(near, mine))
    over2 = lax.ppermute(sent2, "filt", [(0, 1), (1, 0)])
    over3 = lax.ppermute(sent3, "filt", [(0, 1), (1, 0)])
    w1a, w1c, v2a, v2c, bias1, k3, order, same = call(
        first_kernel,
        (
            pltpu.VMEM((256, 2304), BF),
            pltpu.VMEM((128, 1152), BF),
            pltpu.VMEM((128, 1152), BF),
            pltpu.VMEM((128, 1152), BF),
            pltpu.VMEM((8, 256), F32),
            pltpu.VMEM(kernel_three.shape, BF),
            pltpu.VMEM((256, 256), BF),
            pltpu.VMEM((256, 256), BF),
        ),
        kernel_three,
        kernel_one,
        kernel_two,
        b1,
        scratch=[pltpu.SemaphoreType.DMA],
        far=1,
    )
    planes = pltpu.VMEM((2 * (LAYER - 1), 2 * RUN, 256), BF)
    to_first, to_second = call(rim_kernel, (planes, planes), near(mid))

    def swaps(start):
        up = [(i, i + LAYER) for i in range(slabs - LAYER) if i // LAYER % 2 == start]
        both = dict(up + [(b, a) for a, b in up])
        return [(i, both.get(i, i ^ 1)) for i in range(slabs)]

    rim_a = lax.ppermute(to_first, "slab", swaps(0))
    rim_b = lax.ppermute(to_second, "slab", swaps(1))
    other_core = [(i, i ^ 1) for i in range(slabs)]
    beside2 = lax.ppermute(over2, "slab", other_core)
    beside3 = lax.ppermute(over3, "slab", other_core)
    w2a, w2c, bias2, bias3 = call(
        second_kernel,
        (
            pltpu.VMEM((256, 1152), BF),
            pltpu.VMEM((256, 1152), BF),
            pltpu.VMEM((8, 128), F32),
            pltpu.VMEM((8, 128), F32),
        ),
        *map(near, (v2a, v2c, over2, beside2, b2, b3)),
    )

    def space(planes):
        rows = FRAME * planes
        return [pltpu.VMEM((2, 4, rows, 256), BF), pltpu.VMEM((4, rows, 128), BF)]

    acc = call(
        inner_kernel,
        pltpu.VMEM((2, 2, FRAME * (LAYER + 2), 256), F32),
        *map(near, (mid, w1a, w1c)),
        scratch=space(LAYER),
        limit=24,
    )
    skips, pooled = call(
        one_kernel,
        (pltpu.VMEM((peers, 32, 256), BF), pltpu.VMEM((3, FRAME * (LAYER + 4), 256), BF)),
        *map(near, (rim_a, rim_b, w1a, w1c, bias1, acc)),
        scratch=space(6),
        limit=24,
    )
    hidden = call(
        two_kernel,
        pltpu.VMEM((3, FRAME * (LAYER + 2), 512), BF),
        *map(near, (pooled, w2a, w2c, bias2)),
        limit=24,
    )
    out = call(
        three_kernel,
        pltpu.VMEM((peers, 48, 256), BF),
        *map(near, (hidden, k3, over3, beside3, bias3, skips)),
        limit=24,
    )
    home = exchange(out)
    outs = (shape(256, 256), shape(256, 128))
    skip, features = call(unpack_kernel, outs, *map(near, (home, order, same)))
    return skip.reshape(volume.shape), features.reshape(1, 4, 64, 128)


def fits(volume, kernels, slabs, halves):
    return (
        volume == (1, 4, 64, 256)
        and kernels == [(27, 64, 64), (27, 64, 64), (27, 64, 128)]
        and halves == 2
        and slabs % LAYER == 0
    )


def per_device(volume, *rest):
    kernels = [r.shape for r in rest[::2]]
    good = fits(volume.shape, kernels, lax.axis_size("slab"), lax.axis_size("filt"))
    if not good:
        return by_planes(volume, *rest)
    return by_columns(volume, *rest)


def solution(mesh):
    return jax.shard_map(
        per_device,
        mesh=mesh,
        in_specs=(
            P("slab", "filt", None, None),
            P(),
            P(),
            P(None, "filt", None),
            P("filt"),
            P(None, "filt", None),
            P("filt"),
        ),
        out_specs=(P("slab", "filt", None, None), P("slab", None, "filt", None)),
        check_vma=False,
    )
```

```python
import functools

import jax
import jax.numpy as jnp
from jax import lax
from jax.experimental import pallas as pl
from jax.experimental.pallas import tpu as pltpu
from jax.sharding import PartitionSpec as P


BF = jnp.bfloat16
F32 = jnp.float32
NT = (((1,), (1,)), ((), ()))
NN = (((1,), (0,)), ((), ()))

LAYER = 4
RUN = 24
FRAME = RUN
LEAD = 4


def extended(block, sides, width):
    for axis, dim in sides:
        count = lax.axis_size(axis)
        forward = [(i, i + 1) for i in range(count - 1)]
        backward = [(target, source) for source, target in forward]
        low = lax.ppermute(
            lax.slice_in_dim(block, block.shape[dim] - width, None, axis=dim), axis, forward
        )
        high = lax.ppermute(lax.slice_in_dim(block, 0, width, axis=dim), axis, backward)
        block = jnp.concatenate([low, block, high], axis=dim)
    return block


def pad_columns(field):
    return jnp.pad(field, ((0, 0), (0, 0), (0, 0), (1, 1)))


def accumulate(total, padded, kernel):
    planes, rows, _, cols = total.shape
    for kd in range(3):
        for kh in range(3):
            for kw in range(3):
                tap = 9 * kd + 3 * kh + kw
                total = total + jnp.einsum(
                    "oc,dhcw->dhow",
                    kernel[tap],
                    padded[kd : kd + planes, kh : kh + rows, :, kw : kw + cols],
                    preferred_element_type=jnp.float32,
                )
    return total


def finish(total, bias):
    return jnp.maximum(total + bias.astype(jnp.float32)[None, None, :, None], 0.0).astype(
        jnp.bfloat16
    )


def by_planes(volume, kernel_one, bias_one, kernel_two, bias_two, kernel_three, bias_three):
    planes, rows, chans, cols = volume.shape
    rimmed = extended(volume, (("slab", 0), ("filt", 1)), 1)
    start_one = jnp.zeros((planes, rows, kernel_one.shape[1], cols), jnp.float32)
    skip_one = finish(accumulate(start_one, pad_columns(rimmed), kernel_one), bias_one)
    pooled = jnp.max(skip_one.reshape(planes, rows // 2, 2, chans, cols // 2, 2), axis=(2, 5))
    full_rows = lax.all_gather(pooled, "filt", axis=1, tiled=True)
    planed = extended(full_rows, (("slab", 0),), 1)
    padded = jnp.pad(planed, ((0, 0), (1, 1), (0, 0), (1, 1)))
    height = full_rows.shape[1]
    width = full_rows.shape[3]
    start_two = jnp.zeros((planes, height, kernel_two.shape[1], width), jnp.float32)
    hidden = finish(accumulate(start_two, padded, kernel_two), bias_two)
    hidden_planes = extended(hidden, (("slab", 0),), 1)
    start_three = jnp.zeros((planes, height, kernel_three.shape[1], width), jnp.float32)
    piece_padded = jnp.pad(
        lax.all_gather(hidden_planes, "filt", axis=2, tiled=True), ((0, 0), (1, 1), (0, 0), (1, 1))
    )
    summed = accumulate(start_three, piece_padded, kernel_three)
    features_two = finish(summed, bias_three)
    return (skip_one, features_two)


def dot(a, b, dims):
    return lax.dot_general(a, b, dims, preferred_element_type=F32)


def pack_kernel(far, far2, far3, far_b2, far_b3, blocks, k2, k3, b2, b3, volume, sems):
    half = pl.ds(aligned(32 * (lax.axis_index("slab") % 2), 32), 32)
    pairs = (
        (far, volume),
        (far2.at[:, half, :], k2),
        (far3, k3),
        (far_b2, b2),
        (far_b3, b3),
    )
    copies = [pltpu.make_async_copy(*ends, sems.at[i]) for i, ends in enumerate(pairs)]
    for copy in copies:
        copy.start()
    count, width = blocks.shape[0], volume.shape[1]
    shape = (count * 2 * RUN, width)
    row = lax.broadcasted_iota(jnp.int32, shape, 0)
    col = lax.broadcasted_iota(jnp.int32, shape, 1)
    peer, rest = row // (2 * RUN), row % (2 * RUN)
    wanted = (width // count) * peer + 2 * (rest % RUN - LEAD) + rest // RUN
    chosen = jnp.where(wanted == col, 1.0, 0.0).astype(BF)
    copies[0].wait()
    blocks[...] = dot(chosen, volume[...], NT).astype(BF).reshape(blocks.shape)
    for copy in copies[1:]:
        copy.wait()


def aligned(at, by):
    return pl.multiple_of(at, by)


def send_kernel(k2, k3, b2, b3, sent2, sent3):
    half = pl.ds(aligned(32 * (lax.axis_index("slab") % 2), 32), 32)
    for t in range(27):
        sent2[16 * t : 16 * t + 16, :] = jnp.concatenate([k2[t, :16, :], k2[t, 16:, :]], axis=1)
        sent3[32 * t : 32 * t + 32, :] = k3[t, half, :]
    both = jnp.concatenate([b2[...], b3[...]], axis=1)
    sent2[432:448, :] = jnp.broadcast_to(both, (16, 128))


def banded(k_ref):
    def pieces(dp, dw):
        k0, k1, k2 = (k_ref(9 * dp + 3 * dr + dw) for dr in range(3))
        none = jnp.zeros_like(k0)
        join = lambda a, b: jnp.concatenate([a, b], axis=1)
        return join(k1, k2), join(k0, k1), join(k2, none), join(none, k0)

    return pieces


def rim_kernel(mid, to_first, to_second):
    odd = lax.axis_index("slab") // LAYER % 2
    n = to_first.shape[0]
    to_first[...] = mid[pl.ds(2 - 2 * odd, n)]
    to_second[...] = mid[pl.ds(2 * odd, n)]


def first_kernel(k1, k2, b1, w1a, w1c, v2a, v2c, bias, order, same):
    row = lax.broadcasted_iota(jnp.int32, order.shape, 0)
    col = lax.broadcasted_iota(jnp.int32, order.shape, 1)
    source = 32 * (row // 32) + 16 * (row % 2) + row % 32 // 2
    order[...] = jnp.where(source == col, 1.0, 0.0).astype(BF)
    same[...] = jnp.where(row == col, 1.0, 0.0).astype(BF)
    one = banded(lambda t: k1[t])
    two = banded(lambda t: k2[t])
    zero = jnp.zeros((64, 128), BF)
    for dp in range(3):
        for dw in range(3):
            t = 3 * dp + dw
            a, b, c, d = one(dp, dw)
            for i, (low, high) in enumerate(((a, zero), (b, c), (d, a), (zero, b))):
                w1a[64 * i : 64 * i + 64, 256 * t : 256 * t + 128] = low
                w1a[64 * i : 64 * i + 64, 256 * t + 128 : 256 * t + 256] = high
            lanes = slice(128 * t, 128 * t + 128)
            w1c[0:64, lanes] = d
            w1c[64:128, lanes] = c
            a, b, c, d = two(dp, dw)
            v2a[0:64, lanes] = a
            v2a[64:128, lanes] = b
            v2c[0:64, lanes] = c
            v2c[64:128, lanes] = d
    bias[...] = jnp.broadcast_to(jnp.concatenate([b1[...].astype(F32)] * 4, axis=1), bias.shape)


def shifted(x, by):
    return pltpu.roll(x, (-by) % x.shape[0], 0)


TAPS = [(dp, dw) for dp in range(3) for dw in range(3)]


def inside(first, planes):
    half, slab = lax.axis_index("filt"), lax.axis_index("slab")
    layer, layers = slab // LAYER, lax.axis_size("slab") // LAYER
    group = slab % LAYER * lax.axis_size("filt") + half
    row = lax.broadcasted_iota(jnp.int32, (planes * FRAME, 1), 0)
    col = 16 * group - LEAD + row % FRAME
    plane = LAYER * layer + first + row // FRAME
    return (plane >= 0) & (plane < LAYER * layers) & (col >= 0) & (col < 128)


def pair(parts, weights):
    n = parts[0].shape[0]
    all_rows = dot(jnp.concatenate(parts, axis=0), weights, NT)
    return [all_rows[n * i : n * i + n] for i in range(len(parts))]


def lanes_of(ref, n, lo, hi):
    return [ref[dw, FRAME * dp : FRAME * dp + n, lo:hi] for dp, dw in TAPS]


def spread_runs(run, planes, q, x34):
    left = lax.broadcasted_iota(jnp.int32, (1, 128), 1) < 64
    for f in range(2):
        for par in range(2):
            rows = slice(RUN * par, RUN * par + RUN)
            whole = jnp.concatenate([run(v, f, rows).astype(F32) for v in planes], axis=0)
            q[f, 1 + par] = whole.astype(BF)
            if par == 0:
                q[f, 3] = shifted(whole, 1).astype(BF)
            else:
                q[f, 0] = shifted(whole, -1).astype(BF)
    for a in range(4):
        x34[a] = jnp.where(left, q[1, a, :, 0:128], q[0, a, :, 128:256])


def products(q, x34, w1a, w1c, step):
    left = lax.broadcasted_iota(jnp.int32, (1, 128), 1) < 64
    n = LAYER * FRAME
    out = []
    for dp in range(3):
        rows = slice(FRAME * step * dp, FRAME * step * dp + n)

        def pick(ref, par):
            return jnp.concatenate([ref[par + dw, rows, :] for dw in range(3)], axis=1)

        cross = pair([pick(x34, par) for par in range(2)], w1c[:, 384 * dp : 384 * dp + 384])
        weights = w1a[:, 768 * dp : 768 * dp + 768]
        parts = [pick(q.at[f], par) for f in range(2) for par in range(2)]
        if dp < 2:
            together = pair(parts, weights)
        else:
            together = pair(parts[:2], weights) + pair(parts[2:], weights)
        sums = []
        for f in range(2):
            ys = together[2 * f : 2 * f + 2]
            for par in range(2):
                low, high = ys[par][:, :128], ys[par][:, 128:]
                if f == 0:
                    high = high + jnp.where(left, 0.0, cross[par])
                else:
                    low = low + jnp.where(left, cross[par], 0.0)
                ys[par] = jnp.concatenate([low, high], axis=1)
            sums.append(ys)
        out.append(sums)
    return out


def frame(x, i):
    return x[FRAME * i : FRAME * i + FRAME]


def add(terms):
    return functools.reduce(jnp.add, terms)


def inner_kernel(mid, w1a, w1c, acc, q, x34):
    spread_runs(lambda v, f, rows: mid[2 * v + f, rows, :], range(LAYER), q, x34)
    sums = products(q, x34, w1a, w1c, 0)
    for f in range(2):
        for par in range(2):
            for e in range(LAYER + 2):
                terms = [
                    frame(sums[dp][f][par], e - 2 + dp)
                    for dp in range(3)
                    if 0 <= e - 2 + dp < LAYER
                ]
                acc[f, par, FRAME * e : FRAME * e + FRAME, :] = add(terms)


def halo_kernel(rim_a, rim_b, q, x34):
    layer, layers = lax.axis_index("slab") // LAYER, lax.axis_size("slab") // LAYER
    odd = layer % 2 == 1

    def run(v, f, rows):
        at = 2 * (v % 3) + f
        got = jnp.where(odd == (v < 3), rim_a[at, rows, :], rim_b[at, rows, :])
        outside = layer == (0 if v < 3 else layers - 1)
        return jnp.where(outside, jnp.zeros_like(got), got)

    spread_runs(run, range(6), q, x34)


def one_kernel(q, x34, w1a, w1c, b1, acc, skips, pd):
    left = lax.broadcasted_iota(jnp.int32, (1, 128), 1) < 64
    sums = products(q, x34, w1a, w1c, 1)
    u = LAYER + 4
    targets = ((0, 1, 2, u - 1), (0, 1, u - 2, u - 1), (0, u - 3, u - 2, u - 1))
    bias = b1[0:1, :]
    within = inside(-2, u)
    tiles = []
    for f in range(2):
        ys = []
        for par in range(2):
            planes = []
            for plane in range(u):
                terms = [
                    frame(sums[dp][f][par], targets[dp].index(plane))
                    for dp in range(3)
                    if plane in targets[dp]
                ]
                if 1 <= plane <= u - 2:
                    terms.append(acc[f, par, FRAME * (plane - 1) : FRAME * plane, :])
                planes.append(add(terms))
            for s in range(LAYER):
                kept = planes[2 + s][LEAD : LEAD + 16, :]
                kept = jnp.maximum(kept + bias, 0.0).astype(BF)
                skips[2 * s + f, 16 * par : 16 * par + 16, :] = kept
            ys.append(jnp.concatenate(planes, axis=0))
        y = jnp.maximum(ys[0], ys[1])
        y0, y1 = y[:, :128], y[:, 128:]
        y0 = jnp.maximum(y0, pltpu.roll(y0, 64, 1))
        y1 = jnp.maximum(y1, pltpu.roll(y1, 64, 1))
        y = jnp.maximum(jnp.where(left, y0, y1) + bias[:, :128], 0.0)
        tiles.append(jnp.where(within, y, 0.0))
    pooled = jnp.concatenate(tiles, axis=1)
    for dw in range(3):
        pd[dw] = shifted(pooled, dw - 1).astype(BF)


def second_kernel(v2a, v2c, over, beside, b2, b3, w2a, w2c, bias2, bias3):
    half, core = lax.axis_index("filt"), lax.axis_index("slab") % 2
    mine, other = half * 64, 64 - half * 64
    for row in range(2):
        w2a[pl.ds(aligned(128 * row + mine, 64), 64), :] = v2a[64 * row : 64 * row + 64, :]
        w2c[pl.ds(aligned(128 * row + mine, 64), 64), :] = v2c[64 * row : 64 * row + 64, :]

    def piece(ref):
        def rows(t):
            both = ref[16 * t : 16 * t + 16, :]
            return jnp.concatenate([both[:, :64], both[:, 64:]], axis=0)

        return banded(rows)

    for rows, at in ((piece(over), other + 32 * core), (piece(beside), other + 32 - 32 * core)):
        for dp, dw in TAPS:
            lanes = slice(128 * (3 * dp + dw), 128 * (3 * dp + dw) + 128)
            a, b, c, d = rows(dp, dw)
            w2a[pl.ds(aligned(at, 32), 32), lanes] = a
            w2a[pl.ds(aligned(128 + at, 32), 32), lanes] = b
            w2c[pl.ds(aligned(at, 32), 32), lanes] = c
            w2c[pl.ds(aligned(128 + at, 32), 32), lanes] = d
    theirs = over[432:433, :].astype(F32)
    here2, here3 = b2[...].astype(F32), b3[...].astype(F32)
    there2, there3 = theirs[:, :64], theirs[:, 64:]
    low = jnp.where(half == 0, here2, there2)
    high = jnp.where(half == 0, there2, here2)
    bias2[...] = jnp.broadcast_to(jnp.concatenate([low, high], axis=1), bias2.shape)
    turned = jnp.concatenate([there3[:, 32:], there3[:, :32]], axis=1)
    order3 = jnp.concatenate([here3, jnp.where(core == 1, turned, there3)], axis=1)
    bias3[...] = jnp.broadcast_to(order3, bias3.shape)


def two_kernel(pd, w2a, w2c, b2, hd):
    left = lax.broadcasted_iota(jnp.int32, (1, 128), 1) < 64
    m = (LAYER + 2) * FRAME
    pairs = pair(
        [jnp.concatenate(lanes_of(pd, m, 128 * a, 128 * a + 128), axis=1) for a in range(2)],
        w2a[...],
    )
    parts = [jnp.where(left, b, a) for a, b in zip(lanes_of(pd, m, 0, 128), lanes_of(pd, m, 128, 256))]
    mixed = dot(jnp.concatenate(parts, axis=1), w2c[...], NT)
    hidden = jnp.concatenate(
        [
            pairs[0][:, :128],
            pairs[0][:, 128:] + mixed[:, :128],
            pairs[1][:, :128] + mixed[:, 128:],
            pairs[1][:, 128:],
        ],
        axis=1,
    )
    bias = jnp.concatenate([b2[0:1, :]] * 4, axis=1)
    hidden = jnp.where(inside(-1, LAYER + 2), jnp.maximum(hidden + bias, 0.0), 0.0).astype(BF).astype(F32)
    for dw in range(3):
        hd[dw] = shifted(hidden, dw - 1).astype(BF)


def three_kernel(hd, k3, over, beside, b3, skips, out):
    half, core = lax.axis_index("filt"), lax.axis_index("slab") % 2
    lane = lax.broadcasted_iota(jnp.int32, (1, 128), 1)
    left = lane < 64
    out[:, 0:32, :] = skips[...]
    m = LAYER * FRAME

    def third(t):
        rows = slice(32 * t, 32 * t + 32)
        return jnp.concatenate([k3[t], over[rows, :], beside[rows, :]], axis=0)

    straight, low, high = [[], []], [], []
    for dp, dw in TAPS:
        k0, k1, k2 = (third(9 * dp + 3 * dr + dw) for dr in range(3))
        straight[0] += [k1, k2]
        straight[1] += [k0, k1]
        low.append(k0)
        high.append(k2)
    w3a = jnp.concatenate([jnp.concatenate(rows, axis=1) for rows in straight], axis=0)
    both = jnp.concatenate(
        [jnp.concatenate(lanes_of(hd, m, 256 * a, 256 * a + 256), axis=1) for a in range(2)], axis=0
    )
    both = dot(both, w3a, NT)
    cat = lambda parts: jnp.concatenate(parts, axis=1)
    up = dot(cat(lanes_of(hd, m, 256, 384)), cat(high), NT)
    down = dot(cat(lanes_of(hd, m, 128, 256)), cat(low), NT)
    t0, t1 = both[:m, :128], both[:m, 128:] + up
    t2, t3 = both[m:, :128] + down, both[m:, 128:]
    t0, t1, t2, t3 = (jnp.maximum(t + b3[0:1, :], 0.0) for t in (t0, t1, t2, t3))
    r0, r1, r2, r3 = (pltpu.roll(t, 64, 1) for t in (t0, t1, t2, t3))
    first = jnp.concatenate([jnp.where(left, t0, r1), jnp.where(left, t2, r3)], axis=1)
    second = jnp.concatenate([jnp.where(left, r0, t1), jnp.where(left, r2, t3)], axis=1)
    lane = lax.broadcasted_iota(jnp.int32, (1, 256), 1)
    swapped = jnp.where(lane % 64 < 32, pltpu.roll(second, 224, 1), pltpu.roll(second, 32, 1))
    second = jnp.where(core == 1, swapped, second)
    for s in range(LAYER):
        top = FRAME * s + LEAD
        out[2 * s + half, 32:48, :] = first[top : top + 16, :].astype(BF)
        out[2 * s + 1 - half, 32:48, :] = second[top : top + 16, :].astype(BF)


def unpack_kernel(got, order, same, skip, features):
    count = got.shape[0]
    ones = got[:, 0:32, :].reshape(count * 32, 256)
    twos = got[:, 32:48, :].reshape(count * 16, 256)
    by_column = dot(order[...], ones, NN).astype(BF)
    skip[...] = dot(same[...], by_column, NT).astype(BF)
    features[...] = dot(same[...], twos, NT).astype(BF)


def shape(*dims):
    return jax.ShapeDtypeStruct(dims, BF)


def call(kernel, outs, *operands, scratch=(), limit=8, far=0):
    spec = pl.BlockSpec(memory_space=pltpu.VMEM)
    hbm = pl.BlockSpec(memory_space=pltpu.HBM)
    there = [pltpu.with_memory_space_constraint(x, pltpu.HBM) for x in operands[:far]]
    operands = [*there, *operands[far:]]
    return pl.pallas_call(
        kernel,
        out_shape=outs,
        in_specs=[hbm] * far + [spec] * (len(operands) - far),
        out_specs=jax.tree.map(lambda _: spec, outs),
        scratch_shapes=scratch,
        compiler_params=pltpu.CompilerParams(vmem_limit_bytes=limit << 20),
    )(*operands)


def near(x):
    return pltpu.with_memory_space_constraint(x, pltpu.VMEM)


def by_columns(volume, kernel_one, bias_one, kernel_two, bias_two, kernel_three, bias_three):
    slabs, halves = lax.axis_size("slab"), lax.axis_size("filt")
    peers = LAYER * halves
    groups = [[peers * g + i for i in range(peers)] for g in range(slabs // LAYER)]
    exchange = functools.partial(
        lax.all_to_all,
        axis_name=("slab", "filt"),
        split_axis=0,
        concat_axis=0,
        axis_index_groups=groups,
        tiled=True,
    )
    b1, b2, b3 = bias_one[None, :], bias_two[None, :], bias_three[None, :]
    blocks, *mine = call(
        pack_kernel,
        (
            pltpu.VMEM((peers, 2 * RUN, 256), BF),
            pltpu.VMEM((27, 32, 64), BF),
            pltpu.VMEM(kernel_three.shape, BF),
            pltpu.VMEM((1, 64), BF),
            pltpu.VMEM((1, 64), BF),
        ),
        volume.reshape(256, 256),
        kernel_two,
        kernel_three,
        b2,
        b3,
        scratch=[pltpu.VMEM((256, 256), BF), pltpu.SemaphoreType.DMA((5,))],
        far=5,
    )
    mid = exchange(blocks)
    halves_sent = (pltpu.VMEM((448, 128), BF), pltpu.VMEM((864, 128), BF))
    sent2, sent3 = call(send_kernel, halves_sent, *map(near, mine))
    over2 = lax.ppermute(sent2, "filt", [(0, 1), (1, 0)])
    over3 = lax.ppermute(sent3, "filt", [(0, 1), (1, 0)])
    w1a, w1c, v2a, v2c, bias1, order, same = call(
        first_kernel,
        (
            pltpu.VMEM((256, 2304), BF),
            pltpu.VMEM((128, 1152), BF),
            pltpu.VMEM((128, 1152), BF),
            pltpu.VMEM((128, 1152), BF),
            pltpu.VMEM((8, 256), F32),
            pltpu.VMEM((256, 256), BF),
            pltpu.VMEM((256, 256), BF),
        ),
        kernel_one,
        kernel_two,
        b1,
    )
    planes = pltpu.VMEM((2 * (LAYER - 1), 2 * RUN, 256), BF)
    to_first, to_second = call(rim_kernel, (planes, planes), near(mid))

    def swaps(start):
        up = [(i, i + LAYER) for i in range(slabs - LAYER) if i // LAYER % 2 == start]
        both = dict(up + [(b, a) for a, b in up])
        return [(i, both.get(i, i ^ 1)) for i in range(slabs)]

    rim_a = lax.ppermute(to_first, "slab", swaps(0))
    rim_b = lax.ppermute(to_second, "slab", swaps(1))
    other_core = [(i, i ^ 1) for i in range(slabs)]
    beside2 = lax.ppermute(over2, "slab", other_core)
    beside3 = lax.ppermute(over3, "slab", other_core)
    w2a, w2c, bias2, bias3 = call(
        second_kernel,
        (
            pltpu.VMEM((256, 1152), BF),
            pltpu.VMEM((256, 1152), BF),
            pltpu.VMEM((8, 128), F32),
            pltpu.VMEM((8, 128), F32),
        ),
        *map(near, (v2a, v2c, over2, beside2, b2, b3)),
    )

    def space(planes):
        rows = FRAME * planes
        return [pltpu.VMEM((2, 4, rows, 256), BF), pltpu.VMEM((4, rows, 128), BF)]

    acc = call(
        inner_kernel,
        pltpu.VMEM((2, 2, FRAME * (LAYER + 2), 256), F32),
        *map(near, (mid, w1a, w1c)),
        scratch=space(LAYER),
        limit=24,
    )
    halo = call(halo_kernel, tuple(space(6)), near(rim_a), near(rim_b), limit=24)
    skips, pooled = call(
        one_kernel,
        (pltpu.VMEM((peers, 32, 256), BF), pltpu.VMEM((3, FRAME * (LAYER + 4), 256), BF)),
        *map(near, (*halo, w1a, w1c, bias1, acc)),
        limit=24,
    )
    hidden = call(
        two_kernel,
        pltpu.VMEM((3, FRAME * (LAYER + 2), 512), BF),
        *map(near, (pooled, w2a, w2c, bias2)),
        limit=24,
    )
    out = call(
        three_kernel,
        pltpu.VMEM((peers, 48, 256), BF),
        *map(near, (hidden, mine[1], over3, beside3, bias3, skips)),
        limit=24,
    )
    home = exchange(out)
    outs = (shape(256, 256), shape(256, 128))
    skip, features = call(unpack_kernel, outs, *map(near, (home, order, same)))
    return skip.reshape(volume.shape), features.reshape(1, 4, 64, 128)


def fits(volume, kernels, slabs, halves):
    return (
        volume == (1, 4, 64, 256)
        and kernels == [(27, 64, 64), (27, 64, 64), (27, 64, 128)]
        and halves == 2
        and slabs % LAYER == 0
    )


def per_device(volume, *rest):
    kernels = [r.shape for r in rest[::2]]
    good = fits(volume.shape, kernels, lax.axis_size("slab"), lax.axis_size("filt"))
    if not good:
        return by_planes(volume, *rest)
    return by_columns(volume, *rest)


def solution(mesh):
    return jax.shard_map(
        per_device,
        mesh=mesh,
        in_specs=(
            P("slab", "filt", None, None),
            P(),
            P(),
            P(None, "filt", None),
            P("filt"),
            P(None, "filt", None),
            P("filt"),
        ),
        out_specs=(P("slab", "filt", None, None), P("slab", None, "filt", None)),
        check_vma=False,
    )
```

```python
import functools

import jax
import jax.numpy as jnp
from jax import lax
from jax.experimental import pallas as pl
from jax.experimental.pallas import tpu as pltpu
from jax.sharding import PartitionSpec as P


BF = jnp.bfloat16
F32 = jnp.float32
NT = (((1,), (1,)), ((), ()))
NN = (((1,), (0,)), ((), ()))

LAYER = 4
RUN = 24
FRAME = RUN
LEAD = 4


def extended(block, sides, width):
    for axis, dim in sides:
        count = lax.axis_size(axis)
        forward = [(i, i + 1) for i in range(count - 1)]
        backward = [(target, source) for source, target in forward]
        low = lax.ppermute(
            lax.slice_in_dim(block, block.shape[dim] - width, None, axis=dim), axis, forward
        )
        high = lax.ppermute(lax.slice_in_dim(block, 0, width, axis=dim), axis, backward)
        block = jnp.concatenate([low, block, high], axis=dim)
    return block


def pad_columns(field):
    return jnp.pad(field, ((0, 0), (0, 0), (0, 0), (1, 1)))


def accumulate(total, padded, kernel):
    planes, rows, _, cols = total.shape
    for kd in range(3):
        for kh in range(3):
            for kw in range(3):
                tap = 9 * kd + 3 * kh + kw
                total = total + jnp.einsum(
                    "oc,dhcw->dhow",
                    kernel[tap],
                    padded[kd : kd + planes, kh : kh + rows, :, kw : kw + cols],
                    preferred_element_type=jnp.float32,
                )
    return total


def finish(total, bias):
    return jnp.maximum(total + bias.astype(jnp.float32)[None, None, :, None], 0.0).astype(
        jnp.bfloat16
    )


def by_planes(volume, kernel_one, bias_one, kernel_two, bias_two, kernel_three, bias_three):
    planes, rows, chans, cols = volume.shape
    rimmed = extended(volume, (("slab", 0), ("filt", 1)), 1)
    start_one = jnp.zeros((planes, rows, kernel_one.shape[1], cols), jnp.float32)
    skip_one = finish(accumulate(start_one, pad_columns(rimmed), kernel_one), bias_one)
    pooled = jnp.max(skip_one.reshape(planes, rows // 2, 2, chans, cols // 2, 2), axis=(2, 5))
    full_rows = lax.all_gather(pooled, "filt", axis=1, tiled=True)
    planed = extended(full_rows, (("slab", 0),), 1)
    padded = jnp.pad(planed, ((0, 0), (1, 1), (0, 0), (1, 1)))
    height = full_rows.shape[1]
    width = full_rows.shape[3]
    start_two = jnp.zeros((planes, height, kernel_two.shape[1], width), jnp.float32)
    hidden = finish(accumulate(start_two, padded, kernel_two), bias_two)
    hidden_planes = extended(hidden, (("slab", 0),), 1)
    start_three = jnp.zeros((planes, height, kernel_three.shape[1], width), jnp.float32)
    piece_padded = jnp.pad(
        lax.all_gather(hidden_planes, "filt", axis=2, tiled=True), ((0, 0), (1, 1), (0, 0), (1, 1))
    )
    summed = accumulate(start_three, piece_padded, kernel_three)
    features_two = finish(summed, bias_three)
    return (skip_one, features_two)


def dot(a, b, dims):
    return lax.dot_general(a, b, dims, preferred_element_type=F32)


def pack_kernel(far, far2, far3, far_b2, far_b3, blocks, k2, k3, b2, b3, volume, sems):
    half = pl.ds(aligned(32 * (lax.axis_index("slab") % 2), 32), 32)
    pairs = (
        (far, volume),
        (far2.at[:, half, :], k2),
        (far3, k3),
        (far_b2, b2),
        (far_b3, b3),
    )
    copies = [pltpu.make_async_copy(*ends, sems.at[i]) for i, ends in enumerate(pairs)]
    for copy in copies:
        copy.start()
    count, width = blocks.shape[0], volume.shape[1]
    row = lax.broadcasted_iota(jnp.int32, (RUN, width), 0)
    col = lax.broadcasted_iota(jnp.int32, (RUN, width), 1)
    ahead = 2 * (row - LEAD) - col
    chosen = jnp.concatenate(
        [
            jnp.where(ahead == -(width // count) * peer - par, 1.0, 0.0)
            for peer in range(count)
            for par in range(2)
        ],
        axis=0,
    ).astype(BF)
    copies[0].wait()
    blocks[...] = dot(chosen, volume[...], NT).astype(BF).reshape(blocks.shape)
    for copy in copies[1:]:
        copy.wait()


def aligned(at, by):
    return pl.multiple_of(at, by)


def send_kernel(k2, k3, b2, b3, sent2, sent3):
    half = pl.ds(aligned(32 * (lax.axis_index("slab") % 2), 32), 32)
    for t in range(27):
        sent2[16 * t : 16 * t + 16, :] = jnp.concatenate([k2[t, :16, :], k2[t, 16:, :]], axis=1)
        sent3[32 * t : 32 * t + 32, :] = k3[t, half, :]
    both = jnp.concatenate([b2[...], b3[...]], axis=1)
    sent2[432:448, :] = jnp.broadcast_to(both, (16, 128))


def banded(k_ref):
    def pieces(dp, dw):
        k0, k1, k2 = (k_ref(9 * dp + 3 * dr + dw) for dr in range(3))
        none = jnp.zeros_like(k0)
        join = lambda a, b: jnp.concatenate([a, b], axis=1)
        return join(k1, k2), join(k0, k1), join(k2, none), join(none, k0)

    return pieces


def rim_kernel(mid, to_first, to_second):
    odd = lax.axis_index("slab") // LAYER % 2
    n = to_first.shape[0]
    to_first[...] = mid[pl.ds(2 - 2 * odd, n)]
    to_second[...] = mid[pl.ds(2 * odd, n)]


def first_kernel(k1, k2, b1, w1a, w1c, v2a, v2c, bias, order, same):
    row = lax.broadcasted_iota(jnp.int32, order.shape, 0)
    col = lax.broadcasted_iota(jnp.int32, order.shape, 1)
    source = 32 * (row // 32) + 16 * (row % 2) + row % 32 // 2
    order[...] = jnp.where(source == col, 1.0, 0.0).astype(BF)
    same[...] = jnp.where(row == col, 1.0, 0.0).astype(BF)
    one = banded(lambda t: k1[t])
    two = banded(lambda t: k2[t])
    zero = jnp.zeros((64, 128), BF)
    for dp in range(3):
        for dw in range(3):
            t = 3 * dp + dw
            a, b, c, d = one(dp, dw)
            for i, (low, high) in enumerate(((a, zero), (b, c), (d, a), (zero, b))):
                w1a[64 * i : 64 * i + 64, 256 * t : 256 * t + 128] = low
                w1a[64 * i : 64 * i + 64, 256 * t + 128 : 256 * t + 256] = high
            lanes = slice(128 * t, 128 * t + 128)
            w1c[0:64, lanes] = d
            w1c[64:128, lanes] = c
            a, b, c, d = two(dp, dw)
            v2a[0:64, lanes] = a
            v2a[64:128, lanes] = b
            v2c[0:64, lanes] = c
            v2c[64:128, lanes] = d
    bias[...] = jnp.broadcast_to(jnp.concatenate([b1[...].astype(F32)] * 4, axis=1), bias.shape)


def shifted(x, by):
    return pltpu.roll(x, (-by) % x.shape[0], 0)


TAPS = [(dp, dw) for dp in range(3) for dw in range(3)]


def inside(first, planes):
    half, slab = lax.axis_index("filt"), lax.axis_index("slab")
    layer, layers = slab // LAYER, lax.axis_size("slab") // LAYER
    group = slab % LAYER * lax.axis_size("filt") + half
    row = lax.broadcasted_iota(jnp.int32, (planes * FRAME, 1), 0)
    col = 16 * group - LEAD + row % FRAME
    plane = LAYER * layer + first + row // FRAME
    within = (plane >= 0) & (plane < LAYER * layers) & (col >= 0) & (col < 128)
    return jnp.broadcast_to(jnp.where(within, 1.0, 0.0), (planes * FRAME, 128))


def pair(parts, weights):
    n = parts[0].shape[0]
    all_rows = dot(jnp.concatenate(parts, axis=0), weights, NT)
    return [all_rows[n * i : n * i + n] for i in range(len(parts))]


def lanes_of(ref, n, lo, hi):
    return [ref[dw, FRAME * dp : FRAME * dp + n, lo:hi] for dp, dw in TAPS]


def spread_runs(run, planes, q, x34):
    left = lax.broadcasted_iota(jnp.int32, (1, 128), 1) < 64
    for f in range(2):
        for par in range(2):
            rows = slice(RUN * par, RUN * par + RUN)
            whole = jnp.concatenate([run(v, f, rows).astype(F32) for v in planes], axis=0)
            q[f, 1 + par] = whole.astype(BF)
            if par == 0:
                q[f, 3] = shifted(whole, 1).astype(BF)
            else:
                q[f, 0] = shifted(whole, -1).astype(BF)
    for a in range(4):
        x34[a] = jnp.where(left, q[1, a, :, 0:128], q[0, a, :, 128:256])


def products(q, x34, w1a, w1c, step):
    left = lax.broadcasted_iota(jnp.int32, (1, 128), 1) < 64
    n = LAYER * FRAME
    out = []
    for dp in range(3):
        rows = slice(FRAME * step * dp, FRAME * step * dp + n)

        def pick(ref, par):
            return jnp.concatenate([ref[par + dw, rows, :] for dw in range(3)], axis=1)

        cross = pair([pick(x34, par) for par in range(2)], w1c[:, 384 * dp : 384 * dp + 384])
        weights = w1a[:, 768 * dp : 768 * dp + 768]
        parts = [pick(q.at[f], par) for f in range(2) for par in range(2)]
        if dp < 2:
            together = pair(parts, weights)
        else:
            together = pair(parts[:2], weights) + pair(parts[2:], weights)
        sums = []
        for f in range(2):
            ys = together[2 * f : 2 * f + 2]
            for par in range(2):
                low, high = ys[par][:, :128], ys[par][:, 128:]
                if f == 0:
                    high = high + jnp.where(left, 0.0, cross[par])
                else:
                    low = low + jnp.where(left, cross[par], 0.0)
                ys[par] = jnp.concatenate([low, high], axis=1)
            sums.append(ys)
        out.append(sums)
    return out


def frame(x, i):
    return x[FRAME * i : FRAME * i + FRAME]


def add(terms):
    return functools.reduce(jnp.add, terms)


def inner_kernel(mid, w1a, w1c, acc, within1, within2, q, x34):
    within1[...] = inside(-2, LAYER + 4)
    within2[...] = inside(-1, LAYER + 2)
    spread_runs(lambda v, f, rows: mid[2 * v + f, rows, :], range(LAYER), q, x34)
    sums = products(q, x34, w1a, w1c, 0)
    for f in range(2):
        for par in range(2):
            for e in range(LAYER + 2):
                terms = [
                    frame(sums[dp][f][par], e - 2 + dp)
                    for dp in range(3)
                    if 0 <= e - 2 + dp < LAYER
                ]
                acc[f, par, FRAME * e : FRAME * e + FRAME, :] = add(terms)


def halo_kernel(rim_a, rim_b, q, x34):
    layer, layers = lax.axis_index("slab") // LAYER, lax.axis_size("slab") // LAYER
    odd = layer % 2 == 1

    def run(v, f, rows):
        at = 2 * (v % 3) + f
        got = jnp.where(odd == (v < 3), rim_a[at, rows, :], rim_b[at, rows, :])
        outside = layer == (0 if v < 3 else layers - 1)
        return jnp.where(outside, jnp.zeros_like(got), got)

    spread_runs(run, range(6), q, x34)


def one_kernel(q, x34, w1a, w1c, b1, acc, within, skips, pd):
    left = lax.broadcasted_iota(jnp.int32, (1, 128), 1) < 64
    sums = products(q, x34, w1a, w1c, 1)
    u = LAYER + 4
    targets = ((0, 1, 2, u - 1), (0, 1, u - 2, u - 1), (0, u - 3, u - 2, u - 1))
    bias = b1[0:1, :]
    tiles = []
    for f in range(2):
        ys = []
        for par in range(2):
            planes = []
            for plane in range(u):
                terms = [
                    frame(sums[dp][f][par], targets[dp].index(plane))
                    for dp in range(3)
                    if plane in targets[dp]
                ]
                if 1 <= plane <= u - 2:
                    terms.append(acc[f, par, FRAME * (plane - 1) : FRAME * plane, :])
                planes.append(add(terms))
            for s in range(LAYER):
                kept = planes[2 + s][LEAD : LEAD + 16, :]
                kept = jnp.maximum(kept + bias, 0.0).astype(BF)
                skips[2 * s + f, 16 * par : 16 * par + 16, :] = kept
            ys.append(jnp.concatenate(planes, axis=0))
        y = jnp.maximum(ys[0], ys[1])
        y0, y1 = y[:, :128], y[:, 128:]
        y0 = jnp.maximum(y0, pltpu.roll(y0, 64, 1))
        y1 = jnp.maximum(y1, pltpu.roll(y1, 64, 1))
        y = jnp.maximum(jnp.where(left, y0, y1) + bias[:, :128], 0.0)
        tiles.append(jnp.where(within[...] > 0.0, y, 0.0))
    pooled = jnp.concatenate(tiles, axis=1)
    for dw in range(3):
        pd[dw] = shifted(pooled, dw - 1).astype(BF)


def second_kernel(v2a, v2c, over, beside, b2, b3, w2a, w2c, bias2, bias3):
    half, core = lax.axis_index("filt"), lax.axis_index("slab") % 2
    mine, other = half * 64, 64 - half * 64
    for row in range(2):
        w2a[pl.ds(aligned(128 * row + mine, 64), 64), :] = v2a[64 * row : 64 * row + 64, :]
        w2c[pl.ds(aligned(128 * row + mine, 64), 64), :] = v2c[64 * row : 64 * row + 64, :]

    def piece(ref):
        def rows(t):
            both = ref[16 * t : 16 * t + 16, :]
            return jnp.concatenate([both[:, :64], both[:, 64:]], axis=0)

        return banded(rows)

    for rows, at in ((piece(over), other + 32 * core), (piece(beside), other + 32 - 32 * core)):
        for dp, dw in TAPS:
            lanes = slice(128 * (3 * dp + dw), 128 * (3 * dp + dw) + 128)
            a, b, c, d = rows(dp, dw)
            w2a[pl.ds(aligned(at, 32), 32), lanes] = a
            w2a[pl.ds(aligned(128 + at, 32), 32), lanes] = b
            w2c[pl.ds(aligned(at, 32), 32), lanes] = c
            w2c[pl.ds(aligned(128 + at, 32), 32), lanes] = d
    theirs = over[432:433, :].astype(F32)
    here2, here3 = b2[...].astype(F32), b3[...].astype(F32)
    there2, there3 = theirs[:, :64], theirs[:, 64:]
    low = jnp.where(half == 0, here2, there2)
    high = jnp.where(half == 0, there2, here2)
    bias2[...] = jnp.broadcast_to(jnp.concatenate([low, high], axis=1), bias2.shape)
    turned = jnp.concatenate([there3[:, 32:], there3[:, :32]], axis=1)
    order3 = jnp.concatenate([here3, jnp.where(core == 1, turned, there3)], axis=1)
    bias3[...] = jnp.broadcast_to(order3, bias3.shape)


def two_kernel(pd, w2a, w2c, b2, within, hd):
    left = lax.broadcasted_iota(jnp.int32, (1, 128), 1) < 64
    m = (LAYER + 2) * FRAME
    pairs = pair(
        [jnp.concatenate(lanes_of(pd, m, 128 * a, 128 * a + 128), axis=1) for a in range(2)],
        w2a[...],
    )
    parts = [jnp.where(left, b, a) for a, b in zip(lanes_of(pd, m, 0, 128), lanes_of(pd, m, 128, 256))]
    mixed = dot(jnp.concatenate(parts, axis=1), w2c[...], NT)
    hidden = jnp.concatenate(
        [
            pairs[0][:, :128],
            pairs[0][:, 128:] + mixed[:, :128],
            pairs[1][:, :128] + mixed[:, 128:],
            pairs[1][:, 128:],
        ],
        axis=1,
    )
    bias = jnp.concatenate([b2[0:1, :]] * 4, axis=1)
    within = jnp.concatenate([within[...]] * 4, axis=1)
    hidden = jnp.where(within > 0.0, jnp.maximum(hidden + bias, 0.0), 0.0).astype(BF).astype(F32)
    for dw in range(3):
        hd[dw] = shifted(hidden, dw - 1).astype(BF)


def three_kernel(hd, k3, over, beside, b3, skips, out):
    half, core = lax.axis_index("filt"), lax.axis_index("slab") % 2
    lane = lax.broadcasted_iota(jnp.int32, (1, 128), 1)
    left = lane < 64
    out[:, 0:32, :] = skips[...]
    m = LAYER * FRAME

    def third(t):
        rows = slice(32 * t, 32 * t + 32)
        return jnp.concatenate([k3[t], over[rows, :], beside[rows, :]], axis=0)

    straight, low, high = [[], []], [], []
    for dp, dw in TAPS:
        k0, k1, k2 = (third(9 * dp + 3 * dr + dw) for dr in range(3))
        straight[0] += [k1, k2]
        straight[1] += [k0, k1]
        low.append(k0)
        high.append(k2)
    w3a = jnp.concatenate([jnp.concatenate(rows, axis=1) for rows in straight], axis=0)
    both = jnp.concatenate(
        [jnp.concatenate(lanes_of(hd, m, 256 * a, 256 * a + 256), axis=1) for a in range(2)], axis=0
    )
    both = dot(both, w3a, NT)
    cat = lambda parts: jnp.concatenate(parts, axis=1)
    up = dot(cat(lanes_of(hd, m, 256, 384)), cat(high), NT)
    down = dot(cat(lanes_of(hd, m, 128, 256)), cat(low), NT)
    t0, t1 = both[:m, :128], both[:m, 128:] + up
    t2, t3 = both[m:, :128] + down, both[m:, 128:]
    t0, t1, t2, t3 = (jnp.maximum(t + b3[0:1, :], 0.0) for t in (t0, t1, t2, t3))
    r0, r1, r2, r3 = (pltpu.roll(t, 64, 1) for t in (t0, t1, t2, t3))
    first = jnp.concatenate([jnp.where(left, t0, r1), jnp.where(left, t2, r3)], axis=1)
    second = jnp.concatenate([jnp.where(left, r0, t1), jnp.where(left, r2, t3)], axis=1)
    lane = lax.broadcasted_iota(jnp.int32, (1, 256), 1)
    swapped = jnp.where(lane % 64 < 32, pltpu.roll(second, 224, 1), pltpu.roll(second, 32, 1))
    second = jnp.where(core == 1, swapped, second)
    for s in range(LAYER):
        top = FRAME * s + LEAD
        out[2 * s + half, 32:48, :] = first[top : top + 16, :].astype(BF)
        out[2 * s + 1 - half, 32:48, :] = second[top : top + 16, :].astype(BF)


def unpack_kernel(got, order, same, skip, features):
    count = got.shape[0]
    ones = got[:, 0:32, :].reshape(count * 32, 256)
    twos = got[:, 32:48, :].reshape(count * 16, 256)
    by_column = dot(order[...], ones, NN).astype(BF)
    skip[...] = dot(same[...], by_column, NT).astype(BF)
    features[...] = dot(same[...], twos, NT).astype(BF)


def shape(*dims):
    return jax.ShapeDtypeStruct(dims, BF)


def call(kernel, outs, *operands, scratch=(), limit=8, far=0):
    spec = pl.BlockSpec(memory_space=pltpu.VMEM)
    hbm = pl.BlockSpec(memory_space=pltpu.HBM)
    there = [pltpu.with_memory_space_constraint(x, pltpu.HBM) for x in operands[:far]]
    operands = [*there, *operands[far:]]
    return pl.pallas_call(
        kernel,
        out_shape=outs,
        in_specs=[hbm] * far + [spec] * (len(operands) - far),
        out_specs=jax.tree.map(lambda _: spec, outs),
        scratch_shapes=scratch,
        compiler_params=pltpu.CompilerParams(vmem_limit_bytes=limit << 20),
    )(*operands)


def near(x):
    return pltpu.with_memory_space_constraint(x, pltpu.VMEM)


def by_columns(volume, kernel_one, bias_one, kernel_two, bias_two, kernel_three, bias_three):
    slabs, halves = lax.axis_size("slab"), lax.axis_size("filt")
    peers = LAYER * halves
    groups = [[peers * g + i for i in range(peers)] for g in range(slabs // LAYER)]
    exchange = functools.partial(
        lax.all_to_all,
        axis_name=("slab", "filt"),
        split_axis=0,
        concat_axis=0,
        axis_index_groups=groups,
        tiled=True,
    )
    b1, b2, b3 = bias_one[None, :], bias_two[None, :], bias_three[None, :]
    blocks, *mine = call(
        pack_kernel,
        (
            pltpu.VMEM((peers, 2 * RUN, 256), BF),
            pltpu.VMEM((27, 32, 64), BF),
            pltpu.VMEM(kernel_three.shape, BF),
            pltpu.VMEM((1, 64), BF),
            pltpu.VMEM((1, 64), BF),
        ),
        volume.reshape(256, 256),
        kernel_two,
        kernel_three,
        b2,
        b3,
        scratch=[pltpu.VMEM((256, 256), BF), pltpu.SemaphoreType.DMA((5,))],
        far=5,
    )
    mid = exchange(blocks)
    halves_sent = (pltpu.VMEM((448, 128), BF), pltpu.VMEM((864, 128), BF))
    sent2, sent3 = call(send_kernel, halves_sent, *map(near, mine))
    over2 = lax.ppermute(sent2, "filt", [(0, 1), (1, 0)])
    over3 = lax.ppermute(sent3, "filt", [(0, 1), (1, 0)])
    w1a, w1c, v2a, v2c, bias1, order, same = call(
        first_kernel,
        (
            pltpu.VMEM((256, 2304), BF),
            pltpu.VMEM((128, 1152), BF),
            pltpu.VMEM((128, 1152), BF),
            pltpu.VMEM((128, 1152), BF),
            pltpu.VMEM((8, 256), F32),
            pltpu.VMEM((256, 256), BF),
            pltpu.VMEM((256, 256), BF),
        ),
        kernel_one,
        kernel_two,
        b1,
    )
    planes = pltpu.VMEM((2 * (LAYER - 1), 2 * RUN, 256), BF)
    to_first, to_second = call(rim_kernel, (planes, planes), near(mid))

    def swaps(start):
        up = [(i, i + LAYER) for i in range(slabs - LAYER) if i // LAYER % 2 == start]
        both = dict(up + [(b, a) for a, b in up])
        return [(i, both.get(i, i ^ 1)) for i in range(slabs)]

    rim_a = lax.ppermute(to_first, "slab", swaps(0))
    rim_b = lax.ppermute(to_second, "slab", swaps(1))
    other_core = [(i, i ^ 1) for i in range(slabs)]
    beside2 = lax.ppermute(over2, "slab", other_core)
    beside3 = lax.ppermute(over3, "slab", other_core)
    w2a, w2c, bias2, bias3 = call(
        second_kernel,
        (
            pltpu.VMEM((256, 1152), BF),
            pltpu.VMEM((256, 1152), BF),
            pltpu.VMEM((8, 128), F32),
            pltpu.VMEM((8, 128), F32),
        ),
        *map(near, (v2a, v2c, over2, beside2, b2, b3)),
    )

    def space(planes):
        rows = FRAME * planes
        return [pltpu.VMEM((2, 4, rows, 256), BF), pltpu.VMEM((4, rows, 128), BF)]

    acc, within1, within2 = call(
        inner_kernel,
        (
            pltpu.VMEM((2, 2, FRAME * (LAYER + 2), 256), F32),
            pltpu.VMEM((FRAME * (LAYER + 4), 128), F32),
            pltpu.VMEM((FRAME * (LAYER + 2), 128), F32),
        ),
        *map(near, (mid, w1a, w1c)),
        scratch=space(LAYER),
        limit=24,
    )
    halo = call(halo_kernel, tuple(space(6)), near(rim_a), near(rim_b), limit=24)
    skips, pooled = call(
        one_kernel,
        (pltpu.VMEM((peers, 32, 256), BF), pltpu.VMEM((3, FRAME * (LAYER + 4), 256), BF)),
        *map(near, (*halo, w1a, w1c, bias1, acc, within1)),
        limit=24,
    )
    hidden = call(
        two_kernel,
        pltpu.VMEM((3, FRAME * (LAYER + 2), 512), BF),
        *map(near, (pooled, w2a, w2c, bias2, within2)),
        limit=24,
    )
    out = call(
        three_kernel,
        pltpu.VMEM((peers, 48, 256), BF),
        *map(near, (hidden, mine[1], over3, beside3, bias3, skips)),
        limit=24,
    )
    home = exchange(out)
    outs = (shape(256, 256), shape(256, 128))
    skip, features = call(unpack_kernel, outs, *map(near, (home, order, same)))
    return skip.reshape(volume.shape), features.reshape(1, 4, 64, 128)


def fits(volume, kernels, slabs, halves):
    return (
        volume == (1, 4, 64, 256)
        and kernels == [(27, 64, 64), (27, 64, 64), (27, 64, 128)]
        and halves == 2
        and slabs % LAYER == 0
    )


def per_device(volume, *rest):
    kernels = [r.shape for r in rest[::2]]
    good = fits(volume.shape, kernels, lax.axis_size("slab"), lax.axis_size("filt"))
    if not good:
        return by_planes(volume, *rest)
    return by_columns(volume, *rest)


def solution(mesh):
    return jax.shard_map(
        per_device,
        mesh=mesh,
        in_specs=(
            P("slab", "filt", None, None),
            P(),
            P(),
            P(None, "filt", None),
            P("filt"),
            P(None, "filt", None),
            P("filt"),
        ),
        out_specs=(P("slab", "filt", None, None), P("slab", None, "filt", None)),
        check_vma=False,
    )
```

```python
import functools

import jax
import jax.numpy as jnp
from jax import lax
from jax.experimental import pallas as pl
from jax.experimental.pallas import tpu as pltpu
from jax.sharding import PartitionSpec as P


BF = jnp.bfloat16
F32 = jnp.float32
NT = (((1,), (1,)), ((), ()))
NN = (((1,), (0,)), ((), ()))

LAYER = 4
RUN = 24
FRAME = RUN
LEAD = 4


def extended(block, sides, width):
    for axis, dim in sides:
        count = lax.axis_size(axis)
        forward = [(i, i + 1) for i in range(count - 1)]
        backward = [(target, source) for source, target in forward]
        low = lax.ppermute(
            lax.slice_in_dim(block, block.shape[dim] - width, None, axis=dim), axis, forward
        )
        high = lax.ppermute(lax.slice_in_dim(block, 0, width, axis=dim), axis, backward)
        block = jnp.concatenate([low, block, high], axis=dim)
    return block


def pad_columns(field):
    return jnp.pad(field, ((0, 0), (0, 0), (0, 0), (1, 1)))


def accumulate(total, padded, kernel):
    planes, rows, _, cols = total.shape
    for kd in range(3):
        for kh in range(3):
            for kw in range(3):
                tap = 9 * kd + 3 * kh + kw
                total = total + jnp.einsum(
                    "oc,dhcw->dhow",
                    kernel[tap],
                    padded[kd : kd + planes, kh : kh + rows, :, kw : kw + cols],
                    preferred_element_type=jnp.float32,
                )
    return total


def finish(total, bias):
    return jnp.maximum(total + bias.astype(jnp.float32)[None, None, :, None], 0.0).astype(
        jnp.bfloat16
    )


def by_planes(volume, kernel_one, bias_one, kernel_two, bias_two, kernel_three, bias_three):
    planes, rows, chans, cols = volume.shape
    rimmed = extended(volume, (("slab", 0), ("filt", 1)), 1)
    start_one = jnp.zeros((planes, rows, kernel_one.shape[1], cols), jnp.float32)
    skip_one = finish(accumulate(start_one, pad_columns(rimmed), kernel_one), bias_one)
    pooled = jnp.max(skip_one.reshape(planes, rows // 2, 2, chans, cols // 2, 2), axis=(2, 5))
    full_rows = lax.all_gather(pooled, "filt", axis=1, tiled=True)
    planed = extended(full_rows, (("slab", 0),), 1)
    padded = jnp.pad(planed, ((0, 0), (1, 1), (0, 0), (1, 1)))
    height = full_rows.shape[1]
    width = full_rows.shape[3]
    start_two = jnp.zeros((planes, height, kernel_two.shape[1], width), jnp.float32)
    hidden = finish(accumulate(start_two, padded, kernel_two), bias_two)
    hidden_planes = extended(hidden, (("slab", 0),), 1)
    start_three = jnp.zeros((planes, height, kernel_three.shape[1], width), jnp.float32)
    piece_padded = jnp.pad(
        lax.all_gather(hidden_planes, "filt", axis=2, tiled=True), ((0, 0), (1, 1), (0, 0), (1, 1))
    )
    summed = accumulate(start_three, piece_padded, kernel_three)
    features_two = finish(summed, bias_three)
    return (skip_one, features_two)


def dot(a, b, dims):
    return lax.dot_general(a, b, dims, preferred_element_type=F32)


def pack_kernel(far, far2, far3, far_b2, far_b3, blocks, k2, k3, b2, b3, volume, sems):
    half = pl.ds(aligned(32 * (lax.axis_index("slab") % 2), 32), 32)
    pairs = (
        (far, volume),
        (far2.at[:, half, :], k2),
        (far3, k3),
        (far_b2, b2),
        (far_b3, b3),
    )
    copies = [pltpu.make_async_copy(*ends, sems.at[i]) for i, ends in enumerate(pairs)]
    for copy in copies:
        copy.start()
    count, width = blocks.shape[0], volume.shape[1]
    row = lax.broadcasted_iota(jnp.int32, (RUN, width), 0)
    col = lax.broadcasted_iota(jnp.int32, (RUN, width), 1)
    ahead = 2 * (row - LEAD) - col
    chosen = jnp.concatenate(
        [
            jnp.where(ahead == -(width // count) * peer - par, 1.0, 0.0)
            for peer in range(count)
            for par in range(2)
        ],
        axis=0,
    ).astype(BF)
    copies[0].wait()
    blocks[...] = dot(chosen, volume[...], NT).astype(BF).reshape(blocks.shape)
    for copy in copies[1:]:
        copy.wait()


def aligned(at, by):
    return pl.multiple_of(at, by)


def send_kernel(k2, k3, b2, b3, sent2, sent3):
    half = pl.ds(aligned(32 * (lax.axis_index("slab") % 2), 32), 32)
    for t in range(27):
        sent2[16 * t : 16 * t + 16, :] = jnp.concatenate([k2[t, :16, :], k2[t, 16:, :]], axis=1)
        sent3[32 * t : 32 * t + 32, :] = k3[t, half, :]
    both = jnp.concatenate([b2[...], b3[...]], axis=1)
    sent2[432:448, :] = jnp.broadcast_to(both, (16, 128))


def banded(k_ref):
    def pieces(dp, dw):
        k0, k1, k2 = (k_ref(9 * dp + 3 * dr + dw) for dr in range(3))
        none = jnp.zeros_like(k0)
        join = lambda a, b: jnp.concatenate([a, b], axis=1)
        return join(k1, k2), join(k0, k1), join(k2, none), join(none, k0)

    return pieces


def rim_kernel(mid, to_first, to_second):
    odd = lax.axis_index("slab") // LAYER % 2
    n = to_first.shape[0]
    to_first[...] = mid[pl.ds(2 - 2 * odd, n)]
    to_second[...] = mid[pl.ds(2 * odd, n)]


def first_kernel(k1, k2, b1, w1a, w1c, v2a, v2c, bias, order, same):
    row = lax.broadcasted_iota(jnp.int32, order.shape, 0)
    col = lax.broadcasted_iota(jnp.int32, order.shape, 1)
    source = 32 * (row // 32) + 16 * (row % 2) + row % 32 // 2
    order[...] = jnp.where(source == col, 1.0, 0.0).astype(BF)
    same[...] = jnp.where(row == col, 1.0, 0.0).astype(BF)
    one = banded(lambda t: k1[t])
    two = banded(lambda t: k2[t])
    zero = jnp.zeros((64, 128), BF)
    for dp in range(3):
        for dw in range(3):
            t = 3 * dp + dw
            a, b, c, d = one(dp, dw)
            for i, (low, high) in enumerate(((a, zero), (b, c), (d, a), (zero, b))):
                w1a[64 * i : 64 * i + 64, 256 * t : 256 * t + 128] = low
                w1a[64 * i : 64 * i + 64, 256 * t + 128 : 256 * t + 256] = high
            lanes = slice(128 * t, 128 * t + 128)
            w1c[0:64, lanes] = d
            w1c[64:128, lanes] = c
            a, b, c, d = two(dp, dw)
            v2a[0:64, lanes] = a
            v2a[64:128, lanes] = b
            v2c[0:64, lanes] = c
            v2c[64:128, lanes] = d
    bias[...] = jnp.broadcast_to(jnp.concatenate([b1[...].astype(F32)] * 4, axis=1), bias.shape)


def shifted(x, by):
    return pltpu.roll(x, (-by) % x.shape[0], 0)


TAPS = [(dp, dw) for dp in range(3) for dw in range(3)]


def inside(first, planes):
    half, slab = lax.axis_index("filt"), lax.axis_index("slab")
    layer, layers = slab // LAYER, lax.axis_size("slab") // LAYER
    group = slab % LAYER * lax.axis_size("filt") + half
    row = lax.broadcasted_iota(jnp.int32, (planes * FRAME, 1), 0)
    col = 16 * group - LEAD + row % FRAME
    plane = LAYER * layer + first + row // FRAME
    within = (plane >= 0) & (plane < LAYER * layers) & (col >= 0) & (col < 128)
    return jnp.broadcast_to(jnp.where(within, 1.0, 0.0), (planes * FRAME, 128))


def pair(parts, weights):
    n = parts[0].shape[0]
    all_rows = dot(jnp.concatenate(parts, axis=0), weights, NT)
    return [all_rows[n * i : n * i + n] for i in range(len(parts))]


def lanes_of(ref, n, lo, hi):
    return [ref[dw, FRAME * dp : FRAME * dp + n, lo:hi] for dp, dw in TAPS]


def spread_runs(run, planes, q, x34):
    left = lax.broadcasted_iota(jnp.int32, (1, 128), 1) < 64
    for f in range(2):
        for par in range(2):
            rows = slice(RUN * par, RUN * par + RUN)
            whole = jnp.concatenate([run(v, f, rows).astype(F32) for v in planes], axis=0)
            q[f, 1 + par] = whole.astype(BF)
            if par == 0:
                q[f, 3] = shifted(whole, 1).astype(BF)
            else:
                q[f, 0] = shifted(whole, -1).astype(BF)
    for a in range(4):
        x34[a] = jnp.where(left, q[1, a, :, 0:128], q[0, a, :, 128:256])


def products(q, x34, w1a, w1c, step):
    left = lax.broadcasted_iota(jnp.int32, (1, 128), 1) < 64
    n = LAYER * FRAME
    out = []
    for dp in range(3):
        rows = slice(FRAME * step * dp, FRAME * step * dp + n)

        def pick(ref, par):
            return jnp.concatenate([ref[par + dw, rows, :] for dw in range(3)], axis=1)

        cross = pair([pick(x34, par) for par in range(2)], w1c[:, 384 * dp : 384 * dp + 384])
        weights = w1a[:, 768 * dp : 768 * dp + 768]
        parts = [pick(q.at[f], par) for f in range(2) for par in range(2)]
        if dp < 2:
            together = pair(parts, weights)
        else:
            together = pair(parts[:2], weights) + pair(parts[2:], weights)
        sums = []
        for f in range(2):
            ys = together[2 * f : 2 * f + 2]
            for par in range(2):
                low, high = ys[par][:, :128], ys[par][:, 128:]
                if f == 0:
                    high = high + jnp.where(left, 0.0, cross[par])
                else:
                    low = low + jnp.where(left, cross[par], 0.0)
                ys[par] = jnp.concatenate([low, high], axis=1)
            sums.append(ys)
        out.append(sums)
    return out


def frame(x, i):
    return x[FRAME * i : FRAME * i + FRAME]


def add(terms):
    return functools.reduce(jnp.add, terms)


def inner_kernel(mid, w1a, w1c, acc, within1, within2, q, x34):
    within1[...] = inside(-2, LAYER + 4)
    within2[...] = inside(-1, LAYER + 2)
    spread_runs(lambda v, f, rows: mid[2 * v + f, rows, :], range(LAYER), q, x34)
    sums = products(q, x34, w1a, w1c, 0)
    for f in range(2):
        for par in range(2):
            for e in range(LAYER + 2):
                terms = [
                    frame(sums[dp][f][par], e - 2 + dp)
                    for dp in range(3)
                    if 0 <= e - 2 + dp < LAYER
                ]
                acc[f, par, FRAME * e : FRAME * e + FRAME, :] = add(terms)


def halo_kernel(rim_a, rim_b, q, x34):
    layer, layers = lax.axis_index("slab") // LAYER, lax.axis_size("slab") // LAYER
    odd = layer % 2 == 1

    def run(v, f, rows):
        at = 2 * (v % 3) + f
        got = jnp.where(odd == (v < 3), rim_a[at, rows, :], rim_b[at, rows, :])
        outside = layer == (0 if v < 3 else layers - 1)
        return jnp.where(outside, jnp.zeros_like(got), got)

    spread_runs(run, range(6), q, x34)


def one_kernel(q, x34, w1a, w1c, b1, acc, within, skips, pd):
    left = lax.broadcasted_iota(jnp.int32, (1, 128), 1) < 64
    sums = products(q, x34, w1a, w1c, 1)
    u = LAYER + 4
    targets = ((0, 1, 2, u - 1), (0, 1, u - 2, u - 1), (0, u - 3, u - 2, u - 1))
    bias = b1[0:1, :]
    tiles = []
    for f in range(2):
        ys = []
        for par in range(2):
            planes = []
            for plane in range(u):
                terms = [
                    frame(sums[dp][f][par], targets[dp].index(plane))
                    for dp in range(3)
                    if plane in targets[dp]
                ]
                if 1 <= plane <= u - 2:
                    terms.append(acc[f, par, FRAME * (plane - 1) : FRAME * plane, :])
                planes.append(add(terms))
            for s in range(LAYER):
                kept = planes[2 + s][LEAD : LEAD + 16, :]
                kept = jnp.maximum(kept + bias, 0.0).astype(BF)
                skips[2 * s + f, 16 * par : 16 * par + 16, :] = kept
            ys.append(jnp.concatenate(planes, axis=0))
        y = jnp.maximum(ys[0], ys[1])
        y0, y1 = y[:, :128], y[:, 128:]
        y0 = jnp.maximum(y0, pltpu.roll(y0, 64, 1))
        y1 = jnp.maximum(y1, pltpu.roll(y1, 64, 1))
        y = jnp.maximum(jnp.where(left, y0, y1) + bias[:, :128], 0.0)
        tiles.append(jnp.where(within[...] > 0.0, y, 0.0))
    pooled = jnp.concatenate(tiles, axis=1)
    for dw in range(3):
        pd[dw] = shifted(pooled, dw - 1).astype(BF)


def second_kernel(v2a, v2c, over, beside, b2, b3, w2a, w2c, bias2, bias3):
    half, core = lax.axis_index("filt"), lax.axis_index("slab") % 2
    mine, other = half * 64, 64 - half * 64
    for row in range(2):
        w2a[pl.ds(aligned(128 * row + mine, 64), 64), :] = v2a[64 * row : 64 * row + 64, :]
        w2c[pl.ds(aligned(128 * row + mine, 64), 64), :] = v2c[64 * row : 64 * row + 64, :]

    def piece(ref):
        def rows(t):
            both = ref[16 * t : 16 * t + 16, :]
            return jnp.concatenate([both[:, :64], both[:, 64:]], axis=0)

        return banded(rows)

    for rows, at in ((piece(over), other + 32 * core), (piece(beside), other + 32 - 32 * core)):
        for dp, dw in TAPS:
            lanes = slice(128 * (3 * dp + dw), 128 * (3 * dp + dw) + 128)
            a, b, c, d = rows(dp, dw)
            w2a[pl.ds(aligned(at, 32), 32), lanes] = a
            w2a[pl.ds(aligned(128 + at, 32), 32), lanes] = b
            w2c[pl.ds(aligned(at, 32), 32), lanes] = c
            w2c[pl.ds(aligned(128 + at, 32), 32), lanes] = d
    theirs = over[432:433, :].astype(F32)
    here2, here3 = b2[...].astype(F32), b3[...].astype(F32)
    there2, there3 = theirs[:, :64], theirs[:, 64:]
    low = jnp.where(half == 0, here2, there2)
    high = jnp.where(half == 0, there2, here2)
    bias2[...] = jnp.broadcast_to(jnp.concatenate([low, high], axis=1), bias2.shape)
    turned = jnp.concatenate([there3[:, 32:], there3[:, :32]], axis=1)
    order3 = jnp.concatenate([here3, jnp.where(core == 1, turned, there3)], axis=1)
    bias3[...] = jnp.broadcast_to(order3, bias3.shape)


def two_kernel(pd, w2a, w2c, b2, within, hd):
    left = lax.broadcasted_iota(jnp.int32, (1, 128), 1) < 64
    m = (LAYER + 2) * FRAME
    pairs = pair(
        [jnp.concatenate(lanes_of(pd, m, 128 * a, 128 * a + 128), axis=1) for a in range(2)],
        w2a[...],
    )
    parts = [jnp.where(left, b, a) for a, b in zip(lanes_of(pd, m, 0, 128), lanes_of(pd, m, 128, 256))]
    mixed = dot(jnp.concatenate(parts, axis=1), w2c[...], NT)
    hidden = jnp.concatenate(
        [
            pairs[0][:, :128],
            pairs[0][:, 128:] + mixed[:, :128],
            pairs[1][:, :128] + mixed[:, 128:],
            pairs[1][:, 128:],
        ],
        axis=1,
    )
    bias = jnp.concatenate([b2[0:1, :]] * 4, axis=1)
    within = jnp.concatenate([within[...]] * 4, axis=1)
    hidden = jnp.where(within > 0.0, jnp.maximum(hidden + bias, 0.0), 0.0).astype(BF).astype(F32)
    for dw in range(3):
        hd[dw] = shifted(hidden, dw - 1).astype(BF)


def three_kernel(hd, k3, over, beside, b3, skips, out):
    half, core = lax.axis_index("filt"), lax.axis_index("slab") % 2
    lane = lax.broadcasted_iota(jnp.int32, (1, 128), 1)
    left = lane < 64
    m = LAYER * FRAME

    def third(t):
        rows = slice(32 * t, 32 * t + 32)
        return jnp.concatenate([k3[t], over[rows, :], beside[rows, :]], axis=0)

    straight, low, high = [[], []], [], []
    for dp, dw in TAPS:
        k0, k1, k2 = (third(9 * dp + 3 * dr + dw) for dr in range(3))
        straight[0] += [k1, k2]
        straight[1] += [k0, k1]
        low.append(k0)
        high.append(k2)
    w3a = jnp.concatenate([jnp.concatenate(rows, axis=1) for rows in straight], axis=0)
    both = jnp.concatenate(
        [jnp.concatenate(lanes_of(hd, m, 256 * a, 256 * a + 256), axis=1) for a in range(2)], axis=0
    )
    both = dot(both, w3a, NT)
    cat = lambda parts: jnp.concatenate(parts, axis=1)
    up = dot(cat(lanes_of(hd, m, 256, 384)), cat(high), NT)
    down = dot(cat(lanes_of(hd, m, 128, 256)), cat(low), NT)
    t0, t1 = both[:m, :128], both[:m, 128:] + up
    t2, t3 = both[m:, :128] + down, both[m:, 128:]
    t0, t1, t2, t3 = (jnp.maximum(t + b3[0:1, :], 0.0) for t in (t0, t1, t2, t3))
    r0, r1, r2, r3 = (pltpu.roll(t, 64, 1) for t in (t0, t1, t2, t3))
    first = jnp.concatenate([jnp.where(left, t0, r1), jnp.where(left, t2, r3)], axis=1)
    second = jnp.concatenate([jnp.where(left, r0, t1), jnp.where(left, r2, t3)], axis=1)
    lane = lax.broadcasted_iota(jnp.int32, (1, 256), 1)
    swapped = jnp.where(lane % 64 < 32, pltpu.roll(second, 224, 1), pltpu.roll(second, 32, 1))
    second = jnp.where(core == 1, swapped, second)
    for s in range(LAYER):
        top = FRAME * s + LEAD
        out[2 * s + half, 32:48, :] = first[top : top + 16, :].astype(BF)
        out[2 * s + 1 - half, 32:48, :] = second[top : top + 16, :].astype(BF)


def unpack_kernel(got, order, same, skip, features):
    count = got.shape[0]
    ones = got[:, 0:32, :].reshape(count * 32, 256)
    twos = got[:, 32:48, :].reshape(count * 16, 256)
    by_column = dot(order[...], ones, NN).astype(BF)
    skip[...] = dot(same[...], by_column, NT).astype(BF)
    features[...] = dot(same[...], twos, NT).astype(BF)


def shape(*dims):
    return jax.ShapeDtypeStruct(dims, BF)


def call(kernel, outs, *operands, scratch=(), limit=8, far=0, aliases={}):
    spec = pl.BlockSpec(memory_space=pltpu.VMEM)
    hbm = pl.BlockSpec(memory_space=pltpu.HBM)
    there = [pltpu.with_memory_space_constraint(x, pltpu.HBM) for x in operands[:far]]
    operands = [*there, *operands[far:]]
    return pl.pallas_call(
        kernel,
        out_shape=outs,
        in_specs=[hbm] * far + [spec] * (len(operands) - far),
        out_specs=jax.tree.map(lambda _: spec, outs),
        scratch_shapes=scratch,
        input_output_aliases=aliases,
        compiler_params=pltpu.CompilerParams(vmem_limit_bytes=limit << 20),
    )(*operands)


def near(x):
    return pltpu.with_memory_space_constraint(x, pltpu.VMEM)


def by_columns(volume, kernel_one, bias_one, kernel_two, bias_two, kernel_three, bias_three):
    slabs, halves = lax.axis_size("slab"), lax.axis_size("filt")
    peers = LAYER * halves
    groups = [[peers * g + i for i in range(peers)] for g in range(slabs // LAYER)]
    exchange = functools.partial(
        lax.all_to_all,
        axis_name=("slab", "filt"),
        split_axis=0,
        concat_axis=0,
        axis_index_groups=groups,
        tiled=True,
    )
    b1, b2, b3 = bias_one[None, :], bias_two[None, :], bias_three[None, :]
    blocks, *mine = call(
        pack_kernel,
        (
            pltpu.VMEM((peers, 2 * RUN, 256), BF),
            pltpu.VMEM((27, 32, 64), BF),
            pltpu.VMEM(kernel_three.shape, BF),
            pltpu.VMEM((1, 64), BF),
            pltpu.VMEM((1, 64), BF),
        ),
        volume.reshape(256, 256),
        kernel_two,
        kernel_three,
        b2,
        b3,
        scratch=[pltpu.VMEM((256, 256), BF), pltpu.SemaphoreType.DMA((5,))],
        far=5,
    )
    mid = exchange(blocks)
    halves_sent = (pltpu.VMEM((448, 128), BF), pltpu.VMEM((864, 128), BF))
    sent2, sent3 = call(send_kernel, halves_sent, *map(near, mine))
    over2 = lax.ppermute(sent2, "filt", [(0, 1), (1, 0)])
    over3 = lax.ppermute(sent3, "filt", [(0, 1), (1, 0)])
    w1a, w1c, v2a, v2c, bias1, order, same = call(
        first_kernel,
        (
            pltpu.VMEM((256, 2304), BF),
            pltpu.VMEM((128, 1152), BF),
            pltpu.VMEM((128, 1152), BF),
            pltpu.VMEM((128, 1152), BF),
            pltpu.VMEM((8, 256), F32),
            pltpu.VMEM((256, 256), BF),
            pltpu.VMEM((256, 256), BF),
        ),
        kernel_one,
        kernel_two,
        b1,
    )
    planes = pltpu.VMEM((2 * (LAYER - 1), 2 * RUN, 256), BF)
    to_first, to_second = call(rim_kernel, (planes, planes), near(mid))

    def swaps(start):
        up = [(i, i + LAYER) for i in range(slabs - LAYER) if i // LAYER % 2 == start]
        both = dict(up + [(b, a) for a, b in up])
        return [(i, both.get(i, i ^ 1)) for i in range(slabs)]

    rim_a = lax.ppermute(to_first, "slab", swaps(0))
    rim_b = lax.ppermute(to_second, "slab", swaps(1))
    other_core = [(i, i ^ 1) for i in range(slabs)]
    beside2 = lax.ppermute(over2, "slab", other_core)
    beside3 = lax.ppermute(over3, "slab", other_core)
    w2a, w2c, bias2, bias3 = call(
        second_kernel,
        (
            pltpu.VMEM((256, 1152), BF),
            pltpu.VMEM((256, 1152), BF),
            pltpu.VMEM((8, 128), F32),
            pltpu.VMEM((8, 128), F32),
        ),
        *map(near, (v2a, v2c, over2, beside2, b2, b3)),
    )

    def space(planes):
        rows = FRAME * planes
        return [pltpu.VMEM((2, 4, rows, 256), BF), pltpu.VMEM((4, rows, 128), BF)]

    acc, within1, within2 = call(
        inner_kernel,
        (
            pltpu.VMEM((2, 2, FRAME * (LAYER + 2), 256), F32),
            pltpu.VMEM((FRAME * (LAYER + 4), 128), F32),
            pltpu.VMEM((FRAME * (LAYER + 2), 128), F32),
        ),
        *map(near, (mid, w1a, w1c)),
        scratch=space(LAYER),
        limit=24,
    )
    halo = call(halo_kernel, tuple(space(6)), near(rim_a), near(rim_b), limit=24)
    skips, pooled = call(
        one_kernel,
        (pltpu.VMEM((peers, 48, 256), BF), pltpu.VMEM((3, FRAME * (LAYER + 4), 256), BF)),
        *map(near, (*halo, w1a, w1c, bias1, acc, within1)),
        limit=24,
    )
    hidden = call(
        two_kernel,
        pltpu.VMEM((3, FRAME * (LAYER + 2), 512), BF),
        *map(near, (pooled, w2a, w2c, bias2, within2)),
        limit=24,
    )
    out = call(
        three_kernel,
        pltpu.VMEM((peers, 48, 256), BF),
        *map(near, (hidden, mine[1], over3, beside3, bias3, skips)),
        aliases={5: 0},
        limit=24,
    )
    home = exchange(out)
    outs = (shape(256, 256), shape(256, 128))
    skip, features = call(unpack_kernel, outs, *map(near, (home, order, same)))
    return skip.reshape(volume.shape), features.reshape(1, 4, 64, 128)


def fits(volume, kernels, slabs, halves):
    return (
        volume == (1, 4, 64, 256)
        and kernels == [(27, 64, 64), (27, 64, 64), (27, 64, 128)]
        and halves == 2
        and slabs % LAYER == 0
    )


def per_device(volume, *rest):
    kernels = [r.shape for r in rest[::2]]
    good = fits(volume.shape, kernels, lax.axis_size("slab"), lax.axis_size("filt"))
    if not good:
        return by_planes(volume, *rest)
    return by_columns(volume, *rest)


def solution(mesh):
    return jax.shard_map(
        per_device,
        mesh=mesh,
        in_specs=(
            P("slab", "filt", None, None),
            P(),
            P(),
            P(None, "filt", None),
            P("filt"),
            P(None, "filt", None),
            P("filt"),
        ),
        out_specs=(P("slab", "filt", None, None), P("slab", None, "filt", None)),
        check_vma=False,
    )
```
